32 devices in a mesh: wide: 8 (over z, x), narrow: 4 (over y, core).
Axes of the slice: x: 2, y: 2, z: 4, core: 2. Of those that a mesh axis runs over, the one named last changes fastest.
Arguments:
- tokens: bfloat16 [96, 568, 640], P(('wide', 'narrow')), may hold values from -6 to 6
- lengths: int32 [96], P(('wide', 'narrow')), may hold values from 142 to 568, as said below
- masked_flags: int32 [96, 568], P(('wide', 'narrow')), may hold values from 0 to 1, as said below
- labels: int32 [96, 568], P(('wide', 'narrow')), may hold values from 0 to 32
- attn_weights: bfloat16 [2560, 640], P(('wide', 'narrow')), may hold values from -3 to 3
- ffn_weights: bfloat16 [2, 2560, 640], P(None, ('wide', 'narrow')), may hold values from -0.25 to 0.25
- ffn_bias: bfloat16 [2560], P(('wide', 'narrow')), may hold values from -3 to 3
- norm_gains: bfloat16 [2, 640], P(None, 'wide'), may hold values from 0.25 to 1.75
- biases: bfloat16 [7, 640], P(None, 'wide'), may hold values from -3 to 3
- head_weight: bfloat16 [640, 33], replicated, may hold values from -0.75 to 0.75
- cotangent: bfloat16 [96, 568, 640], P(('wide', 'narrow')), may hold values from -6 to 6
Outputs:
- output: bfloat16 [96, 568, 640], P(('wide', 'narrow'))
- grad_tokens: float32 [96, 568, 640], P(('wide', 'narrow'))
- grad_attn_weights: float32 [2560, 640], P(('wide', 'narrow'))
- grad_ffn_weights: float32 [2, 2560, 640], P(None, ('wide', 'narrow'))
- grad_ffn_bias: float32 [2560], P(('wide', 'narrow'))
- grad_norm_gains: float32 [2, 640], P(None, 'wide')
- grad_biases: float32 [7, 640], P(None, 'wide')
- head_stats: float32 [2], replicated
The draws below stay inside these ranges and needn't reach their ends.
Inputs may be any that keep to these rules, and one draw needn't show every extreme that they name: Positions below lengths are real residues, the others padding; some sequence has all 568 real and some has 142. `masked_flags`: position 0 of every sequence is marked.
All inputs are finite; a program needn't handle non-finite values.
Results may differ from the reference program's by a relative error of at most 0.01.
The reference program's roundings to bfloat16 on the way count: a program that leaves them out, or rounds other values in their place, can miss the bound.
Values may be sent and summed in bfloat16 or wider, within the bound.
A program may use at most 192 MiB of HBM per device.

```python
import math
import jax
import jax.numpy as jnp
from jax import lax

D = 640
HEADS = 20
HEAD = 32
FF = 2560
VOCAB = 33
L = 568
SEQ_DEV = 3
SEQS = 96
N_WIDE = 8
N_NARROW = 4


def draw_lengths(key, part):
    ratio = jax.random.randint(key, (SEQS,), 1, 64)
    spans = jnp.minimum(L, L // 4 + 4 * L // ratio)
    chosen = jax.random.randint(jax.random.fold_in(key, 11), (), 0, SEQS)
    offset = jax.random.randint(jax.random.fold_in(key, 13), (), 1, SEQS)
    shortest = (chosen + offset) % SEQS
    positions = jnp.arange(SEQS)
    spans = jnp.where(positions == shortest, L // 4, spans)
    return jnp.where(positions == chosen, L, spans).astype(jnp.int32)


def draw_masked_flags(key, part):
    rows_index = jnp.arange(SEQS)[:, None]
    cutoff = 100 + 300 * rows_index // SEQS
    samples = jax.random.randint(key, (SEQS, L), 0, 1000)
    leading = jnp.arange(L)[None, :] == 0
    return jnp.where(leading | (samples < cutoff), 1, 0).astype(jnp.int32)


def draw_attn_weights(key, part):
    base = jnp.clip(jax.random.normal(key, (4 * D, D), jnp.float32), -3.0, 3.0)
    rows_index = jnp.arange(4 * D)[:, None]
    factor = jnp.where(rows_index >= 3 * D, 8.0, 1.0) / math.sqrt(D)
    return (base * factor).astype(jnp.bfloat16)


def plant(drawn, key, least, top_value):
    spot = [jax.random.randint(jax.random.fold_in(key, axis), (), 0, length) for axis, length in enumerate(drawn.shape)]
    main_axis = drawn.shape.index(max(drawn.shape))
    next_to = spot[:main_axis] + [(spot[main_axis] + 1) % drawn.shape[main_axis]] + spot[main_axis + 1:]
    return drawn.at[tuple(spot)].set(least).at[tuple(next_to)].set(top_value)


def spiked(entries, rng, source, target, blocks, factor):
    owner, partner = [(jnp.arange(entries.shape[dim]) // (entries.shape[dim] // blocks)).reshape([-1 if axis == dim else 1 for axis in range(entries.ndim)]) for dim in (source, target)]
    chosen = jax.random.permutation(rng, blocks)[partner]
    strong = (owner == chosen) | (owner == (partner + blocks // 2) % blocks)
    return jnp.where(strong, factor * entries, entries)


def shard_levels(key, dims, split, low, high):
    factor_of = 1.0
    for axis_at, parts in split:
        draws = jax.random.uniform(jax.random.fold_in(jax.random.fold_in(key, 6), axis_at), (parts,), jnp.float32, low / len(split), high / len(split))
        factor_of = factor_of * jnp.repeat(jnp.exp(draws), dims[axis_at] // parts).reshape((-1,) + (1,) * (len(dims) - 1 - axis_at))
    return factor_of


def noise(stream_key, extent, width, limit, split=(), kind=jnp.bfloat16):
    level = shard_levels(stream_key, extent, split, -0.22, 0.18) if split else 1.0
    result = jax.random.normal(stream_key, extent, jnp.float32) * width * level
    return jnp.minimum(jnp.maximum(result, -limit), limit).astype(kind)


def heavy_noise(key, shape, scale, reach, shards, heavy, kind=jnp.bfloat16):
    result = scale * jax.random.normal(key, shape, jnp.float32)
    if shards:
        result = result * shard_levels(key, shape, shards, -0.22, 0.18)
    return jnp.clip(spiked(result, jax.random.fold_in(key, 3), *heavy), -reach, reach).astype(kind)


def setup_inputs(seed: int = 0) -> dict:
    arg_keys = jax.random.split(jax.random.key(seed), 12)
    tokens = heavy_noise(arg_keys[0], (SEQS, L, D), 1.0, 6.0, ((0, 32),), (0, 2, 32, 2.75))
    lengths = draw_lengths(jax.random.fold_in(arg_keys[11], 71), 0)
    masked_flags = draw_masked_flags(jax.random.fold_in(arg_keys[11], 71), 0)
    labels = plant(jax.random.randint(arg_keys[3], (SEQS, L), 0, VOCAB), jax.random.fold_in(arg_keys[3], 1), 0, VOCAB - 1).astype(jnp.int32)
    attn_weights = draw_attn_weights(jax.random.fold_in(arg_keys[11], 71), 0)
    ffn_weights = noise(arg_keys[5], (2, FF, D), D ** -0.5, 0.25, ((1, 32),))
    ffn_bias = noise(arg_keys[6], (FF,), 0.5, 3.0, ((0, 32),))
    norm_gains = jnp.clip(1.0 + 0.15 * jax.random.normal(arg_keys[7], (2, D), jnp.float32), 0.25, 1.75).astype(jnp.bfloat16)
    biases = noise(arg_keys[8], (7, D), 0.5, 3.0, ((1, 8),))
    head_weight = noise(arg_keys[9], (D, VOCAB), (D // 9) ** -0.5, 0.75)
    cotangent = heavy_noise(arg_keys[10], (SEQS, L, D), 1.0, 6.0, ((0, 32),), (0, 2, 32, 2.75))
    return {"tokens": tokens, "lengths": lengths, "masked_flags": masked_flags, "labels": labels, "attn_weights": attn_weights, "ffn_weights": ffn_weights, "ffn_bias": ffn_bias, "norm_gains": norm_gains, "biases": biases, "head_weight": head_weight, "cotangent": cotangent}


@jax.custom_vjp
def low(v):
    return lax.optimization_barrier(v.astype(jnp.bfloat16)).astype(jnp.float32)

@jax.custom_vjp
def low_back(v):
    return v

def low_keep(v):
    return (low(v), None)

def low_pass(kept, grad):
    return (grad,)

def back_keep(v):
    return (v, None)

def back_low(kept, grad):
    return (low(grad),)
low.defvjp(low_keep, low_pass)
low_back.defvjp(back_keep, back_low)

def matmul(left, right):
    return jnp.dot(left, right, precision=lax.Precision.HIGHEST, preferred_element_type=jnp.float32)

def layer_norm(values, gain_row, shift_row):
    center = lax.optimization_barrier(jnp.mean(values, axis=-1, keepdims=True))
    offset = values - center
    spread = lax.optimization_barrier(jnp.mean(offset * offset, axis=-1, keepdims=True))
    return offset * lax.rsqrt(spread + 1e-05) * gain_row + shift_row

def rotary_tables(length):
    half_head = HEAD // 2
    frequency = 1.0 / 10000.0 ** (jnp.arange(half_head, dtype=jnp.float32) * (2.0 / HEAD))
    angles = jnp.arange(length, dtype=jnp.float32)[:, None] * frequency[None, :]
    angles = jnp.concatenate([angles, angles], axis=1)
    return (jnp.cos(angles), jnp.sin(angles))

def turn_half(values):
    half_head = HEAD // 2
    return jnp.concatenate([-values[..., half_head:], values[..., :half_head]], axis=-1)

def rotate(values, cosine_table, sine_table):
    return values * cosine_table[:, None, :] + turn_half(values) * sine_table[:, None, :]

def attend_sequence(pieces):
    queries, keyset, values, limit_len = pieces
    scores = low_back(jnp.einsum('qhd,khd->hqk', queries, keyset, precision=lax.Precision.HIGHEST))
    usable = jnp.arange(L, dtype=jnp.int32) < limit_len
    scores = jnp.where(usable[None, None, :], scores, -1000000000.0)
    peak_score = lax.optimization_barrier(jnp.max(scores, axis=-1, keepdims=True))
    exponent = jnp.exp(scores - peak_score)
    weights = low(exponent / lax.optimization_barrier(jnp.sum(exponent, axis=-1, keepdims=True)))
    return jnp.einsum('hqk,khd->qhd', weights, values, precision=lax.Precision.HIGHEST)

def forward(tokens, attn_weights, ffn_weights, ffn_bias, norm_gains, biases, lengths):
    seq_count = tokens.shape[0]
    row_count = seq_count * L
    cosine_table, sine_table = rotary_tables(L)
    score_scale = 1.0 / math.sqrt(HEAD)
    heads_shape = (seq_count, L, HEADS, HEAD)
    inputs_flat = tokens.reshape(row_count, D)
    hidden_one = low(layer_norm(inputs_flat, norm_gains[0], biases[0]))
    query_lin = low_back(matmul(hidden_one, attn_weights[0:D]) + biases[2])
    key_lin = low_back(matmul(hidden_one, attn_weights[D:2 * D]) + biases[3])
    value_low = low(low_back(matmul(hidden_one, attn_weights[2 * D:3 * D]) + biases[4]))
    query_rot = low(rotate(query_lin.reshape(heads_shape), cosine_table, sine_table) * score_scale)
    key_rot = low(rotate(key_lin.reshape(heads_shape), cosine_table, sine_table))
    mixed = lax.map(jax.checkpoint(attend_sequence), (query_rot, key_rot, value_low.reshape(heads_shape), lengths))
    mixed_low = low(low_back(mixed.reshape(row_count, D)))
    branch = low_back(matmul(mixed_low, attn_weights[3 * D:4 * D]) + biases[5])
    middle = inputs_flat + branch
    hidden_two = low(layer_norm(middle, norm_gains[1], biases[1]))
    upward = low_back(matmul(hidden_two, ffn_weights[0].T) + ffn_bias)
    act_low = low(jax.nn.gelu(upward, approximate=False))
    down_rows = low_back(matmul(act_low, ffn_weights[1]) + biases[6])
    return (middle + down_rows).reshape(tokens.shape)

def head_terms(result_rows, masked_flags, labels, lengths, head_full):
    whitened = layer_norm(result_rows, 1.0, 0.0).reshape(-1, D)
    logits = matmul(low(whitened), head_full)
    shifted = logits - lax.optimization_barrier(jnp.max(logits, axis=-1, keepdims=True))
    logprob = shifted - jnp.log(lax.optimization_barrier(jnp.sum(jnp.exp(shifted), axis=-1, keepdims=True)))
    matches = labels.reshape(-1)[:, None] == jnp.arange(VOCAB, dtype=jnp.int32)[None, :]
    picked = lax.optimization_barrier(jnp.sum(jnp.where(matches, logprob, 0.0), axis=-1))
    living = ((masked_flags == 1) & (jnp.arange(L, dtype=jnp.int32)[None, :] < lengths[:, None])).reshape(-1)
    loglik = jnp.sum(jnp.where(living, picked, 0.0))
    hits = jnp.sum(jnp.where(living, jnp.exp(picked), 0.0))
    return jnp.stack([loglik, hits])

def reference(tokens, lengths, masked_flags, labels, attn_weights, ffn_weights, ffn_bias, norm_gains, biases, head_weight, cotangent):
    groups = N_WIDE * N_NARROW
    params = tuple((weight_arg.astype(jnp.float32) for weight_arg in (attn_weights, ffn_weights, ffn_bias, norm_gains, biases)))
    head_full = head_weight.astype(jnp.float32)

    def by_group(values):
        return values.reshape((groups, SEQ_DEV) + values.shape[1:])

    def scan_step(running, pieces):
        block_tokens, block_lengths, block_flags, block_labels, block_cot = pieces

        def closure(inputs_block, attn_arg, ffn_arg, ffnbias_arg, gain_arg, bias_arg):
            return forward(inputs_block, attn_arg, ffn_arg, ffnbias_arg, gain_arg, bias_arg, block_lengths)
        result_rows, pullback = jax.vjp(closure, block_tokens.astype(jnp.float32), *params)
        gradients = pullback(block_cot.astype(jnp.float32))
        running = tuple((earlier + addition for earlier, addition in zip(running, gradients[1:])))
        partial_stats = head_terms(result_rows, block_flags, block_labels, block_lengths, head_full)
        return (running, (result_rows.astype(jnp.bfloat16), gradients[0], partial_stats))
    start_zeros = tuple((jnp.zeros(weight_arg.shape, jnp.float32) for weight_arg in params))
    totals, (outputs, grad_tokens, partials) = lax.scan(scan_step, start_zeros, (by_group(tokens), by_group(lengths), by_group(masked_flags), by_group(labels), by_group(cotangent)))
    head_stats = lax.optimization_barrier(jnp.sum(partials, axis=0)) * jnp.array([1.0, VOCAB], jnp.float32) / (SEQS * L)
    return (outputs.reshape(SEQS, L, D), grad_tokens.reshape(SEQS, L, D), totals[0], totals[1], totals[2], totals[3], totals[4], head_stats)
```

```python
import functools
import math

import jax
import jax.numpy as jnp
import numpy as np
from jax import lax
from jax.experimental import pallas as pl
from jax.experimental.pallas import tpu as pltpu
from jax.sharding import PartitionSpec as P

D = 640
HEADS = 20
HEAD = 32
HALF = HEAD // 2
VOCAB = 33
EPS = 1e-05
ROOT_HALF = 0.7071067811865476
INV_ROOT_TWO_PI = 0.3989422804014327
BF = jnp.bfloat16
F32 = jnp.float32
VMEM_LIMIT = 60 << 20


def dot_nn(a, b):
    return lax.dot_general(a, b, (((1,), (0,)), ((), ())), preferred_element_type=F32)


def dot_nt(a, b):
    return lax.dot_general(a, b, (((1,), (1,)), ((), ())), preferred_element_type=F32)


def dot_tn(a, b):
    return lax.dot_general(a, b, (((0,), (0,)), ((), ())), preferred_element_type=F32)


def whiten(values):
    center = jnp.mean(values, axis=-1, keepdims=True)
    offset = values - center
    spread = jnp.mean(offset * offset, axis=-1, keepdims=True)
    inverse = lax.rsqrt(spread + EPS)
    return offset * inverse, inverse


def whiten_back(gradient, whitened, inverse, gain):
    scaled = gradient * gain
    mean_grad = jnp.mean(scaled, axis=-1, keepdims=True)
    mean_cross = jnp.mean(scaled * whitened, axis=-1, keepdims=True)
    return inverse * (scaled - mean_grad - whitened * mean_cross)


def rotary_tables(length):
    frequency = (
        np.float32(1.0)
        / np.float32(10000.0) ** (np.arange(HALF, dtype=np.float32) * np.float32(2.0 / HEAD))
    ).astype(np.float32)
    angles = frequency[:, None] * np.arange(length, dtype=np.float32)[None, :]
    return np.cos(angles).astype(np.float32), np.sin(angles).astype(np.float32)


def key_extents(length):
    extents = list(range(256, length, 128))
    return extents + [length]


def halves(values):
    length = values.shape[-1]
    split = values.reshape(values.shape[0] // HEAD, 2, HALF, length)
    return split[:, 0], split[:, 1]


def joined(first, second):
    length = first.shape[-1]
    both = jnp.concatenate([first[:, None], second[:, None]], axis=1)
    return both.reshape(first.shape[0] * HEAD, length)


def score_block(key_t, query_t, low, limit):
    scores = dot_tn(key_t, query_t)
    count = scores.shape[0]
    tail = scores[low:]
    rows = lax.broadcasted_iota(jnp.int32, tail.shape, 0) + low
    tail = jnp.where(rows < limit, tail, -1e9)
    return jnp.concatenate([scores[:low], tail], axis=0) if low else tail


def forward_attention(
    lens, x_ref, w_ref, gain_ref, bias_ref, bias_t_ref, cos_ref, sin_ref,
    q_ref, k_ref, v_ref, mix_ref, raw_ref, lse_ref, w_t,
):
    length = x_ref.shape[1]

    @pl.when(pl.program_id(0) == 0)
    def _():
        for j in range(3):
            w_t[j] = w_ref[pl.ds(j * D, D), :].T

    whitened, _ = whiten(x_ref[0].astype(F32))
    hidden = (whitened * gain_ref[0:1, :] + bias_ref[0:1, :]).astype(BF)
    cosine, sine = cos_ref[...], sin_ref[...]
    scale = 1.0 / math.sqrt(HEAD)
    for j, out_ref in enumerate((q_ref, k_ref, v_ref)):
        lin = dot_nt(w_t[j], hidden) + bias_t_ref[:, 2 + j : 3 + j]
        if j < 2:
            first, second = halves(lin)
            lin = joined(first * cosine - second * sine, second * cosine + first * sine)
            if j == 0:
                lin = lin * scale
        out_ref[0] = lin.astype(BF)

    limit = lens[pl.program_id(0)]
    low_edge = 0
    for extent in key_extents(length):
        base = extent - 128 if extent % 128 == 0 else extent // 128 * 128

        @pl.when((limit > low_edge) & (limit <= extent))
        def _(extent=extent, base=base if low_edge else 128):
            def group(g, carry):
                for h in range(4):
                    at = pl.ds(pl.multiple_of(g * 128 + h * HEAD, HEAD), HEAD)
                    scores = score_block(
                        k_ref[0, at, 0:extent], q_ref[0, at, :], base, limit
                    )
                    peak = jnp.max(scores, axis=0, keepdims=True)
                    exponent = jnp.exp(scores - peak)
                    total = jnp.sum(exponent, axis=0, keepdims=True)
                    mixed = dot_nn(v_ref[0, at, 0:extent], exponent.astype(BF)) / total
                    raw_ref[0, at, :] = mixed
                    mix_ref[0, at, :] = mixed.astype(BF)
                    lse_ref[0, g, h : h + 1, :] = peak + jnp.log(total)
                return carry

            lax.fori_loop(0, HEADS // 4, group, 0)

        low_edge = extent


def backward_attention(
    lens, x_ref, w_ref, gain_ref, bias_ref, cos_ref, sin_ref,
    q_ref, k_ref, v_ref, gmix_ref, raw_ref, lse_ref, gmid_ref,
    gx_ref, gw_ref, small_ref, gbias_ref, w_t, g_t,
):
    length = x_ref.shape[1]
    step = pl.program_id(0)

    @pl.when(step == 0)
    def _():
        for j in range(3):
            w_t[pl.ds(j * D, D), :] = w_ref[pl.ds(j * D, D), :].T
        gw_ref[...] = jnp.zeros_like(gw_ref)
        small_ref[...] = jnp.zeros_like(small_ref)
        gbias_ref[...] = jnp.zeros_like(gbias_ref)

    limit = lens[step]
    scale = 1.0 / math.sqrt(HEAD)
    low_edge = 0
    for extent in key_extents(length):
        base = extent - 128 if extent % 128 == 0 else extent // 128 * 128

        @pl.when((limit > low_edge) & (limit <= extent))
        def _(extent=extent, base=base if low_edge else 128):
            cosine, sine = cos_ref[...], sin_ref[...]
            if extent < length:
                g_t[pl.ds(D, 2 * D), extent:length] = jnp.zeros((2 * D, length - extent), BF)

            def back_turn(w, c, s):
                first, second = w[:HALF], w[HALF:]
                return jnp.concatenate(
                    [first * c + second * s, second * c - first * s], axis=0
                ).astype(BF)

            def group(g, carry):
                for h in range(4):
                    start = pl.multiple_of(g * 128 + h * HEAD, HEAD)
                    at = pl.ds(start, HEAD)
                    query, key = q_ref[0, at, :], k_ref[0, at, 0:extent]
                    grad_mixed = gmix_ref[0, at, :]
                    scores = score_block(key, query, base, limit)
                    probs = jnp.exp(scores - lse_ref[0, g, h : h + 1, :])
                    inner = jnp.sum(
                        raw_ref[0, at, :] * grad_mixed.astype(F32), axis=0, keepdims=True
                    )
                    grad_probs = dot_tn(v_ref[0, at, 0:extent], grad_mixed)
                    grad_scores = (probs * (grad_probs - inner)).astype(BF)
                    grad_value = dot_nt(grad_mixed, probs.astype(BF))
                    grad_key = dot_nt(query, grad_scores)
                    grad_query = dot_nn(key, grad_scores) * scale
                    g_t[pl.ds(start, HEAD), :] = back_turn(grad_query, cosine, sine)
                    g_t[pl.ds(start + D, HEAD), 0:extent] = back_turn(
                        grad_key, cosine[:, 0:extent], sine[:, 0:extent]
                    )
                    g_t[pl.ds(start + 2 * D, HEAD), 0:extent] = grad_value.astype(BF)
                return carry

            lax.fori_loop(0, HEADS // 4, group, 0)

        low_edge = extent

    whitened, inverse = whiten(x_ref[0].astype(F32))
    gain = gain_ref[0:1, :]
    hidden = (whitened * gain + bias_ref[0:1, :]).astype(BF)
    hidden_t = hidden.T
    grads = g_t[...]
    gbias_ref[...] += jnp.sum(grads.astype(F32), axis=1, keepdims=True)
    grad_hidden = dot_tn(grads, w_t[...])
    for j in range(3):
        gw_ref[pl.ds(j * D, D), :] += dot_nt(hidden_t, grads[j * D : (j + 1) * D])
    small_ref[0:1, :] += jnp.sum(grad_hidden * whitened, axis=0, keepdims=True)
    small_ref[1:2, :] += jnp.sum(grad_hidden, axis=0, keepdims=True)
    gx_ref[0] = gmid_ref[0] + whiten_back(grad_hidden, whitened, inverse, gain)


def feed_forward(
    x_ref, mix_ref, wo_ref, gain_ref, bias_ref, cot_ref, u_ref, v_ref, fbias_ref,
    head_ref, label_ref, live_ref,
    out_ref, gmid_ref, gmix_ref, gu_ref, gv_ref, gfb_ref, gwo_ref, small_ref, stat_ref,
    middle, hidden, cot, down, grad_hidden, act_low, grad_low,
):
    seqs, length = x_ref.shape[0], x_ref.shape[1]
    pad = hidden.shape[0] // seqs
    step = pl.program_id(0)

    @pl.when(step == 0)
    def _():
        for s in range(seqs):
            branch = dot_tn(mix_ref[s], wo_ref[...]) + bias_ref[5:6, :]
            mid = x_ref[s].astype(F32) + branch
            middle[s] = mid
            whitened, _ = whiten(mid)
            low = (whitened * gain_ref[1:2, :] + bias_ref[1:2, :]).astype(BF)
            blank = jnp.zeros((pad - length, D), BF)
            hidden[pl.ds(s * pad, pad), :] = jnp.concatenate([low, blank], axis=0)
            cot[pl.ds(s * pad, pad), :] = jnp.concatenate([cot_ref[s], blank], axis=0)
        down[...] = jnp.zeros_like(down)
        grad_hidden[...] = jnp.zeros_like(grad_hidden)

    up_w, down_w = u_ref[0], v_ref[0]
    fbias = fbias_ref[0]
    total = jnp.zeros_like(fbias)
    for s in range(seqs):
        rows = pl.ds(s * pad, pad)
        upward = dot_nt(hidden[rows, :], up_w) + fbias
        grad_act = dot_nt(cot[rows, :], down_w)
        phi = 0.5 * (1.0 + lax.erf(upward * ROOT_HALF))
        act = (upward * phi).astype(BF)
        slope = phi + upward * jnp.exp(-0.5 * upward * upward) * INV_ROOT_TWO_PI
        grad_up = (grad_act * slope).astype(BF)
        act_low[rows, :] = act
        grad_low[rows, :] = grad_up
        total += jnp.sum(grad_up.astype(F32), axis=0, keepdims=True)
        down[rows, :] += dot_nn(act, down_w)
        grad_hidden[rows, :] += dot_nn(grad_up, up_w)
    gfb_ref[0] = total
    gu_ref[0] = dot_tn(grad_low[...], hidden[...])
    gv_ref[0] = dot_tn(act_low[...], cot[...])

    @pl.when(step == pl.num_programs(0) - 1)
    def _():
        gain = gain_ref[1:2, :]
        gain_sum = jnp.zeros((1, D), F32)
        shift_sum = jnp.zeros((1, D), F32)
        branch_sum = jnp.zeros((1, D), F32)
        cot_sum = jnp.zeros((1, D), F32)
        loglik = jnp.zeros((1, length), F32)
        hits = jnp.zeros((1, length), F32)
        gwo_ref[...] = jnp.zeros_like(gwo_ref)
        for s in range(seqs):
            rows = pl.ds(s * pad, length)
            mid = middle[s]
            final = mid + (down[rows, :] + bias_ref[6:7, :])
            out_ref[s] = final.astype(BF)
            unit, _ = whiten(final)
            logits = dot_nt(head_ref[...], unit.astype(BF))
            slot = lax.broadcasted_iota(jnp.int32, logits.shape, 0)
            logits = jnp.where(slot < VOCAB, logits, -1e30)
            shifted = logits - jnp.max(logits, axis=0, keepdims=True)
            logprob = shifted - jnp.log(jnp.sum(jnp.exp(shifted), axis=0, keepdims=True))
            picked = jnp.sum(
                jnp.where(slot == label_ref[s : s + 1, :], logprob, 0.0), axis=0, keepdims=True
            )
            live = live_ref[s : s + 1, :] != 0
            loglik += jnp.where(live, picked, 0.0)
            hits += jnp.where(live, jnp.exp(picked), 0.0)

            gradient = grad_hidden[rows, :]
            whitened, inverse = whiten(mid)
            gain_sum += jnp.sum(gradient * whitened, axis=0, keepdims=True)
            shift_sum += jnp.sum(gradient, axis=0, keepdims=True)
            own = cot_ref[s].astype(F32)
            cot_sum += jnp.sum(own, axis=0, keepdims=True)
            grad_mid = own + whiten_back(gradient, whitened, inverse, gain)
            gmid_ref[s] = grad_mid
            low = grad_mid.astype(BF)
            branch_sum += jnp.sum(low.astype(F32), axis=0, keepdims=True)
            gmix_ref[s] = dot_nt(wo_ref[...], low).astype(BF)
            gwo_ref[...] += dot_nn(mix_ref[s], low)
        small_ref[0:1, :] = gain_sum
        small_ref[1:2, :] = shift_sum
        small_ref[2:3, :] = branch_sum
        small_ref[3:4, :] = cot_sum
        stat_ref[0:1, :] = jnp.broadcast_to(jnp.sum(loglik, axis=1, keepdims=True), (1, 128))
        stat_ref[1:2, :] = jnp.broadcast_to(jnp.sum(hits, axis=1, keepdims=True), (1, 128))


def whole(shape):
    return pl.BlockSpec(shape, lambda *_: (0,) * len(shape))


def leading(shape):
    return pl.BlockSpec((1,) + tuple(shape[1:]), lambda i, *_: (i,) + (0,) * (len(shape) - 1))


def shaped(shape, dtype=F32):
    return jax.ShapeDtypeStruct(shape, dtype)


def attention_forward(lengths, tokens, attn, gains, biases, biases_t, cosine, sine):
    seqs, length, _ = tokens.shape
    flat = (seqs, D, length)
    lse = (seqs, HEADS // 4, 4, length)
    return pl.pallas_call(
        forward_attention,
        grid_spec=pltpu.PrefetchScalarGridSpec(
            num_scalar_prefetch=1,
            grid=(seqs,),
            in_specs=[
                leading(tokens.shape), whole(attn.shape), whole(gains.shape),
                whole(biases.shape), whole(biases_t.shape), whole(cosine.shape),
                whole(sine.shape),
            ],
            out_specs=[leading(flat)] * 5 + [leading(lse)],
            scratch_shapes=[pltpu.VMEM((3, D, D), BF)],
        ),
        out_shape=[shaped(flat, BF)] * 4 + [shaped(flat), shaped(lse)],
        compiler_params=pltpu.CompilerParams(vmem_limit_bytes=VMEM_LIMIT),
        name="attention_forward",
    )(lengths, tokens, attn, gains, biases, biases_t, cosine, sine)


def attention_backward(
    lengths, tokens, attn, gains, biases, cosine, sine, query, key, value, grad_mixed, raw,
    lse, grad_middle,
):
    seqs, length, _ = tokens.shape
    operands = (query, key, value, grad_mixed, raw, lse, grad_middle)
    return pl.pallas_call(
        backward_attention,
        grid_spec=pltpu.PrefetchScalarGridSpec(
            num_scalar_prefetch=1,
            grid=(seqs,),
            in_specs=[
                leading(tokens.shape), whole(attn.shape), whole(gains.shape),
                whole(biases.shape), whole(cosine.shape), whole(sine.shape),
            ]
            + [leading(item.shape) for item in operands],
            out_specs=[
                leading(tokens.shape), whole((3 * D, D)), whole((8, D)), whole((3 * D, 1)),
            ],
            scratch_shapes=[pltpu.VMEM((3 * D, D), BF), pltpu.VMEM((3 * D, length), BF)],
        ),
        out_shape=[
            shaped(tokens.shape), shaped((3 * D, D)), shaped((8, D)), shaped((3 * D, 1)),
        ],
        compiler_params=pltpu.CompilerParams(vmem_limit_bytes=VMEM_LIMIT),
        name="attention_backward",
    )(lengths, tokens, attn, gains, biases, cosine, sine, *operands)


def feed_forward_both(
    tokens, mixed, w_out, gains, biases, cotangent, up_w, down_w, fbias, head_t, labels, live,
    chunk,
):
    seqs, length, _ = tokens.shape
    pad = (length + 15) // 16 * 16
    hidden_units = up_w.shape[0]
    steps = hidden_units // chunk
    rows = seqs * pad
    chunked = (steps, chunk, D)
    return pl.pallas_call(
        feed_forward,
        grid=(steps,),
        in_specs=[
            whole(tokens.shape), whole(mixed.shape), whole(w_out.shape), whole(gains.shape),
            whole(biases.shape), whole(cotangent.shape), leading(chunked), leading(chunked),
            leading((steps, 1, chunk)), whole(head_t.shape), whole(labels.shape),
            whole(live.shape),
        ],
        out_specs=[
            whole(tokens.shape), whole(tokens.shape), whole(mixed.shape), leading(chunked),
            leading(chunked), leading((steps, 1, chunk)), whole((D, D)), whole((8, D)),
            whole((8, 128)),
        ],
        out_shape=[
            shaped(tokens.shape, BF), shaped(tokens.shape), shaped(mixed.shape, BF),
            shaped(chunked), shaped(chunked), shaped((steps, 1, chunk)), shaped((D, D)),
            shaped((8, D)), shaped((8, 128)),
        ],
        scratch_shapes=[
            pltpu.VMEM(tokens.shape, F32),
            pltpu.VMEM((rows, D), BF),
            pltpu.VMEM((rows, D), BF),
            pltpu.VMEM((rows, D), F32),
            pltpu.VMEM((rows, D), F32),
            pltpu.VMEM((rows, chunk), BF),
            pltpu.VMEM((rows, chunk), BF),
        ],
        compiler_params=pltpu.CompilerParams(vmem_limit_bytes=VMEM_LIMIT),
        name="feed_forward",
    )(
        tokens, mixed, w_out, gains, biases, cotangent, up_w.reshape(chunked),
        down_w.reshape(chunked), fbias.reshape(steps, 1, chunk), head_t, labels, live,
    )


def per_device(
    tokens, lengths, masked_flags, labels, attn_weights, ffn_weights, ffn_bias, norm_gains,
    biases, head_weight, cotangent,
):
    both = ("wide", "narrow")
    seqs, length, _ = tokens.shape
    wide, narrow = lax.axis_size("wide"), lax.axis_size("narrow")
    devices = wide * narrow
    shard = D // wide
    attn_full = lax.all_gather(attn_weights, both, axis=0, tiled=True)
    pack = jnp.concatenate([norm_gains.reshape(-1), biases.reshape(-1), ffn_bias])[None]
    packs = lax.all_gather(pack, both, axis=0, tiled=True)
    ffn_full = lax.all_gather(ffn_weights, both, axis=1, tiled=True)
    rows = packs.reshape(wide, narrow, -1)[:, 0, : 9 * shard].reshape(wide, 9, shard)
    rows = rows.transpose(1, 0, 2).reshape(9, D).astype(F32)
    gain_rows = rows[:2]
    bias_rows = jnp.concatenate([rows[2:], jnp.zeros((1, D), F32)], axis=0)
    ffn_bias_full = packs[:, 9 * shard :].reshape(-1).astype(F32)

    cosine, sine = rotary_tables(length)
    query, key, value, mixed, raw, lse = attention_forward(
        lengths, tokens, attn_full, gain_rows, bias_rows, bias_rows.T, cosine, sine
    )
    live = (masked_flags == 1) & (jnp.arange(length)[None, :] < lengths[:, None])
    head_t = jnp.pad(head_weight.T, ((0, 7), (0, 0)))
    (
        output, grad_middle, grad_mixed, grad_up_w, grad_down_w, grad_fbias, grad_wo, small_two,
        stats,
    ) = feed_forward_both(
        tokens, mixed, attn_full[3 * D :], gain_rows, bias_rows, cotangent, ffn_full[0],
        ffn_full[1], ffn_bias_full, head_t, labels, live.astype(jnp.int32), 512,
    )
    hidden_units = ffn_full.shape[1]
    grad_ffn_full = jnp.stack(
        [grad_up_w.reshape(hidden_units, D), grad_down_w.reshape(hidden_units, D)]
    )
    grad_ffn = lax.psum_scatter(grad_ffn_full, both, scatter_dimension=1, tiled=True)
    grad_tokens, grad_qkv, small_one, grad_qkv_bias = attention_backward(
        lengths, tokens, attn_full, gain_rows, bias_rows, cosine, sine, query, key, value,
        grad_mixed, raw, lse, grad_middle,
    )
    grad_attn = lax.psum_scatter(
        jnp.concatenate([grad_qkv, grad_wo], axis=0), both, scatter_dimension=0, tiled=True
    )
    sums = jnp.concatenate(
        [
            small_one[0], small_two[0], small_one[1], small_two[1], grad_qkv_bias.reshape(-1),
            small_two[2], small_two[3], grad_fbias.reshape(-1), stats[:2, 0],
        ]
    )
    sums = lax.psum(sums, both)
    at = lax.axis_index("wide")
    per_row = lax.dynamic_slice_in_dim(sums[: 9 * D].reshape(9, D), at * shard, shard, 1)
    owner = at * narrow + lax.axis_index("narrow")
    units = ffn_bias.shape[0]
    grad_ffn_bias = lax.dynamic_slice_in_dim(sums, 9 * D + owner * units, units, 0)
    head_stats = (
        sums[-2:] * jnp.array([1.0, VOCAB], F32) / (seqs * length * devices)
    )
    return (
        output, grad_tokens, grad_attn, grad_ffn, grad_ffn_bias, per_row[:2], per_row[2:],
        head_stats,
    )


def solution(mesh):
    both = ("wide", "narrow")
    return jax.shard_map(
        per_device,
        mesh=mesh,
        in_specs=(
            P(both, None, None),
            P(both),
            P(both, None),
            P(both, None),
            P(both, None),
            P(None, both, None),
            P(both),
            P(None, "wide"),
            P(None, "wide"),
            P(),
            P(both, None, None),
        ),
        out_specs=(
            P(both, None, None),
            P(both, None, None),
            P(both, None),
            P(None, both, None),
            P(both),
            P(None, "wide"),
            P(None, "wide"),
            P(),
        ),
        check_vma=False,
    )
```

```python
import functools
import math

import jax
import jax.numpy as jnp
import numpy as np
from jax import lax
from jax.experimental import pallas as pl
from jax.experimental.pallas import tpu as pltpu
from jax.sharding import PartitionSpec as P

D = 640
HEADS = 20
HEAD = 32
HALF = HEAD // 2
VOCAB = 33
EPS = 1e-05
ROOT_HALF = 0.7071067811865476
INV_ROOT_TWO_PI = 0.3989422804014327
BF = jnp.bfloat16
F32 = jnp.float32
VMEM_LIMIT = 60 << 20

MESH = pl.DeviceIdType.MESH
ROWS = 16


def position():
    wide, narrow = lax.axis_index("wide"), lax.axis_index("narrow")
    return {
        "z": lax.div(wide, 2), "x": lax.rem(wide, 2),
        "y": lax.div(narrow, 2), "c": lax.rem(narrow, 2),
    }


def partner(me, axis, offset, size):
    there = dict(me)
    there[axis] = lax.rem(me[axis] + offset, size)
    return (there["z"] * 2 + there["x"], there["y"] * 2 + there["c"])


def meet(me, layers):
    barrier = pltpu.get_barrier_semaphore()
    peers = [partner(me, axis, 1, 2) for axis in "cyx"]
    peers += [partner(me, "z", offset, layers) for offset in range(1, layers)]
    for peer in peers:
        pl.semaphore_signal(barrier, inc=1, device_id=peer, device_id_type=MESH)
    pl.semaphore_wait(barrier, len(peers))


def reduce_scratch(slots, layers):
    def blocks(count, dtype):
        return pltpu.VMEM((slots, count, ROWS, D), dtype)

    return [
        blocks(4 * layers, BF), blocks(4 * layers, BF),
        blocks(2 * layers, BF), blocks(2 * layers, BF), blocks(2 * layers, F32),
        blocks(layers, BF), blocks(layers, BF), blocks(layers, F32),
        blocks(layers, BF), blocks(layers, BF), blocks(1, F32),
        pltpu.SemaphoreType.DMA((slots, 3 + layers)),
        pltpu.SemaphoreType.DMA((slots, 3 + layers)),
    ]


class PieceReduce:
    def __init__(self, me, layers, refs, slot, first):
        (
            self.s0, self.r0, self.s1, self.r1, self.k1, self.s2, self.r2, self.k2,
            self.s3, self.r3, self.k3,
        ) = (ref.at[slot] for ref in refs[:11])
        self.send, self.recv = (ref.at[slot] for ref in refs[11:])
        self.me, self.layers = me, layers
        self.first, self.second = ("y", "x") if first == "y" else ("x", "y")

    def exchange(self, stage, source, target, axis):
        return pltpu.make_async_remote_copy(
            src_ref=source, dst_ref=target, send_sem=self.send.at[stage],
            recv_sem=self.recv.at[stage], device_id=partner(self.me, axis, 1, 2),
            device_id_type=MESH,
        )

    def layer_copies(self):
        me, layers = self.me, self.layers
        return [
            pltpu.make_async_remote_copy(
                src_ref=self.s3.at[lax.rem(me["z"] + offset, layers)],
                dst_ref=self.r3.at[offset], send_sem=self.send.at[2 + offset],
                recv_sem=self.recv.at[2 + offset],
                device_id=partner(me, "z", offset, layers), device_id_type=MESH,
            )
            for offset in range(1, layers)
        ]

    def rest(self, along, other):
        return other * 2 + along if self.first == "y" else along * 2 + other

    def over_cores(self, get):
        core = self.me["c"]
        for layer in range(self.layers):
            for rest in range(4):
                self.s0[layer * 4 + rest] = get(layer, rest, 1 - core).astype(BF)
        self.exchange(0, self.s0, self.r0, "c").start()

    def over_first(self, get):
        self.exchange(0, self.s0, self.r0, "c").wait()
        core, along = self.me["c"], self.me[self.first]
        for layer in range(self.layers):
            for other in range(2):
                away, near = self.rest(1 - along, other), self.rest(along, other)
                at = layer * 2 + other
                self.s1[at] = (
                    get(layer, away, core) + self.r0[layer * 4 + away].astype(F32)
                ).astype(BF)
                self.k1[at] = get(layer, near, core) + self.r0[layer * 4 + near].astype(F32)
        self.exchange(1, self.s1, self.r1, self.first).start()

    def over_second(self):
        self.exchange(1, self.s1, self.r1, self.first).wait()
        along = self.me[self.second]
        for layer in range(self.layers):
            away, near = layer * 2 + (1 - along), layer * 2 + along
            self.s2[layer] = (self.k1[away] + self.r1[away].astype(F32)).astype(BF)
            self.k2[layer] = self.k1[near] + self.r1[near].astype(F32)
        self.exchange(2, self.s2, self.r2, self.second).start()

    def over_layers(self):
        self.exchange(2, self.s2, self.r2, self.second).wait()
        own = self.me["z"]
        for layer in range(self.layers):
            self.s3[layer] = (self.k2[layer] + self.r2[layer].astype(F32)).astype(BF)
        self.k3[0] = self.k2[own] + self.r2[own].astype(F32)
        for copy in self.layer_copies():
            copy.start()

    def finish(self):
        for copy in self.layer_copies():
            copy.wait()
        total = self.k3[0]
        for offset in range(1, self.layers):
            total = total + self.r3[offset].astype(F32)
        return total


class SmallReduce:
    def __init__(self, me, layers, sent, got, send, recv):
        self.me, self.layers = me, layers
        self.sent, self.got, self.send, self.recv = sent, got, send, recv

    def exchange(self, stage):
        return pltpu.make_async_remote_copy(
            src_ref=self.sent.at[stage], dst_ref=self.got.at[stage],
            send_sem=self.send.at[stage], recv_sem=self.recv.at[stage],
            device_id=partner(self.me, "cyx"[stage], 1, 2), device_id_type=MESH,
        )

    def layer_copies(self):
        own = self.me["z"]
        return [
            pltpu.make_async_remote_copy(
                src_ref=self.sent.at[3], dst_ref=self.got.at[3 + own],
                send_sem=self.send.at[2 + offset], recv_sem=self.recv.at[2 + offset],
                device_id=partner(self.me, "z", offset, self.layers), device_id_type=MESH,
            )
            for offset in range(1, self.layers)
        ]

    def start(self, stage):
        if stage:
            self.exchange(stage - 1).wait()
            self.sent[stage] = self.sent[stage - 1] + self.got[stage - 1]
        if stage < 3:
            self.exchange(stage).start()
        else:
            for copy in self.layer_copies():
                copy.start()
            self.got[3 + self.me["z"]] = self.sent[3]

    def finish(self):
        for copy in self.layer_copies():
            copy.wait()
        total = self.got[3]
        for layer in range(1, self.layers):
            total = total + self.got[3 + layer]
        return total


def gradient_tail(layers, pieces, qkv_ref, wo_ref, one_ref, two_ref, units_ref,
                  grad_ref, sums_ref, sent, got, small_send, small_recv, *refs):
    me = position()
    meet(me, layers)
    sent[0, 0:8] = one_ref[...]
    sent[0, 8:16] = two_ref[...]
    for k in range(8):
        sent[0, 16 + k : 17 + k] = units_ref[k]
    small = SmallReduce(me, layers, sent, got, small_send, small_recv)
    small.start(0)

    def getter(piece):
        rows = slice(piece * ROWS, (piece + 1) * ROWS)

        def get(layer, rest, core):
            at = rest * 2 + core
            return wo_ref[at, rows] if layer == 3 else qkv_ref[layer * 8 + at, rows]

        return get

    ops = [PieceReduce(me, layers, refs, p, "yx"[p % 2]) for p in range(pieces)]
    for p, op in enumerate(ops):
        op.over_cores(getter(p))
    small.start(1)
    for p, op in enumerate(ops):
        op.over_first(getter(p))
    small.start(2)
    for op in ops:
        op.over_second()
    small.start(3)
    for op in ops:
        op.over_layers()
    for p, op in enumerate(ops):
        grad_ref[p * ROWS : (p + 1) * ROWS] = op.finish()
    sums_ref[...] = small.finish()


def dot_nn(a, b):
    return lax.dot_general(a, b, (((1,), (0,)), ((), ())), preferred_element_type=F32)


def dot_nt(a, b):
    return lax.dot_general(a, b, (((1,), (1,)), ((), ())), preferred_element_type=F32)


def dot_tn(a, b):
    return lax.dot_general(a, b, (((0,), (0,)), ((), ())), preferred_element_type=F32)


def matrix(ref, j):
    rows = ref.shape[1]
    blocks = D // rows
    return ref[j * blocks : (j + 1) * blocks].reshape(D, D)


def whiten(values):
    center = jnp.mean(values, axis=-1, keepdims=True)
    offset = values - center
    spread = jnp.mean(offset * offset, axis=-1, keepdims=True)
    inverse = lax.rsqrt(spread + EPS)
    return offset * inverse, inverse


def whiten_back(gradient, whitened, inverse, gain):
    scaled = gradient * gain
    mean_grad = jnp.mean(scaled, axis=-1, keepdims=True)
    mean_cross = jnp.mean(scaled * whitened, axis=-1, keepdims=True)
    return inverse * (scaled - mean_grad - whitened * mean_cross)


def rotary_tables(length):
    frequency = (
        np.float32(1.0)
        / np.float32(10000.0) ** (np.arange(HALF, dtype=np.float32) * np.float32(2.0 / HEAD))
    ).astype(np.float32)
    angles = frequency[:, None] * np.arange(length, dtype=np.float32)[None, :]
    return np.cos(angles).astype(np.float32), np.sin(angles).astype(np.float32)


def key_extents(length):
    extents = list(range(256, length, 128))
    return extents + [length]


def halves(values):
    length = values.shape[-1]
    split = values.reshape(values.shape[0] // HEAD, 2, HALF, length)
    return split[:, 0], split[:, 1]


def joined(first, second):
    length = first.shape[-1]
    both = jnp.concatenate([first[:, None], second[:, None]], axis=1)
    return both.reshape(first.shape[0] * HEAD, length)


def score_block(key_t, query_t, low, limit):
    scores = dot_tn(key_t, query_t)
    count = scores.shape[0]
    tail = scores[low:]
    rows = lax.broadcasted_iota(jnp.int32, tail.shape, 0) + low
    tail = jnp.where(rows < limit, tail, -1e9)
    return jnp.concatenate([scores[:low], tail], axis=0) if low else tail


def forward_attention(
    lens, x_ref, w_ref, gain_ref, bias_ref, bias_t_ref, cos_ref, sin_ref,
    q_ref, k_ref, v_ref, mix_ref, raw_ref, lse_ref, w_t,
):
    length = x_ref.shape[1]

    @pl.when(pl.program_id(0) == 0)
    def _():
        for j in range(3):
            w_t[j] = matrix(w_ref, j).T

    whitened, _ = whiten(x_ref[0].astype(F32))
    hidden = (whitened * gain_ref[0:1, :] + bias_ref[0:1, :]).astype(BF)
    cosine, sine = cos_ref[...], sin_ref[...]
    scale = 1.0 / math.sqrt(HEAD)
    for j, out_ref in enumerate((q_ref, k_ref, v_ref)):
        lin = dot_nt(w_t[j], hidden) + bias_t_ref[:, 2 + j : 3 + j]
        if j < 2:
            first, second = halves(lin)
            lin = joined(first * cosine - second * sine, second * cosine + first * sine)
            if j == 0:
                lin = lin * scale
        out_ref[0] = lin.astype(BF)

    limit = lens[pl.program_id(0)]
    low_edge = 0
    for extent in key_extents(length):
        base = extent - 128 if extent % 128 == 0 else extent // 128 * 128

        @pl.when((limit > low_edge) & (limit <= extent))
        def _(extent=extent, base=base if low_edge else 128):
            def group(g, carry):
                for h in range(4):
                    at = pl.ds(pl.multiple_of(g * 128 + h * HEAD, HEAD), HEAD)
                    scores = score_block(
                        k_ref[0, at, 0:extent], q_ref[0, at, :], base, limit
                    )
                    peak = jnp.max(scores, axis=0, keepdims=True)
                    exponent = jnp.exp(scores - peak)
                    total = jnp.sum(exponent, axis=0, keepdims=True)
                    mixed = dot_nn(v_ref[0, at, 0:extent], exponent.astype(BF)) / total
                    raw_ref[0, at, :] = mixed
                    mix_ref[0, at, :] = mixed.astype(BF)
                    lse_ref[0, g, h : h + 1, :] = peak + jnp.log(total)
                return carry

            lax.fori_loop(0, HEADS // 4, group, 0)

        low_edge = extent


def backward_attention(
    lens, x_ref, w_ref, gain_ref, bias_ref, cos_ref, sin_ref,
    q_ref, k_ref, v_ref, gmix_ref, raw_ref, lse_ref, gmid_ref,
    gx_ref, gw_ref, small_ref, w_t, g_t,
):
    length = x_ref.shape[1]
    step = pl.program_id(0)

    @pl.when(step == 0)
    def _():
        for j in range(3):
            w_t[pl.ds(j * D, D), :] = matrix(w_ref, j).T
        gw_ref[...] = jnp.zeros_like(gw_ref)
        small_ref[...] = jnp.zeros_like(small_ref)

    limit = lens[step]
    scale = 1.0 / math.sqrt(HEAD)
    low_edge = 0
    for extent in key_extents(length):
        base = extent - 128 if extent % 128 == 0 else extent // 128 * 128

        @pl.when((limit > low_edge) & (limit <= extent))
        def _(extent=extent, base=base if low_edge else 128):
            cosine, sine = cos_ref[...], sin_ref[...]
            if extent < length:
                g_t[pl.ds(D, 2 * D), extent:length] = jnp.zeros((2 * D, length - extent), BF)

            def back_turn(w, c, s):
                first, second = w[:HALF], w[HALF:]
                return jnp.concatenate(
                    [first * c + second * s, second * c - first * s], axis=0
                ).astype(BF)

            def group(g, carry):
                for h in range(4):
                    start = pl.multiple_of(g * 128 + h * HEAD, HEAD)
                    at = pl.ds(start, HEAD)
                    query, key = q_ref[0, at, :], k_ref[0, at, 0:extent]
                    grad_mixed = gmix_ref[0, at, :]
                    scores = score_block(key, query, base, limit)
                    probs = jnp.exp(scores - lse_ref[0, g, h : h + 1, :])
                    inner = jnp.sum(
                        raw_ref[0, at, :] * grad_mixed.astype(F32), axis=0, keepdims=True
                    )
                    grad_probs = dot_tn(v_ref[0, at, 0:extent], grad_mixed)
                    grad_scores = (probs * (grad_probs - inner)).astype(BF)
                    grad_value = dot_nt(grad_mixed, probs.astype(BF))
                    grad_key = dot_nt(query, grad_scores)
                    grad_query = dot_nn(key, grad_scores) * scale
                    g_t[pl.ds(start, HEAD), :] = back_turn(grad_query, cosine, sine)
                    g_t[pl.ds(start + D, HEAD), 0:extent] = back_turn(
                        grad_key, cosine[:, 0:extent], sine[:, 0:extent]
                    )
                    g_t[pl.ds(start + 2 * D, HEAD), 0:extent] = grad_value.astype(BF)
                return carry

            lax.fori_loop(0, HEADS // 4, group, 0)

        low_edge = extent

    whitened, inverse = whiten(x_ref[0].astype(F32))
    gain = gain_ref[0:1, :]
    hidden = (whitened * gain + bias_ref[0:1, :]).astype(BF)
    hidden_t = hidden.T
    grads = g_t[...]
    ones = jnp.ones((8, length), BF)
    for j in range(3):
        part = grads[j * D : (j + 1) * D]
        small_ref[2 + j : 3 + j, :] += dot_nt(ones, part)[0:1]
    grad_hidden = dot_tn(grads, w_t[...])
    for j in range(3):
        gw_ref[pl.ds(j * D, D), :] += dot_nt(hidden_t, grads[j * D : (j + 1) * D])
    small_ref[0:1, :] += jnp.sum(grad_hidden * whitened, axis=0, keepdims=True)
    small_ref[1:2, :] += jnp.sum(grad_hidden, axis=0, keepdims=True)
    gx_ref[0] = gmid_ref[0] + whiten_back(grad_hidden, whitened, inverse, gain)


def feed_forward(
    layers,
    x_ref, mix_ref, wo_ref, gain_ref, bias_ref, cot_ref, u_ref, v_ref, fbias_ref,
    head_ref, label_ref, live_ref,
    out_ref, gmid_ref, gmix_ref, gu_ref, gv_ref, gfb_ref, gwo_ref, small_ref,
    middle, hidden, cot, down, grad_hidden, act_low, grad_low, *comm,
):
    seqs, length = x_ref.shape[0], x_ref.shape[1]
    pad = hidden.shape[0] // seqs
    step = pl.program_id(0)
    last = pl.num_programs(0) - 1
    chunk = act_low.shape[1]
    if layers:
        me = position()
        terms, comm = comm[:2], comm[2:]

        def pieces(k):
            slot = lax.rem(k, 2) * 2
            return [PieceReduce(me, layers, comm, slot + j, "yx"[j]) for j in range(2)]

        def getter(j):
            def get(layer, rest, core):
                at = ((layer * 4 + rest) * 2 + core) * ROWS
                return terms[j][pl.ds(pl.multiple_of(at, ROWS), ROWS), :]

            return get

        def over_first(k):
            for j, op in enumerate(pieces(k)):
                op.over_first(getter(j))

        def over_second(k):
            for op in pieces(k):
                op.over_second()

        def over_layers(k):
            for op in pieces(k):
                op.over_layers()

        def finish(k):
            rows = pl.ds(pl.multiple_of(k * ROWS, ROWS), ROWS)
            for op, ref in zip(pieces(k), (gu_ref, gv_ref)):
                ref[rows, :] = op.finish()

    def later(stage, delay):
        if layers:
            pl.when(step >= delay)(lambda: stage(step - delay))

    @pl.when(step == 0)
    def _():
        if layers:
            meet(me, layers)
        for s in range(seqs):
            branch = dot_tn(mix_ref[s], matrix(wo_ref, 0)) + bias_ref[5:6, :]
            mid = x_ref[s].astype(F32) + branch
            middle[s] = mid
            whitened, _ = whiten(mid)
            low = (whitened * gain_ref[1:2, :] + bias_ref[1:2, :]).astype(BF)
            blank = jnp.zeros((pad - length, D), BF)
            hidden[pl.ds(s * pad, pad), :] = jnp.concatenate([low, blank], axis=0)
            cot[pl.ds(s * pad, pad), :] = jnp.concatenate([cot_ref[s], blank], axis=0)
        down[...] = jnp.zeros_like(down)
        grad_hidden[...] = jnp.zeros_like(grad_hidden)

    up_w = u_ref[0].reshape(chunk, D)
    down_w = v_ref[0].reshape(chunk, D)
    fbias = fbias_ref[0]
    total = jnp.zeros_like(fbias)
    for s in range(seqs):
        rows = pl.ds(s * pad, pad)
        upward = dot_nt(hidden[rows, :], up_w) + fbias
        grad_act = dot_nt(cot[rows, :], down_w)
        phi = 0.5 * (1.0 + lax.erf(upward * ROOT_HALF))
        act = (upward * phi).astype(BF)
        slope = phi + upward * jnp.exp(-0.5 * upward * upward) * INV_ROOT_TWO_PI
        grad_up = (grad_act * slope).astype(BF)
        act_low[rows, :] = act
        grad_low[rows, :] = grad_up
        total += jnp.sum(grad_up.astype(F32), axis=0, keepdims=True)
        down[rows, :] += dot_nn(act, down_w)
        grad_hidden[rows, :] += dot_nn(grad_up, up_w)
        if layers:
            if s == 0:
                later(over_first, 1)
            if s == 1:
                later(finish, 2)
            if s == seqs - 1:
                later(over_second, 1)
    gfb_ref[0] = total
    grad_u = dot_tn(grad_low[...], hidden[...])
    if layers:
        terms[0][...] = grad_u
        later(over_layers, 1)
        terms[1][...] = dot_tn(act_low[...], cot[...])
        for j, op in enumerate(pieces(step)):
            op.over_cores(getter(j))
    else:
        gu_ref[0] = grad_u
        gv_ref[0] = dot_tn(act_low[...], cot[...])

    @pl.when(step == last)
    def _():
        gain = gain_ref[1:2, :]
        gain_sum = jnp.zeros((1, D), F32)
        shift_sum = jnp.zeros((1, D), F32)
        branch_sum = jnp.zeros((1, D), F32)
        cot_sum = jnp.zeros((1, D), F32)
        loglik = jnp.zeros((1, length), F32)
        hits = jnp.zeros((1, length), F32)
        gwo_ref[...] = jnp.zeros_like(gwo_ref)
        for s in range(seqs):
            rows = pl.ds(s * pad, length)
            mid = middle[s]
            final = mid + (down[rows, :] + bias_ref[6:7, :])
            out_ref[s] = final.astype(BF)
            unit, _ = whiten(final)
            logits = dot_nt(head_ref[...], unit.astype(BF))
            slot = lax.broadcasted_iota(jnp.int32, logits.shape, 0)
            logits = jnp.where(slot < VOCAB, logits, -1e30)
            shifted = logits - jnp.max(logits, axis=0, keepdims=True)
            logprob = shifted - jnp.log(jnp.sum(jnp.exp(shifted), axis=0, keepdims=True))
            picked = jnp.sum(
                jnp.where(slot == label_ref[s : s + 1, :], logprob, 0.0), axis=0, keepdims=True
            )
            live = live_ref[s : s + 1, :] != 0
            loglik += jnp.where(live, picked, 0.0)
            hits += jnp.where(live, jnp.exp(picked), 0.0)

            gradient = grad_hidden[rows, :]
            whitened, inverse = whiten(mid)
            gain_sum += jnp.sum(gradient * whitened, axis=0, keepdims=True)
            shift_sum += jnp.sum(gradient, axis=0, keepdims=True)
            own = cot_ref[s].astype(F32)
            cot_sum += jnp.sum(own, axis=0, keepdims=True)
            grad_mid = own + whiten_back(gradient, whitened, inverse, gain)
            gmid_ref[s] = grad_mid
            low = grad_mid.astype(BF)
            branch_sum += jnp.sum(low.astype(F32), axis=0, keepdims=True)
            gmix_ref[s] = dot_nt(matrix(wo_ref, 0), low).astype(BF)
            gwo_ref[...] += dot_nn(mix_ref[s], low)
            if layers:
                if s == 0:
                    over_first(last)
                    finish(last - 1)
                if s == seqs - 2:
                    over_second(last)
                if s == seqs - 1:
                    over_layers(last)
        small_ref[0:1, :] = gain_sum
        small_ref[1:2, :] = shift_sum
        small_ref[2:3, :] = branch_sum
        small_ref[3:4, :] = cot_sum
        small_ref[4:8, :] = jnp.zeros((4, D), F32)
        small_ref[4:5, 0:128] = jnp.broadcast_to(
            jnp.sum(loglik, axis=1, keepdims=True), (1, 128)
        )
        small_ref[4:5, 128:256] = jnp.broadcast_to(
            jnp.sum(hits, axis=1, keepdims=True), (1, 128)
        )
        if layers:
            finish(last)


def whole(shape):
    return pl.BlockSpec(shape, lambda *_: (0,) * len(shape), pipeline_mode=pl.Buffered(1))


def block_of(shape, *index):
    return pl.BlockSpec(shape, lambda *_: index, pipeline_mode=pl.Buffered(1))


def leading(shape):
    return pl.BlockSpec((1,) + tuple(shape[1:]), lambda i, *_: (i,) + (0,) * (len(shape) - 1))


def shaped(shape, dtype=F32):
    return jax.ShapeDtypeStruct(shape, dtype)


def projections(attn, first, count):
    blocks = attn.shape[0] // 4
    rows = D // blocks
    return block_of((blocks * count, rows, D), first // count, 0, 0)


def attention_forward(lengths, tokens, attn, gains, biases, biases_t, cosine, sine):
    seqs, length, _ = tokens.shape
    flat = (seqs, D, length)
    lse = (seqs, HEADS // 4, 4, length)
    return pl.pallas_call(
        forward_attention,
        grid_spec=pltpu.PrefetchScalarGridSpec(
            num_scalar_prefetch=1,
            grid=(seqs,),
            in_specs=[
                leading(tokens.shape), projections(attn, 0, 3), whole(gains.shape),
                whole(biases.shape), whole(biases_t.shape), whole(cosine.shape),
                whole(sine.shape),
            ],
            out_specs=[leading(flat)] * 5 + [leading(lse)],
            scratch_shapes=[pltpu.VMEM((3, D, D), BF)],
        ),
        out_shape=[shaped(flat, BF)] * 4 + [shaped(flat), shaped(lse)],
        compiler_params=pltpu.CompilerParams(vmem_limit_bytes=VMEM_LIMIT),
        name="attention_forward",
    )(lengths, tokens, attn, gains, biases, biases_t, cosine, sine)


def attention_backward(
    lengths, tokens, attn, gains, biases, cosine, sine, query, key, value, grad_mixed, raw,
    lse, grad_middle,
):
    seqs, length, _ = tokens.shape
    operands = (query, key, value, grad_mixed, raw, lse, grad_middle)
    return pl.pallas_call(
        backward_attention,
        grid_spec=pltpu.PrefetchScalarGridSpec(
            num_scalar_prefetch=1,
            grid=(seqs,),
            in_specs=[
                leading(tokens.shape), projections(attn, 0, 3), whole(gains.shape),
                whole(biases.shape), whole(cosine.shape), whole(sine.shape),
            ]
            + [leading(item.shape) for item in operands],
            out_specs=[
                leading(tokens.shape), whole((3 * D, D)), whole((8, D)),
            ],
            scratch_shapes=[pltpu.VMEM((3 * D, D), BF), pltpu.VMEM((3 * D, length), BF)],
        ),
        out_shape=[shaped(tokens.shape), shaped((3 * D, D)), shaped((8, D))],
        compiler_params=pltpu.CompilerParams(vmem_limit_bytes=VMEM_LIMIT),
        name="attention_backward",
    )(lengths, tokens, attn, gains, biases, cosine, sine, *operands)


def feed_forward_both(
    tokens, mixed, attn, gains, biases, cotangent, ffn, fbias, head_t, labels, live, layers,
):
    seqs, length, _ = tokens.shape
    pad = (length + 15) // 16 * 16
    rows = seqs * pad
    steps, chunk = fbias.shape
    if layers:
        devices, owned = ffn.shape[1], ffn.shape[2]
        up_spec, down_spec = (
            pl.BlockSpec((1, devices, ROWS, D), lambda k, j=j: (j, 0, k, 0)) for j in range(2)
        )
        ups = downs = ffn
        grad_specs = [whole((owned, D))] * 2
        grad_shapes = [shaped((owned, D))] * 2
        extra = [pltpu.VMEM((chunk, D), F32)] * 2 + reduce_scratch(4, layers)
    else:
        chunked = (steps, chunk, D)
        ups, downs = ffn[0].reshape(chunked), ffn[1].reshape(chunked)
        up_spec = down_spec = leading(chunked)
        grad_specs = [leading(chunked)] * 2
        grad_shapes = [shaped(chunked)] * 2
        extra = []
    return pl.pallas_call(
        functools.partial(feed_forward, layers),
        grid=(steps,),
        in_specs=[
            whole(tokens.shape), whole(mixed.shape), projections(attn, 3, 1),
            whole(gains.shape), whole(biases.shape), whole(cotangent.shape), up_spec,
            down_spec, leading((steps, 1, chunk)), whole(head_t.shape), whole(labels.shape),
            whole(live.shape),
        ],
        out_specs=[whole(tokens.shape), whole(tokens.shape), whole(mixed.shape)]
        + grad_specs
        + [leading((steps, 1, chunk)), whole((D, D)), whole((8, D))],
        out_shape=[shaped(tokens.shape, BF), shaped(tokens.shape), shaped(mixed.shape, BF)]
        + grad_shapes
        + [shaped((steps, 1, chunk)), shaped((D, D)), shaped((8, D))],
        scratch_shapes=[
            pltpu.VMEM(tokens.shape, F32),
            pltpu.VMEM((rows, D), BF),
            pltpu.VMEM((rows, D), BF),
            pltpu.VMEM((rows, D), F32),
            pltpu.VMEM((rows, D), F32),
            pltpu.VMEM((rows, chunk), BF),
            pltpu.VMEM((rows, chunk), BF),
        ]
        + extra,
        compiler_params=pltpu.CompilerParams(
            vmem_limit_bytes=VMEM_LIMIT, **(dict(collective_id=0, has_side_effects=True) if layers else {})
        ),
        name="feed_forward",
    )(
        tokens, mixed, attn, gains, biases, cotangent, ups, downs,
        fbias.reshape(steps, 1, chunk), head_t, labels, live,
    )


def reduce_tail(grad_qkv, grad_wo, small_one, small_two, units, layers):
    devices = 4 * grad_wo.shape[0]
    owned = grad_wo.shape[1]
    pieces = owned // ROWS
    return pl.pallas_call(
        functools.partial(gradient_tail, layers, pieces),
        in_specs=[pl.BlockSpec(memory_space=pltpu.VMEM)] * 5,
        out_specs=[pl.BlockSpec(memory_space=pltpu.VMEM)] * 2,
        out_shape=[shaped((owned, D)), shaped((24, D))],
        scratch_shapes=[
            pltpu.VMEM((4, 24, D), F32),
            pltpu.VMEM((3 + layers, 24, D), F32),
            pltpu.SemaphoreType.DMA((2 + layers,)),
            pltpu.SemaphoreType.DMA((2 + layers,)),
        ]
        + reduce_scratch(pieces, layers),
        compiler_params=pltpu.CompilerParams(
            vmem_limit_bytes=VMEM_LIMIT, collective_id=1, has_side_effects=True
        ),
        name="gradient_tail",
    )(grad_qkv, grad_wo, small_one, small_two, units)


def per_device(
    tokens, lengths, masked_flags, labels, attn_weights, ffn_weights, ffn_bias, norm_gains,
    biases, head_weight, cotangent,
):
    both = ("wide", "narrow")
    seqs, length, _ = tokens.shape
    wide, narrow = lax.axis_size("wide"), lax.axis_size("narrow")
    devices = wide * narrow
    shard, units = D // wide, ffn_bias.shape[0]
    owned = attn_weights.shape[0]
    layers = 4 if (wide, narrow) == (8, 4) and owned == units and owned % ROWS == 0 else 0
    pack = jnp.concatenate([norm_gains.reshape(-1), biases.reshape(-1), ffn_bias])
    if layers:
        extra = jnp.pad(pack, (0, 8 * D - pack.shape[0])).reshape(8, D)
        attn = lax.all_gather(jnp.concatenate([attn_weights, extra], axis=0), both, axis=0)
        packs = attn[:, owned:].reshape(devices, -1)[:, : pack.shape[0]]
    else:
        attn = lax.all_gather(attn_weights, both, axis=0, tiled=True).reshape(4, D, D)
        packs = lax.all_gather(pack[None], both, axis=0, tiled=True)
    ffn = lax.all_gather(ffn_weights, both, axis=1, tiled=True)
    rows = packs.reshape(wide, narrow, -1)[:, 0, : 9 * shard].reshape(wide, 9, shard)
    rows = rows.transpose(1, 0, 2).reshape(9, D).astype(F32)
    gain_rows = rows[:2]
    bias_rows = jnp.concatenate([rows[2:], jnp.zeros((1, D), F32)], axis=0)
    unit_bias = packs[:, 9 * shard :].astype(F32)
    if layers:
        ffn = ffn.reshape(2, devices, units, D)
        unit_bias = unit_bias.reshape(devices, units // ROWS, ROWS).transpose(1, 0, 2)
        unit_bias = unit_bias.reshape(units // ROWS, devices * ROWS)
    else:
        unit_bias = unit_bias.reshape(-1, 512)

    cosine, sine = rotary_tables(length)
    query, key, value, mixed, raw, lse = attention_forward(
        lengths, tokens, attn, gain_rows, bias_rows, bias_rows.T, cosine, sine
    )
    live = (masked_flags == 1) & (jnp.arange(length)[None, :] < lengths[:, None])
    head_t = jnp.pad(head_weight.T, ((0, 7), (0, 0)))
    (
        output, grad_middle, grad_mixed, grad_up_w, grad_down_w, grad_fbias, grad_wo, small_two,
    ) = feed_forward_both(
        tokens, mixed, attn, gain_rows, bias_rows, cotangent, ffn, unit_bias, head_t, labels,
        live.astype(jnp.int32), layers,
    )
    if not layers:
        grad_ffn = lax.psum_scatter(
            jnp.stack([grad_up_w.reshape(-1, D), grad_down_w.reshape(-1, D)]), both,
            scatter_dimension=1, tiled=True,
        )
    grad_tokens, grad_qkv, small_one = attention_backward(
        lengths, tokens, attn, gain_rows, bias_rows, cosine, sine, query, key, value,
        grad_mixed, raw, lse, grad_middle,
    )
    steps, chunk = unit_bias.shape
    at = lax.axis_index("wide")
    owner = at * narrow + lax.axis_index("narrow")
    if layers:
        grad_ffn = jnp.stack([grad_up_w, grad_down_w])
        blocks = (-1, owned, D)
        unit_sums = jnp.pad(grad_fbias, ((0, 8 - steps), (0, 0), (0, D - chunk)))
        grad_attn, sums = reduce_tail(
            grad_qkv.reshape(blocks), grad_wo.reshape(blocks), small_one, small_two, unit_sums,
            layers,
        )
        grad_ffn_bias = lax.dynamic_slice(
            sums, (16, owner * ROWS), (steps, ROWS)
        ).reshape(units)
    else:
        grad_attn = lax.psum_scatter(
            jnp.concatenate([grad_qkv, grad_wo], axis=0), both, scatter_dimension=0, tiled=True
        )
        unit_sums = jnp.pad(grad_fbias.reshape(-1), (0, 8 * D - steps * chunk))
        sums = lax.psum(
            jnp.concatenate([small_one, small_two, unit_sums.reshape(8, D)], axis=0), both
        )
        grad_ffn_bias = lax.dynamic_slice_in_dim(sums[16:].reshape(-1), owner * units, units, 0)
    local = lax.dynamic_slice_in_dim(sums[:12], at * shard, shard, 1)
    grad_gains = jnp.stack([local[0], local[8]])
    grad_biases = jnp.stack([local[r] for r in (1, 9, 2, 3, 4, 10, 11)])
    head_stats = (
        sums[12, 0:256:128] * jnp.array([1.0, VOCAB], F32) / (seqs * length * devices)
    )
    return (
        output, grad_tokens, grad_attn, grad_ffn, grad_ffn_bias, grad_gains, grad_biases,
        head_stats,
    )


def solution(mesh):
    both = ("wide", "narrow")
    return jax.shard_map(
        per_device,
        mesh=mesh,
        in_specs=(
            P(both, None, None),
            P(both),
            P(both, None),
            P(both, None),
            P(both, None),
            P(None, both, None),
            P(both),
            P(None, "wide"),
            P(None, "wide"),
            P(),
            P(both, None, None),
        ),
        out_specs=(
            P(both, None, None),
            P(both, None, None),
            P(both, None),
            P(None, both, None),
            P(both),
            P(None, "wide"),
            P(None, "wide"),
            P(),
        ),
        check_vma=False,
    )
```

```python
import functools
import math

import jax
import jax.numpy as jnp
import numpy as np
from jax import lax
from jax.experimental import pallas as pl
from jax.experimental.pallas import tpu as pltpu
from jax.sharding import PartitionSpec as P

D = 640
HEADS = 20
HEAD = 32
HALF = HEAD // 2
VOCAB = 33
EPS = 1e-05
ROOT_HALF = 0.7071067811865476
INV_ROOT_TWO_PI = 0.3989422804014327
BF = jnp.bfloat16
F32 = jnp.float32
VMEM_LIMIT = 60 << 20

MESH = pl.DeviceIdType.MESH
ROWS = 16


def position():
    wide, narrow = lax.axis_index("wide"), lax.axis_index("narrow")
    return {
        "z": lax.div(wide, 2), "x": lax.rem(wide, 2),
        "y": lax.div(narrow, 2), "c": lax.rem(narrow, 2),
    }


def partner(me, axis, offset, size):
    there = dict(me)
    there[axis] = lax.rem(me[axis] + offset, size)
    return (there["z"] * 2 + there["x"], there["y"] * 2 + there["c"])


def meet(me, layers):
    barrier = pltpu.get_barrier_semaphore()
    peers = [partner(me, axis, 1, 2) for axis in "cyx"]
    peers += [partner(me, "z", offset, layers) for offset in range(1, layers)]
    for peer in peers:
        pl.semaphore_signal(barrier, inc=1, device_id=peer, device_id_type=MESH)
    pl.semaphore_wait(barrier, len(peers))


def reduce_scratch(slots, layers):
    def blocks(count, dtype):
        return pltpu.VMEM((slots, count, ROWS, D), dtype)

    return [
        blocks(4 * layers, BF), blocks(4 * layers, BF),
        blocks(2 * layers, BF), blocks(2 * layers, BF), blocks(2 * layers, F32),
        blocks(layers, BF), blocks(layers, BF), blocks(layers, F32),
        blocks(layers, BF), blocks(layers, BF), blocks(1, F32),
        pltpu.SemaphoreType.DMA((slots, 3 + layers)),
        pltpu.SemaphoreType.DMA((slots, 3 + layers)),
    ]


class PieceReduce:
    def __init__(self, me, layers, refs, slot, first):
        (
            self.s0, self.r0, self.s1, self.r1, self.k1, self.s2, self.r2, self.k2,
            self.s3, self.r3, self.k3,
        ) = (ref.at[slot] for ref in refs[:11])
        self.send, self.recv = (ref.at[slot] for ref in refs[11:])
        self.me, self.layers = me, layers
        self.first, self.second = ("y", "x") if first == "y" else ("x", "y")

    def exchange(self, stage, source, target, axis):
        return pltpu.make_async_remote_copy(
            src_ref=source, dst_ref=target, send_sem=self.send.at[stage],
            recv_sem=self.recv.at[stage], device_id=partner(self.me, axis, 1, 2),
            device_id_type=MESH,
        )

    def layer_copies(self):
        me, layers = self.me, self.layers
        return [
            pltpu.make_async_remote_copy(
                src_ref=self.s3.at[lax.rem(me["z"] + offset, layers)],
                dst_ref=self.r3.at[offset], send_sem=self.send.at[2 + offset],
                recv_sem=self.recv.at[2 + offset],
                device_id=partner(me, "z", offset, layers), device_id_type=MESH,
            )
            for offset in range(1, layers)
        ]

    def rest(self, along, other):
        return other * 2 + along if self.first == "y" else along * 2 + other

    def over_cores(self, get):
        core = self.me["c"]
        for layer in range(self.layers):
            for rest in range(4):
                self.s0[layer * 4 + rest] = get(layer, rest, 1 - core).astype(BF)
        self.exchange(0, self.s0, self.r0, "c").start()

    def over_first(self, get):
        self.exchange(0, self.s0, self.r0, "c").wait()
        core, along = self.me["c"], self.me[self.first]
        for layer in range(self.layers):
            for other in range(2):
                away, near = self.rest(1 - along, other), self.rest(along, other)
                at = layer * 2 + other
                self.s1[at] = (
                    get(layer, away, core) + self.r0[layer * 4 + away].astype(F32)
                ).astype(BF)
                self.k1[at] = get(layer, near, core) + self.r0[layer * 4 + near].astype(F32)
        self.exchange(1, self.s1, self.r1, self.first).start()

    def over_second(self):
        self.exchange(1, self.s1, self.r1, self.first).wait()
        along = self.me[self.second]
        for layer in range(self.layers):
            away, near = layer * 2 + (1 - along), layer * 2 + along
            self.s2[layer] = (self.k1[away] + self.r1[away].astype(F32)).astype(BF)
            self.k2[layer] = self.k1[near] + self.r1[near].astype(F32)
        self.exchange(2, self.s2, self.r2, self.second).start()

    def over_layers(self):
        self.exchange(2, self.s2, self.r2, self.second).wait()
        own = self.me["z"]
        for layer in range(self.layers):
            self.s3[layer] = (self.k2[layer] + self.r2[layer].astype(F32)).astype(BF)
        self.k3[0] = self.k2[own] + self.r2[own].astype(F32)
        for copy in self.layer_copies():
            copy.start()

    def finish(self):
        for copy in self.layer_copies():
            copy.wait()
        total = self.k3[0]
        for offset in range(1, self.layers):
            total = total + self.r3[offset].astype(F32)
        return total


class PieceGather:
    def __init__(self, me, layers, buf, tail, send, recv, first):
        self.me, self.layers, self.buf, self.tail = me, layers, buf, tail
        self.send, self.recv, self.first = send, recv, first

    def view(self, *lead):
        return self.buf.at[lead + self.tail]

    def copy(self, lead, peer, at):
        return pltpu.make_async_remote_copy(
            src_ref=self.view(*lead), dst_ref=self.view(*lead), send_sem=self.send.at[at],
            recv_sem=self.recv.at[at], device_id=peer, device_id_type=MESH,
        )

    def copies(self, stage):
        me, every = self.me, slice(None)
        z, x, y, core = me["z"], me["x"], me["y"], me["c"]
        if stage == 0:
            return [
                self.copy((z, x, y, core), partner(me, "z", offset, self.layers), 2 + offset)
                for offset in range(1, self.layers)
            ]
        if stage == 1:
            lead, axis = (every, x, y, core), self.first
        elif stage == 2:
            lead = (every, every, y, core) if self.first == "x" else (every, x, every, core)
            axis = "y" if self.first == "x" else "x"
        else:
            lead, axis = (every, every, every, core), "c"
        return [self.copy(lead, partner(me, axis, 1, 2), stage - 1)]

    def start(self, stage):
        for copy in self.copies(stage):
            copy.start()

    def wait(self, stage):
        for copy in self.copies(stage):
            copy.wait()

    def advance(self, stage):
        self.wait(stage - 1)
        self.start(stage)


class SmallReduce:
    def __init__(self, me, layers, sent, got, send, recv):
        self.me, self.layers = me, layers
        self.sent, self.got, self.send, self.recv = sent, got, send, recv

    def exchange(self, stage):
        return pltpu.make_async_remote_copy(
            src_ref=self.sent.at[stage], dst_ref=self.got.at[stage],
            send_sem=self.send.at[stage], recv_sem=self.recv.at[stage],
            device_id=partner(self.me, "cyx"[stage], 1, 2), device_id_type=MESH,
        )

    def layer_copies(self):
        own = self.me["z"]
        return [
            pltpu.make_async_remote_copy(
                src_ref=self.sent.at[3], dst_ref=self.got.at[3 + own],
                send_sem=self.send.at[2 + offset], recv_sem=self.recv.at[2 + offset],
                device_id=partner(self.me, "z", offset, self.layers), device_id_type=MESH,
            )
            for offset in range(1, self.layers)
        ]

    def start(self, stage):
        if stage:
            self.exchange(stage - 1).wait()
            self.sent[stage] = self.sent[stage - 1] + self.got[stage - 1]
        if stage < 3:
            self.exchange(stage).start()
        else:
            for copy in self.layer_copies():
                copy.start()
            self.got[3 + self.me["z"]] = self.sent[3]

    def finish(self):
        for copy in self.layer_copies():
            copy.wait()
        total = self.got[3]
        for layer in range(1, self.layers):
            total = total + self.got[3 + layer]
        return total


def gradient_tail(layers, pieces, qkv_ref, wo_ref, one_ref, two_ref, units_ref,
                  grad_ref, sums_ref, sent, got, small_send, small_recv, *refs):
    me = position()
    meet(me, layers)
    sent[0, 0:8] = one_ref[...]
    sent[0, 8:16] = two_ref[...]
    for k in range(8):
        sent[0, 16 + k : 17 + k] = units_ref[k]
    small = SmallReduce(me, layers, sent, got, small_send, small_recv)
    small.start(0)

    def getter(piece):
        rows = slice(piece * ROWS, (piece + 1) * ROWS)

        def get(layer, rest, core):
            at = rest * 2 + core
            return wo_ref[at, rows] if layer == 3 else qkv_ref[layer * 8 + at, rows]

        return get

    ops = [PieceReduce(me, layers, refs, p, "yx"[p % 2]) for p in range(pieces)]
    for p, op in enumerate(ops):
        op.over_cores(getter(p))
    small.start(1)
    for p, op in enumerate(ops):
        op.over_first(getter(p))
    small.start(2)
    for op in ops:
        op.over_second()
    small.start(3)
    for op in ops:
        op.over_layers()
    for p, op in enumerate(ops):
        grad_ref[p * ROWS : (p + 1) * ROWS] = op.finish()
    sums_ref[...] = small.finish()


def dot_nn(a, b):
    return lax.dot_general(a, b, (((1,), (0,)), ((), ())), preferred_element_type=F32)


def dot_nt(a, b):
    return lax.dot_general(a, b, (((1,), (1,)), ((), ())), preferred_element_type=F32)


def dot_tn(a, b):
    return lax.dot_general(a, b, (((0,), (0,)), ((), ())), preferred_element_type=F32)


def matrix(ref, j):
    rows = ref.shape[1]
    blocks = D // rows
    return ref[j * blocks : (j + 1) * blocks].reshape(D, D)


def whiten(values):
    center = jnp.mean(values, axis=-1, keepdims=True)
    offset = values - center
    spread = jnp.mean(offset * offset, axis=-1, keepdims=True)
    inverse = lax.rsqrt(spread + EPS)
    return offset * inverse, inverse


def whiten_back(gradient, whitened, inverse, gain):
    scaled = gradient * gain
    mean_grad = jnp.mean(scaled, axis=-1, keepdims=True)
    mean_cross = jnp.mean(scaled * whitened, axis=-1, keepdims=True)
    return inverse * (scaled - mean_grad - whitened * mean_cross)


def rotary_tables(length):
    frequency = (
        np.float32(1.0)
        / np.float32(10000.0) ** (np.arange(HALF, dtype=np.float32) * np.float32(2.0 / HEAD))
    ).astype(np.float32)
    angles = frequency[:, None] * np.arange(length, dtype=np.float32)[None, :]
    return np.cos(angles).astype(np.float32), np.sin(angles).astype(np.float32)


def key_extents(length):
    extents = list(range(256, length, 128))
    return extents + [length]


def halves(values):
    length = values.shape[-1]
    split = values.reshape(values.shape[0] // HEAD, 2, HALF, length)
    return split[:, 0], split[:, 1]


def joined(first, second):
    length = first.shape[-1]
    both = jnp.concatenate([first[:, None], second[:, None]], axis=1)
    return both.reshape(first.shape[0] * HEAD, length)


GATHER_AHEAD = (
    (0, 1), (1, 1), (2, 1), (0, 2), (3, 1), (1, 2), (4, 1), (2, 2), (5, 1), (3, 2), (0, 3),
    (4, 2), (1, 3), (0, 4), (5, 2), (6, 1), (2, 3), (1, 4),
)
GATHER_AFTER = {
    0: ((3, 3), (4, 3), (7, 1), (5, 3)), 1: ((6, 2),), 2: ((8, 1), (2, 4)),
    3: ((7, 2), (9, 1)), 4: ((8, 2),), 5: ((9, 2), (3, 4)), 6: ((6, 3),), 7: ((7, 3),),
    8: ((8, 3), (4, 4)), 10: ((9, 3),), 11: ((5, 4),), 12: ((6, 4), (7, 4)),
    13: ((8, 4), (9, 4)),
}


def forward_attention(
    layers,
    lens, x_ref, rows_ref, w_ref, ffn_ref, cos_ref, sin_ref,
    q_ref, k_ref, v_ref, mix_ref, raw_ref, inv_ref, exp_ref, *rest,
):
    seqs, length = x_ref.shape[0], x_ref.shape[1]
    group, seq = pl.program_id(0), pl.program_id(1)
    step = group * seqs + seq
    if layers:
        all_rows_ref, attn_ref, ffn_all_ref, hidden, w_t, bias_t = rest[:6]
        w_all, ffn_all, send, recv, local = rest[6:]
        me = position()
        spot = (me["z"], me["x"], me["y"], me["c"])
        owned, units = w_all.shape[4] - 16, ffn_all.shape[5]
        every = slice(None)
        tails = [(slice(owned, owned + 16), every)]
        tails += [(slice(0, owned), slice(i * 128, i * 128 + 128)) for i in range(D // 128)]
        cut = (units // ROWS + 1) // 2 * ROWS
        parts = (slice(0, cut), slice(cut, units))
        pieces = [
            PieceGather(me, layers, w_all, tail, send.at[i], recv.at[i], "xy"[i % 2])
            for i, tail in enumerate(tails)
        ]
        for part in parts:
            for j in range(2):
                i = len(pieces)
                pieces.append(
                    PieceGather(
                        me, layers, ffn_all.at[j], (part, every), send.at[i], recv.at[i],
                        "xy"[i % 2],
                    )
                )

        def act(actions):
            for piece, stage in actions:
                if stage < 4:
                    pieces[piece].advance(stage)
                else:
                    pieces[piece].wait(3)

        results = [
            pltpu.make_async_copy(w_all.at[:, :, :, :, 0:owned], attn_ref, local.at[0]),
            pltpu.make_async_copy(ffn_all, ffn_all_ref, local.at[1]),
        ]
    else:
        hidden, w_t, bias_t = rest

    @pl.when(step == 0)
    def _():
        if layers:
            own = [
                pltpu.make_async_copy(source, w_all.at[spot + (pl.ds(*at),)], local.at[i])
                for i, source, at in ((0, w_ref, (0, owned)), (2, rows_ref, (owned, 16)))
            ]
            own += [
                pltpu.make_async_copy(ffn_ref.at[j], ffn_all.at[(j,) + spot], local.at[3 + j])
                for j in range(2)
            ]
            for copy in own:
                copy.start()
            for copy in own:
                copy.wait()
            meet(me, layers)
            for piece in pieces:
                piece.start(0)
            act(GATHER_AHEAD)
            rows = jnp.zeros((16, D), F32)
            for z in range(layers):
                for i in range(8):
                    rows += w_all[z, i // 4, i // 2 % 2, i % 2, owned : owned + 16].astype(F32)
            all_rows_ref[...] = rows
        else:
            rows = rows_ref[...]
        bias_t[...] = rows.T
        for s in range(seqs):
            whitened, _ = whiten(x_ref[s].astype(F32))
            hidden[s] = (whitened * rows[0:1] + rows[2:3]).astype(BF)

    columns = pl.ds(pl.multiple_of(group * 128, 128), 128)

    @pl.when(seq == 0)
    def _():
        for j in range(3):
            if layers:
                block = w_all[j, :, :, :, 0:owned, columns].reshape(D, 128)
            else:
                block = w_ref[j, :, columns]
            w_t[j * 128 : (j + 1) * 128] = block.T

    cosine, sine = cos_ref[...], sin_ref[...]
    scale = 1.0 / math.sqrt(HEAD)
    lin = dot_nt(w_t[...], hidden[seq])
    for j, out_ref in enumerate((q_ref, k_ref, v_ref)):
        part = lin[j * 128 : (j + 1) * 128] + bias_t[columns, 4 + j : 5 + j]
        if j < 2:
            first, second = halves(part)
            part = joined(first * cosine - second * sine, second * cosine + first * sine)
            if j == 0:
                part = part * scale
        out_ref[0] = part.astype(BF)

    spots = lax.broadcasted_iota(jnp.int32, (16, length), 1)
    lead = lax.broadcasted_iota(jnp.int32, (16, length), 0) == 0
    mask = jnp.where(lead & (spots >= lens[seq]), -1e9, 0.0).astype(BF)
    ones = jnp.where(lead, 1.0, 0.0).astype(BF)
    for h in range(4):
        at = slice(h * HEAD, (h + 1) * HEAD)
        key = jnp.concatenate([k_ref[0, at], mask], axis=0)
        query = jnp.concatenate([q_ref[0, at], ones], axis=0)
        scores = dot_tn(key, query)
        exponent = jnp.exp(scores - jnp.max(scores, axis=0, keepdims=True))
        inverse = 1.0 / jnp.sum(exponent, axis=0, keepdims=True)
        exponent = exponent.astype(BF)
        exp_ref[0, h] = exponent
        mixed = dot_nn(v_ref[0, at], exponent) * inverse
        raw_ref[0, at] = mixed
        mix_ref[0, at] = mixed.astype(BF)
        inv_ref[0, 0, h : h + 1] = inverse

    if layers:
        for after, actions in GATHER_AFTER.items():
            pl.when(step == after)(functools.partial(act, actions))

        @pl.when(step == 11)
        def _():
            results[0].start()

        @pl.when(step == 13)
        def _():
            results[1].start()

        @pl.when(step == 14)
        def _():
            for copy in results:
                copy.wait()


def backward_attention(
    lens, x_ref, w_ref, rows_ref, cos_ref, sin_ref,
    q_ref, k_ref, v_ref, gmix_ref, raw_ref, inv_ref, exp_ref, gmid_ref,
    gx_ref, gw_ref, small_ref, w_t, g_t,
):
    length = x_ref.shape[1]
    seq, group = pl.program_id(0), pl.program_id(1)

    @pl.when((seq == 0) & (group == 0))
    def _():
        for j in range(3):
            w_t[pl.ds(j * D, D), :] = matrix(w_ref, j).T
        gw_ref[...] = jnp.zeros_like(gw_ref)
        small_ref[...] = jnp.zeros_like(small_ref)

    limit = lens[seq]
    scale = 1.0 / math.sqrt(HEAD)
    low_edge = 0
    for extent in key_extents(length):

        @pl.when((limit > low_edge) & (limit <= extent))
        def _(extent=extent):
            cosine, sine = cos_ref[...], sin_ref[...]
            start = pl.multiple_of(group * 128, 128)
            if extent < length:
                for j in (1, 2):
                    g_t[pl.ds(start + j * D, 128), extent:length] = jnp.zeros(
                        (128, length - extent), BF
                    )

            def back_turn(w, c, s):
                first, second = w[:HALF], w[HALF:]
                return jnp.concatenate(
                    [first * c + second * s, second * c - first * s], axis=0
                ).astype(BF)

            for h in range(4):
                at = slice(h * HEAD, (h + 1) * HEAD)
                row = start + h * HEAD
                query, key = q_ref[0, at], k_ref[0, at, 0:extent]
                exponent = exp_ref[0, h, 0:extent]
                inverse = inv_ref[0, 0, h : h + 1]
                grad_mixed = (gmix_ref[0, at].astype(F32) * inverse).astype(BF)
                inner = jnp.sum(
                    raw_ref[0, at] * grad_mixed.astype(F32), axis=0, keepdims=True
                )
                grad_probs = dot_tn(v_ref[0, at, 0:extent], grad_mixed)
                grad_scores = (exponent.astype(F32) * (grad_probs - inner)).astype(BF)
                grad_value = dot_nt(grad_mixed, exponent)
                grad_key = dot_nt(query, grad_scores)
                grad_query = dot_nn(key, grad_scores) * scale
                g_t[pl.ds(row, HEAD), :] = back_turn(grad_query, cosine, sine)
                g_t[pl.ds(row + D, HEAD), 0:extent] = back_turn(
                    grad_key, cosine[:, 0:extent], sine[:, 0:extent]
                )
                g_t[pl.ds(row + 2 * D, HEAD), 0:extent] = grad_value.astype(BF)

        low_edge = extent

    @pl.when(group == pl.num_programs(1) - 1)
    def _():
        whitened, inverse = whiten(x_ref[0].astype(F32))
        gain = rows_ref[0:1, :]
        hidden = (whitened * gain + rows_ref[2:3, :]).astype(BF)
        hidden_t = hidden.T
        grads = g_t[...]
        ones = jnp.ones((8, length), BF)
        grad_hidden = dot_tn(grads, w_t[...])
        for j in range(3):
            part = grads[j * D : (j + 1) * D]
            small_ref[2 + j : 3 + j, :] += dot_nt(ones, part)[0:1]
            gw_ref[pl.ds(j * D, D), :] += dot_nt(hidden_t, part)
        small_ref[0:1, :] += jnp.sum(grad_hidden * whitened, axis=0, keepdims=True)
        small_ref[1:2, :] += jnp.sum(grad_hidden, axis=0, keepdims=True)
        gx_ref[0] = gmid_ref[0] + whiten_back(grad_hidden, whitened, inverse, gain)


def feed_forward(
    layers,
    x_ref, mix_ref, wo_ref, rows_ref, cot_ref, u_ref, v_ref, fbias_ref,
    head_ref, label_ref, live_ref,
    out_ref, gmid_ref, gmix_ref, gu_ref, gv_ref, gfb_ref, gwo_ref, small_ref,
    middle, hidden, cot, down, grad_hidden, act_low, grad_low, *comm,
):
    seqs, length = x_ref.shape[0], x_ref.shape[1]
    pad = hidden.shape[0] // seqs
    step = pl.program_id(0)
    last = pl.num_programs(0) - 1
    chunk = act_low.shape[1]
    if layers:
        me = position()
        terms, comm = comm[:2], comm[2:]

        def pieces(k):
            slot = lax.rem(k, 2) * 2
            return [PieceReduce(me, layers, comm, slot + j, "yx"[j]) for j in range(2)]

        def getter(j):
            def get(layer, rest, core):
                at = ((layer * 4 + rest) * 2 + core) * ROWS
                return terms[j][pl.ds(pl.multiple_of(at, ROWS), ROWS), :]

            return get

        def over_first(k):
            for j, op in enumerate(pieces(k)):
                op.over_first(getter(j))

        def over_second(k):
            for op in pieces(k):
                op.over_second()

        def over_layers(k):
            for op in pieces(k):
                op.over_layers()

        def finish(k):
            rows = pl.ds(pl.multiple_of(k * ROWS, ROWS), ROWS)
            for op, ref in zip(pieces(k), (gu_ref, gv_ref)):
                ref[rows, :] = op.finish()

    def later(stage, delay):
        if layers:
            pl.when(step >= delay)(lambda: stage(step - delay))

    @pl.when(step == 0)
    def _():
        if layers:
            meet(me, layers)
        for s in range(seqs):
            branch = dot_tn(mix_ref[s], matrix(wo_ref, 0)) + rows_ref[7:8, :]
            mid = x_ref[s].astype(F32) + branch
            middle[s] = mid
            whitened, _ = whiten(mid)
            low = (whitened * rows_ref[1:2, :] + rows_ref[3:4, :]).astype(BF)
            blank = jnp.zeros((pad - length, D), BF)
            hidden[pl.ds(s * pad, pad), :] = jnp.concatenate([low, blank], axis=0)
            cot[pl.ds(s * pad, pad), :] = jnp.concatenate([cot_ref[s], blank], axis=0)
        down[...] = jnp.zeros_like(down)
        grad_hidden[...] = jnp.zeros_like(grad_hidden)

    up_w = u_ref[0].reshape(chunk, D)
    down_w = v_ref[0].reshape(chunk, D)
    fbias = fbias_ref[0]
    total = jnp.zeros_like(fbias)
    for s in range(seqs):
        rows = pl.ds(s * pad, pad)
        upward = dot_nt(hidden[rows, :], up_w) + fbias
        grad_act = dot_nt(cot[rows, :], down_w)
        phi = 0.5 * (1.0 + lax.erf(upward * ROOT_HALF))
        act = (upward * phi).astype(BF)
        slope = phi + upward * jnp.exp(-0.5 * upward * upward) * INV_ROOT_TWO_PI
        grad_up = (grad_act * slope).astype(BF)
        act_low[rows, :] = act
        grad_low[rows, :] = grad_up
        total += jnp.sum(grad_up.astype(F32), axis=0, keepdims=True)
        down[rows, :] += dot_nn(act, down_w)
        grad_hidden[rows, :] += dot_nn(grad_up, up_w)
        if layers:
            if s == 0:
                later(over_first, 1)
            if s == 1:
                later(finish, 2)
            if s == seqs - 1:
                later(over_second, 1)
    gfb_ref[0] = total
    grad_u = dot_tn(grad_low[...], hidden[...])
    if layers:
        terms[0][...] = grad_u
        later(over_layers, 1)
        terms[1][...] = dot_tn(act_low[...], cot[...])
        for j, op in enumerate(pieces(step)):
            op.over_cores(getter(j))
    else:
        gu_ref[0] = grad_u
        gv_ref[0] = dot_tn(act_low[...], cot[...])

    @pl.when(step == last)
    def _():
        gain = rows_ref[1:2, :]
        gain_sum = jnp.zeros((1, D), F32)
        shift_sum = jnp.zeros((1, D), F32)
        branch_sum = jnp.zeros((1, D), F32)
        cot_sum = jnp.zeros((1, D), F32)
        loglik = jnp.zeros((1, length), F32)
        hits = jnp.zeros((1, length), F32)
        gwo_ref[...] = jnp.zeros_like(gwo_ref)
        for s in range(seqs):
            rows = pl.ds(s * pad, length)
            mid = middle[s]
            final = mid + (down[rows, :] + rows_ref[8:9, :])
            out_ref[s] = final.astype(BF)
            unit, _ = whiten(final)
            logits = dot_nt(head_ref[...], unit.astype(BF))
            slot = lax.broadcasted_iota(jnp.int32, logits.shape, 0)
            logits = jnp.where(slot < VOCAB, logits, -1e30)
            shifted = logits - jnp.max(logits, axis=0, keepdims=True)
            logprob = shifted - jnp.log(jnp.sum(jnp.exp(shifted), axis=0, keepdims=True))
            picked = jnp.sum(
                jnp.where(slot == label_ref[s : s + 1, :], logprob, 0.0), axis=0, keepdims=True
            )
            live = live_ref[s : s + 1, :] != 0
            loglik += jnp.where(live, picked, 0.0)
            hits += jnp.where(live, jnp.exp(picked), 0.0)

            gradient = grad_hidden[rows, :]
            whitened, inverse = whiten(mid)
            gain_sum += jnp.sum(gradient * whitened, axis=0, keepdims=True)
            shift_sum += jnp.sum(gradient, axis=0, keepdims=True)
            own = cot_ref[s].astype(F32)
            cot_sum += jnp.sum(own, axis=0, keepdims=True)
            grad_mid = own + whiten_back(gradient, whitened, inverse, gain)
            gmid_ref[s] = grad_mid
            low = grad_mid.astype(BF)
            branch_sum += jnp.sum(low.astype(F32), axis=0, keepdims=True)
            gmix_ref[s] = dot_nt(matrix(wo_ref, 0), low).astype(BF)
            gwo_ref[...] += dot_nn(mix_ref[s], low)
            if layers:
                if s == 0:
                    over_first(last)
                    finish(last - 1)
                if s == seqs - 2:
                    over_second(last)
                if s == seqs - 1:
                    over_layers(last)
        small_ref[0:1, :] = gain_sum
        small_ref[1:2, :] = shift_sum
        small_ref[2:3, :] = branch_sum
        small_ref[3:4, :] = cot_sum
        small_ref[4:8, :] = jnp.zeros((4, D), F32)
        small_ref[4:5, 0:128] = jnp.broadcast_to(
            jnp.sum(loglik, axis=1, keepdims=True), (1, 128)
        )
        small_ref[4:5, 128:256] = jnp.broadcast_to(
            jnp.sum(hits, axis=1, keepdims=True), (1, 128)
        )
        if layers:
            finish(last)


def whole(shape):
    return pl.BlockSpec(shape, lambda *_: (0,) * len(shape), pipeline_mode=pl.Buffered(1))


def block_of(shape, *index):
    return pl.BlockSpec(shape, lambda *_: index, pipeline_mode=pl.Buffered(1))


def leading(shape):
    return pl.BlockSpec((1,) + tuple(shape[1:]), lambda i, *_: (i,) + (0,) * (len(shape) - 1))


def shaped(shape, dtype=F32):
    return jax.ShapeDtypeStruct(shape, dtype)


def projections(attn, first, count):
    blocks = attn.shape[0] // 4
    rows = D // blocks
    return block_of((blocks * count, rows, D), first // count, 0, 0)


def attention_forward(lengths, tokens, rows_all, attn, ffn, cosine, sine, layers):
    seqs, length, _ = tokens.shape
    heads = HEADS // 4
    flat = (seqs, D, length)
    inverse = (seqs, heads, 4, length)
    exponent = (seqs, HEADS, length, length)

    def part(block):
        return pl.BlockSpec(block, lambda g, s, *_: (s, g, 0, 0)[: len(block)])

    out_specs = [part((1, 128, length))] * 5
    out_specs += [part((1, 1, 4, length)), part((1, 4, length, length))]
    out_shape = [shaped(flat, BF)] * 4 + [shaped(flat), shaped(inverse), shaped(exponent, BF)]
    scratch = [
        pltpu.VMEM((seqs, length, D), BF), pltpu.VMEM((384, D), BF), pltpu.VMEM((D, 16), F32),
    ]
    hbm = pl.BlockSpec(memory_space=pl.ANY)
    params = dict(vmem_limit_bytes=VMEM_LIMIT)
    if layers:
        chips = (layers, 2, 2, 2)
        owned, units = attn.shape[0], ffn.shape[1]
        out_specs += [whole((16, D)), hbm, hbm]
        out_shape += [
            shaped((16, D)), shaped(chips + (owned, D), BF),
            shaped((2,) + chips + (units, D), BF),
        ]
        scratch += [
            pltpu.VMEM(chips + (owned + 16, D), BF), pltpu.VMEM((2,) + chips + (units, D), BF),
            pltpu.SemaphoreType.DMA((10, 2 + layers)), pltpu.SemaphoreType.DMA((10, 2 + layers)),
            pltpu.SemaphoreType.DMA((5,)),
        ]
        params.update(collective_id=2, has_side_effects=True)
        sources = [hbm, hbm, hbm]
    else:
        sources = [whole(rows_all.shape), whole(attn.shape), hbm]
    return pl.pallas_call(
        functools.partial(forward_attention, layers),
        grid_spec=pltpu.PrefetchScalarGridSpec(
            num_scalar_prefetch=1,
            grid=(heads, seqs),
            in_specs=[whole(tokens.shape)] + sources + [whole(cosine.shape), whole(sine.shape)],
            out_specs=out_specs,
            scratch_shapes=scratch,
        ),
        out_shape=out_shape,
        compiler_params=pltpu.CompilerParams(**params),
        name="attention_forward",
    )(lengths, tokens, rows_all, attn, ffn, cosine, sine)


def attention_backward(
    lengths, tokens, attn, rows_all, cosine, sine, query, key, value, grad_mixed, raw,
    inverse, exponent, grad_middle,
):
    seqs, length, _ = tokens.shape

    def part(block):
        return pl.BlockSpec(block, lambda s, g, *_: (s, g, 0, 0)[: len(block)])

    return pl.pallas_call(
        backward_attention,
        grid_spec=pltpu.PrefetchScalarGridSpec(
            num_scalar_prefetch=1,
            grid=(seqs, HEADS // 4),
            in_specs=[
                leading(tokens.shape), projections(attn, 0, 3), whole(rows_all.shape),
                whole(cosine.shape), whole(sine.shape),
            ]
            + [part((1, 128, length))] * 5
            + [part((1, 1, 4, length)), part((1, 4, length, length)), leading(tokens.shape)],
            out_specs=[leading(tokens.shape), whole((3 * D, D)), whole((8, D))],
            scratch_shapes=[pltpu.VMEM((3 * D, D), BF), pltpu.VMEM((3 * D, length), BF)],
        ),
        out_shape=[shaped(tokens.shape), shaped((3 * D, D)), shaped((8, D))],
        compiler_params=pltpu.CompilerParams(vmem_limit_bytes=VMEM_LIMIT),
        name="attention_backward",
    )(
        lengths, tokens, attn, rows_all, cosine, sine, query, key, value, grad_mixed, raw,
        inverse, exponent, grad_middle,
    )


def feed_forward_both(
    tokens, mixed, attn, rows_all, cotangent, ffn, fbias, head_t, labels, live, layers,
):
    seqs, length, _ = tokens.shape
    pad = (length + 15) // 16 * 16
    rows = seqs * pad
    steps, chunk = fbias.shape
    if layers:
        devices, owned = ffn.shape[1], ffn.shape[2]
        up_spec, down_spec = (
            pl.BlockSpec((1, devices, ROWS, D), lambda k, j=j: (j, 0, k, 0)) for j in range(2)
        )
        ups = downs = ffn
        grad_specs = [whole((owned, D))] * 2
        grad_shapes = [shaped((owned, D))] * 2
        extra = [pltpu.VMEM((chunk, D), F32)] * 2 + reduce_scratch(4, layers)
    else:
        chunked = (steps, chunk, D)
        ups, downs = ffn[0].reshape(chunked), ffn[1].reshape(chunked)
        up_spec = down_spec = leading(chunked)
        grad_specs = [leading(chunked)] * 2
        grad_shapes = [shaped(chunked)] * 2
        extra = []
    return pl.pallas_call(
        functools.partial(feed_forward, layers),
        grid=(steps,),
        in_specs=[
            whole(tokens.shape), whole(mixed.shape), projections(attn, 3, 1),
            whole(rows_all.shape), whole(cotangent.shape), up_spec, down_spec,
            leading((steps, 1, chunk)), whole(head_t.shape), whole(labels.shape),
            whole(live.shape),
        ],
        out_specs=[whole(tokens.shape), whole(tokens.shape), whole(mixed.shape)]
        + grad_specs
        + [leading((steps, 1, chunk)), whole((D, D)), whole((8, D))],
        out_shape=[shaped(tokens.shape, BF), shaped(tokens.shape), shaped(mixed.shape, BF)]
        + grad_shapes
        + [shaped((steps, 1, chunk)), shaped((D, D)), shaped((8, D))],
        scratch_shapes=[
            pltpu.VMEM(tokens.shape, F32),
            pltpu.VMEM((rows, D), BF),
            pltpu.VMEM((rows, D), BF),
            pltpu.VMEM((rows, D), F32),
            pltpu.VMEM((rows, D), F32),
            pltpu.VMEM((rows, chunk), BF),
            pltpu.VMEM((rows, chunk), BF),
        ]
        + extra,
        compiler_params=pltpu.CompilerParams(
            vmem_limit_bytes=VMEM_LIMIT, **(dict(collective_id=0, has_side_effects=True) if layers else {})
        ),
        name="feed_forward",
    )(
        tokens, mixed, attn, rows_all, cotangent, ups, downs,
        fbias.reshape(steps, 1, chunk), head_t, labels, live,
    )


def reduce_tail(grad_qkv, grad_wo, small_one, small_two, units, layers):
    devices = 4 * grad_wo.shape[0]
    owned = grad_wo.shape[1]
    pieces = owned // ROWS
    return pl.pallas_call(
        functools.partial(gradient_tail, layers, pieces),
        in_specs=[pl.BlockSpec(memory_space=pltpu.VMEM)] * 5,
        out_specs=[pl.BlockSpec(memory_space=pltpu.VMEM)] * 2,
        out_shape=[shaped((owned, D)), shaped((24, D))],
        scratch_shapes=[
            pltpu.VMEM((4, 24, D), F32),
            pltpu.VMEM((3 + layers, 24, D), F32),
            pltpu.SemaphoreType.DMA((2 + layers,)),
            pltpu.SemaphoreType.DMA((2 + layers,)),
        ]
        + reduce_scratch(pieces, layers),
        compiler_params=pltpu.CompilerParams(
            vmem_limit_bytes=VMEM_LIMIT, collective_id=1, has_side_effects=True
        ),
        name="gradient_tail",
    )(grad_qkv, grad_wo, small_one, small_two, units)


def per_device(
    tokens, lengths, masked_flags, labels, attn_weights, ffn_weights, ffn_bias, norm_gains,
    biases, head_weight, cotangent,
):
    both = ("wide", "narrow")
    seqs, length, _ = tokens.shape
    wide, narrow = lax.axis_size("wide"), lax.axis_size("narrow")
    devices = wide * narrow
    shard, units = D // wide, ffn_bias.shape[0]
    owned = attn_weights.shape[0]
    layers = 4 if (wide, narrow) == (8, 4) and owned == units and owned % ROWS == 0 else 0
    at = lax.axis_index("wide")
    owner = at * narrow + lax.axis_index("narrow")
    first = (lax.axis_index("narrow") == 0).astype(BF)
    own = jnp.concatenate([norm_gains, biases], axis=0) * first
    rows_own = lax.dynamic_update_slice(jnp.zeros((16, D), BF), own, (0, at * shard))
    flat = lax.dynamic_update_slice(jnp.zeros((4 * D,), BF), ffn_bias, (owner * units,))
    rows_own = rows_own + jnp.pad(flat.reshape(4, D), ((9, 3), (0, 0)))
    cosine, sine = rotary_tables(length)
    if layers:
        rows_all, attn, ffn = rows_own, attn_weights, ffn_weights
    else:
        attn = lax.all_gather(attn_weights, both, axis=0, tiled=True).reshape(4, D, D)
        ffn = lax.all_gather(ffn_weights, both, axis=1, tiled=True)
        rows_all = lax.psum(rows_own.astype(F32), both)
    query, key, value, mixed, raw, inverse, exponent, *gathered = attention_forward(
        lengths, tokens, rows_all, attn, ffn, cosine, sine, layers
    )
    if layers:
        rows_all, attn, ffn = gathered
        attn = attn.reshape(devices, owned, D)
        ffn = ffn.reshape(2, devices, units, D)
        unit_bias = rows_all[9:13].reshape(devices, units // ROWS, ROWS).transpose(1, 0, 2)
        unit_bias = unit_bias.reshape(units // ROWS, devices * ROWS)
    else:
        unit_bias = rows_all[9:13].reshape(-1, 512)
    live = (masked_flags == 1) & (jnp.arange(length)[None, :] < lengths[:, None])
    head_t = jnp.pad(head_weight.T, ((0, 7), (0, 0)))
    (
        output, grad_middle, grad_mixed, grad_up_w, grad_down_w, grad_fbias, grad_wo, small_two,
    ) = feed_forward_both(
        tokens, mixed, attn, rows_all, cotangent, ffn, unit_bias, head_t, labels,
        live.astype(jnp.int32), layers,
    )
    if not layers:
        grad_ffn = lax.psum_scatter(
            jnp.stack([grad_up_w.reshape(-1, D), grad_down_w.reshape(-1, D)]), both,
            scatter_dimension=1, tiled=True,
        )
    grad_tokens, grad_qkv, small_one = attention_backward(
        lengths, tokens, attn, rows_all, cosine, sine, query, key, value, grad_mixed, raw,
        inverse, exponent, grad_middle,
    )
    steps, chunk = unit_bias.shape
    if layers:
        grad_ffn = jnp.stack([grad_up_w, grad_down_w])
        blocks = (-1, owned, D)
        unit_sums = jnp.pad(grad_fbias, ((0, 8 - steps), (0, 0), (0, D - chunk)))
        grad_attn, sums = reduce_tail(
            grad_qkv.reshape(blocks), grad_wo.reshape(blocks), small_one, small_two, unit_sums,
            layers,
        )
        grad_ffn_bias = lax.dynamic_slice(
            sums, (16, owner * ROWS), (steps, ROWS)
        ).reshape(units)
    else:
        grad_attn = lax.psum_scatter(
            jnp.concatenate([grad_qkv, grad_wo], axis=0), both, scatter_dimension=0, tiled=True
        )
        unit_sums = jnp.pad(grad_fbias.reshape(-1), (0, 8 * D - steps * chunk))
        sums = lax.psum(
            jnp.concatenate([small_one, small_two, unit_sums.reshape(8, D)], axis=0), both
        )
        grad_ffn_bias = lax.dynamic_slice_in_dim(sums[16:].reshape(-1), owner * units, units, 0)
    local = lax.dynamic_slice_in_dim(sums[:12], at * shard, shard, 1)
    grad_gains = jnp.stack([local[0], local[8]])
    grad_biases = jnp.stack([local[r] for r in (1, 9, 2, 3, 4, 10, 11)])
    head_stats = (
        sums[12, 0:256:128] * jnp.array([1.0, VOCAB], F32) / (seqs * length * devices)
    )
    return (
        output, grad_tokens, grad_attn, grad_ffn, grad_ffn_bias, grad_gains, grad_biases,
        head_stats,
    )


def solution(mesh):
    both = ("wide", "narrow")
    return jax.shard_map(
        per_device,
        mesh=mesh,
        in_specs=(
            P(both, None, None),
            P(both),
            P(both, None),
            P(both, None),
            P(both, None),
            P(None, both, None),
            P(both),
            P(None, "wide"),
            P(None, "wide"),
            P(),
            P(both, None, None),
        ),
        out_specs=(
            P(both, None, None),
            P(both, None, None),
            P(both, None),
            P(None, both, None),
            P(both),
            P(None, "wide"),
            P(None, "wide"),
            P(),
        ),
        check_vma=False,
    )
```

```python
import functools
import math

import jax
import jax.numpy as jnp
import numpy as np
from jax import lax
from jax.experimental import pallas as pl
from jax.experimental.pallas import tpu as pltpu
from jax.sharding import PartitionSpec as P

D = 640
HEADS = 20
HEAD = 32
HALF = HEAD // 2
VOCAB = 33
EPS = 1e-05
ROOT_HALF = 0.7071067811865476
INV_ROOT_TWO_PI = 0.3989422804014327
BF = jnp.bfloat16
F32 = jnp.float32
VMEM_LIMIT = 60 << 20

MESH = pl.DeviceIdType.MESH
ROWS = 16


def position():
    wide, narrow = lax.axis_index("wide"), lax.axis_index("narrow")
    return {
        "z": lax.div(wide, 2), "x": lax.rem(wide, 2),
        "y": lax.div(narrow, 2), "c": lax.rem(narrow, 2),
    }


def partner(me, axis, offset, size):
    there = dict(me)
    there[axis] = lax.rem(me[axis] + offset, size)
    return (there["z"] * 2 + there["x"], there["y"] * 2 + there["c"])


def greet(me, layers):
    barrier = pltpu.get_barrier_semaphore()
    peers = [partner(me, axis, 1, 2) for axis in "cyx"]
    peers += [partner(me, "z", offset, layers) for offset in range(1, layers)]
    for peer in peers:
        pl.semaphore_signal(barrier, inc=1, device_id=peer, device_id_type=MESH)


def meet(layers):
    pl.semaphore_wait(pltpu.get_barrier_semaphore(), 2 + layers)


def reduce_scratch(slots, layers):
    def blocks(count, dtype):
        return pltpu.VMEM((slots, count, ROWS, D), dtype)

    return [
        blocks(4 * layers, BF), blocks(4 * layers, BF),
        blocks(2 * layers, BF), blocks(2 * layers, BF), blocks(2 * layers, F32),
        blocks(layers, BF), blocks(layers, BF), blocks(layers, F32),
        blocks(layers, BF), blocks(layers, BF), blocks(1, F32),
        pltpu.SemaphoreType.DMA((slots, 3 + layers)),
        pltpu.SemaphoreType.DMA((slots, 3 + layers)),
    ]


class PieceReduce:
    def __init__(self, me, layers, refs, slot, first):
        (
            self.s0, self.r0, self.s1, self.r1, self.k1, self.s2, self.r2, self.k2,
            self.s3, self.r3, self.k3,
        ) = (ref.at[slot] for ref in refs[:11])
        self.send, self.recv = (ref.at[slot] for ref in refs[11:])
        self.me, self.layers = me, layers
        self.first, self.second = ("y", "x") if first == "y" else ("x", "y")

    def exchange(self, stage, source, target, axis):
        return pltpu.make_async_remote_copy(
            src_ref=source, dst_ref=target, send_sem=self.send.at[stage],
            recv_sem=self.recv.at[stage], device_id=partner(self.me, axis, 1, 2),
            device_id_type=MESH,
        )

    def layer_copies(self):
        me, layers = self.me, self.layers
        return [
            pltpu.make_async_remote_copy(
                src_ref=self.s3.at[lax.rem(me["z"] + offset, layers)],
                dst_ref=self.r3.at[offset], send_sem=self.send.at[2 + offset],
                recv_sem=self.recv.at[2 + offset],
                device_id=partner(me, "z", offset, layers), device_id_type=MESH,
            )
            for offset in range(1, layers)
        ]

    def rest(self, along, other):
        return other * 2 + along if self.first == "y" else along * 2 + other

    def over_cores(self, get):
        core = self.me["c"]
        for layer in range(self.layers):
            for rest in range(4):
                self.s0[layer * 4 + rest] = get(layer, rest, 1 - core).astype(BF)
        self.exchange(0, self.s0, self.r0, "c").start()

    def over_first(self, get):
        self.exchange(0, self.s0, self.r0, "c").wait()
        core, along = self.me["c"], self.me[self.first]
        for layer in range(self.layers):
            for other in range(2):
                away, near = self.rest(1 - along, other), self.rest(along, other)
                at = layer * 2 + other
                self.s1[at] = (
                    get(layer, away, core) + self.r0[layer * 4 + away].astype(F32)
                ).astype(BF)
                self.k1[at] = get(layer, near, core) + self.r0[layer * 4 + near].astype(F32)
        self.exchange(1, self.s1, self.r1, self.first).start()

    def over_second(self):
        self.exchange(1, self.s1, self.r1, self.first).wait()
        along = self.me[self.second]
        for layer in range(self.layers):
            away, near = layer * 2 + (1 - along), layer * 2 + along
            self.s2[layer] = (self.k1[away] + self.r1[away].astype(F32)).astype(BF)
            self.k2[layer] = self.k1[near] + self.r1[near].astype(F32)
        self.exchange(2, self.s2, self.r2, self.second).start()

    def over_layers(self):
        self.exchange(2, self.s2, self.r2, self.second).wait()
        own = self.me["z"]
        for layer in range(self.layers):
            self.s3[layer] = (self.k2[layer] + self.r2[layer].astype(F32)).astype(BF)
        self.k3[0] = self.k2[own] + self.r2[own].astype(F32)
        for copy in self.layer_copies():
            copy.start()

    def finish(self):
        for copy in self.layer_copies():
            copy.wait()
        total = self.k3[0]
        for offset in range(1, self.layers):
            total = total + self.r3[offset].astype(F32)
        return total


class PieceGather:
    def __init__(self, me, layers, buf, tail, send, recv, first):
        self.me, self.layers, self.buf, self.tail = me, layers, buf, tail
        self.send, self.recv, self.first = send, recv, first

    def view(self, *lead):
        return self.buf.at[lead + self.tail]

    def copy(self, lead, peer, at):
        return pltpu.make_async_remote_copy(
            src_ref=self.view(*lead), dst_ref=self.view(*lead), send_sem=self.send.at[at],
            recv_sem=self.recv.at[at], device_id=peer, device_id_type=MESH,
        )

    def copies(self, stage):
        me, every = self.me, slice(None)
        z, x, y, core = me["z"], me["x"], me["y"], me["c"]
        if stage == 0:
            return [
                self.copy((z, x, y, core), partner(me, "z", offset, self.layers), 2 + offset)
                for offset in range(1, self.layers)
            ]
        if stage == 1:
            lead, axis = (every, x, y, core), self.first
        elif stage == 2:
            lead = (every, every, y, core) if self.first == "x" else (every, x, every, core)
            axis = "y" if self.first == "x" else "x"
        else:
            lead, axis = (every, every, every, core), "c"
        return [self.copy(lead, partner(me, axis, 1, 2), stage - 1)]

    def start(self, stage):
        for copy in self.copies(stage):
            copy.start()

    def wait(self, stage):
        for copy in self.copies(stage):
            copy.wait()

    def advance(self, stage):
        self.wait(stage - 1)
        self.start(stage)


class SmallReduce:
    def __init__(self, me, layers, sent, got, send, recv):
        self.me, self.layers = me, layers
        self.sent, self.got, self.send, self.recv = sent, got, send, recv

    def exchange(self, stage):
        return pltpu.make_async_remote_copy(
            src_ref=self.sent.at[stage], dst_ref=self.got.at[stage],
            send_sem=self.send.at[stage], recv_sem=self.recv.at[stage],
            device_id=partner(self.me, "cyx"[stage], 1, 2), device_id_type=MESH,
        )

    def layer_copies(self):
        own = self.me["z"]
        return [
            pltpu.make_async_remote_copy(
                src_ref=self.sent.at[3], dst_ref=self.got.at[3 + own],
                send_sem=self.send.at[2 + offset], recv_sem=self.recv.at[2 + offset],
                device_id=partner(self.me, "z", offset, self.layers), device_id_type=MESH,
            )
            for offset in range(1, self.layers)
        ]

    def start(self, stage):
        if stage:
            self.exchange(stage - 1).wait()
            self.sent[stage] = self.sent[stage - 1] + self.got[stage - 1]
        if stage < 3:
            self.exchange(stage).start()
        else:
            for copy in self.layer_copies():
                copy.start()
            self.got[3 + self.me["z"]] = self.sent[3]

    def finish(self):
        for copy in self.layer_copies():
            copy.wait()
        total = self.got[3]
        for layer in range(1, self.layers):
            total = total + self.got[3 + layer]
        return total


def gradient_tail(layers, pieces, qkv_ref, wo_ref, one_ref, two_ref, units_ref,
                  grad_ref, sums_ref, sent, got, small_send, small_recv, *refs):
    me = position()
    greet(me, layers)
    meet(layers)
    order = [(one_ref, 0), (two_ref, 0), (one_ref, 1), (two_ref, 1)]
    order += [(one_ref, 2), (one_ref, 3), (one_ref, 4), (two_ref, 2), (two_ref, 3), (two_ref, 4)]
    sent[0, 8:16] = jnp.zeros((8, D), F32)
    for row, (ref, at) in enumerate(order):
        sent[0, row : row + 1] = ref[at : at + 1]
    for k in range(8):
        sent[0, 16 + k : 17 + k] = units_ref[k]
    small = SmallReduce(me, layers, sent, got, small_send, small_recv)
    small.start(0)

    def getter(piece):
        rows = slice(piece * ROWS, (piece + 1) * ROWS)

        def get(layer, rest, core):
            at = rest * 2 + core
            return wo_ref[at, rows] if layer == 3 else qkv_ref[layer * 8 + at, rows]

        return get

    ops = [PieceReduce(me, layers, refs, p, "yx"[p % 2]) for p in range(pieces)]
    for p, op in enumerate(ops):
        op.over_cores(getter(p))
    small.start(1)
    for p, op in enumerate(ops):
        op.over_first(getter(p))
    small.start(2)
    for op in ops:
        op.over_second()
    small.start(3)
    for op in ops:
        op.over_layers()
    for p, op in enumerate(ops):
        grad_ref[p * ROWS : (p + 1) * ROWS] = op.finish()
    sums_ref[...] = small.finish()


def dot_nn(a, b):
    return lax.dot_general(a, b, (((1,), (0,)), ((), ())), preferred_element_type=F32)


def dot_nt(a, b):
    return lax.dot_general(a, b, (((1,), (1,)), ((), ())), preferred_element_type=F32)


def dot_tn(a, b):
    return lax.dot_general(a, b, (((0,), (0,)), ((), ())), preferred_element_type=F32)


def matrix(ref, j):
    rows = ref.shape[1]
    blocks = D // rows
    return ref[j * blocks : (j + 1) * blocks].reshape(D, D)


def whiten(values):
    center = jnp.mean(values, axis=-1, keepdims=True)
    offset = values - center
    spread = jnp.mean(offset * offset, axis=-1, keepdims=True)
    inverse = lax.rsqrt(spread + EPS)
    return offset * inverse, inverse


def whiten_back(gradient, whitened, inverse, gain):
    scaled = gradient * gain
    mean_grad = jnp.mean(scaled, axis=-1, keepdims=True)
    mean_cross = jnp.mean(scaled * whitened, axis=-1, keepdims=True)
    return inverse * (scaled - mean_grad - whitened * mean_cross)


def rotary_tables(length):
    frequency = (
        np.float32(1.0)
        / np.float32(10000.0) ** (np.arange(HALF, dtype=np.float32) * np.float32(2.0 / HEAD))
    ).astype(np.float32)
    angles = frequency[:, None] * np.arange(length, dtype=np.float32)[None, :]
    return np.cos(angles).astype(np.float32), np.sin(angles).astype(np.float32)


def key_extents(length):
    extents = list(range(256, length, 128))
    return extents + [length]


def halves(values):
    length = values.shape[-1]
    split = values.reshape(values.shape[0] // HEAD, 2, HALF, length)
    return split[:, 0], split[:, 1]


def joined(first, second):
    length = first.shape[-1]
    both = jnp.concatenate([first[:, None], second[:, None]], axis=1)
    return both.reshape(first.shape[0] * HEAD, length)


GATHER_AHEAD = (
    (0, 1), (1, 1), (2, 1), (0, 2), (3, 1), (1, 2), (4, 1), (2, 2), (5, 1), (3, 2), (0, 3),
    (4, 2), (1, 3), (0, 4), (5, 2), (6, 1), (2, 3), (1, 4),
)
GATHER_AFTER = {
    0: ((3, 3), (4, 3), (7, 1), (5, 3)), 1: ((6, 2),), 2: ((8, 1), (2, 4)),
    3: ((7, 2), (9, 1)), 4: ((8, 2),), 5: ((9, 2), (3, 4)), 6: ((6, 3),), 7: ((7, 3),),
    8: ((8, 3), (4, 4)), 10: ((9, 3),), 11: ((5, 4),), 12: ((6, 4), (7, 4)),
    13: ((8, 4), (9, 4)),
}


def forward_attention(
    layers,
    lens, x_ref, rows_ref, w_ref, ffn_ref, cos_ref, sin_ref,
    q_ref, k_ref, v_ref, mix_ref, raw_ref, inv_ref, exp_ref, *rest,
):
    seqs, length = x_ref.shape[0], x_ref.shape[1]
    group, seq = pl.program_id(0), pl.program_id(1)
    step = group * seqs + seq
    if layers:
        all_rows_ref, attn_ref, ffn_all_ref, hidden, w_t, bias_t = rest[:6]
        w_all, ffn_all, send, recv, local = rest[6:]
        me = position()
        spot = (me["z"], me["x"], me["y"], me["c"])
        owned, units = w_all.shape[4] - 16, ffn_all.shape[5]
        every = slice(None)
        tails = [(slice(owned, owned + 16), every)]
        tails += [(slice(0, owned), slice(i * 128, i * 128 + 128)) for i in range(D // 128)]
        cut = (units // ROWS + 1) // 2 * ROWS
        parts = (slice(0, cut), slice(cut, units))
        pieces = [
            PieceGather(me, layers, w_all, tail, send.at[i], recv.at[i], "xy"[i % 2])
            for i, tail in enumerate(tails)
        ]
        for part in parts:
            for j in range(2):
                i = len(pieces)
                pieces.append(
                    PieceGather(
                        me, layers, ffn_all.at[j], (part, every), send.at[i], recv.at[i],
                        "xy"[i % 2],
                    )
                )

        def act(actions):
            for piece, stage in actions:
                if stage < 4:
                    pieces[piece].advance(stage)
                else:
                    pieces[piece].wait(3)

        results = [
            pltpu.make_async_copy(w_all.at[:, :, :, :, 0:owned], attn_ref, local.at[0]),
            pltpu.make_async_copy(ffn_all, ffn_all_ref, local.at[1]),
        ]
    else:
        hidden, w_t, bias_t = rest

    @pl.when(step == 0)
    def _():
        if layers:
            greet(me, layers)
            own = [
                pltpu.make_async_copy(source, w_all.at[spot + (pl.ds(*at),)], local.at[i])
                for i, source, at in ((0, w_ref, (0, owned)), (2, rows_ref, (owned, 16)))
            ]
            own += [
                pltpu.make_async_copy(ffn_ref.at[j], ffn_all.at[(j,) + spot], local.at[3 + j])
                for j in range(2)
            ]
            for copy in own:
                copy.start()
            for copy in own:
                copy.wait()
            meet(layers)
            for piece in pieces:
                piece.start(0)
            act(GATHER_AHEAD)
            rows = jnp.zeros((16, D), F32)
            for z in range(layers):
                for i in range(8):
                    rows += w_all[z, i // 4, i // 2 % 2, i % 2, owned : owned + 16].astype(F32)
            all_rows_ref[...] = rows
        else:
            rows = rows_ref[...]
        bias_t[...] = rows.T
        for s in range(seqs):
            whitened, _ = whiten(x_ref[s].astype(F32))
            hidden[s] = (whitened * rows[0:1] + rows[2:3]).astype(BF)

    columns = pl.ds(pl.multiple_of(group * 128, 128), 128)

    @pl.when(seq == 0)
    def _():
        for j in range(3):
            if layers:
                block = w_all[j, :, :, :, 0:owned, columns].reshape(D, 128)
            else:
                block = w_ref[j, :, columns]
            w_t[j * 128 : (j + 1) * 128] = block.T

    cosine, sine = cos_ref[...], sin_ref[...]
    scale = 1.0 / math.sqrt(HEAD)
    lin = dot_nt(w_t[...], hidden[seq])
    for j, out_ref in enumerate((q_ref, k_ref, v_ref)):
        part = lin[j * 128 : (j + 1) * 128] + bias_t[columns, 4 + j : 5 + j]
        if j < 2:
            first, second = halves(part)
            part = joined(first * cosine - second * sine, second * cosine + first * sine)
            if j == 0:
                part = part * scale
        out_ref[0] = part.astype(BF)

    spots = lax.broadcasted_iota(jnp.int32, (16, length), 1)
    lead = lax.broadcasted_iota(jnp.int32, (16, length), 0) == 0
    mask = jnp.where(lead & (spots >= lens[seq]), -1e9, 0.0).astype(BF)
    ones = jnp.where(lead, 1.0, 0.0).astype(BF)
    keys = jnp.concatenate([k_ref[0], mask], axis=0).T

    def scored(h):
        blank = jnp.zeros((HEAD, length), BF)
        rows_q = [blank] * 4
        rows_q[h] = q_ref[0, h * HEAD : (h + 1) * HEAD]
        return dot_nn(keys, jnp.concatenate(rows_q + [ones], axis=0))

    def soft(h, scores):
        exponent = jnp.exp(scores - jnp.max(scores, axis=0, keepdims=True))
        inverse = 1.0 / jnp.sum(exponent, axis=0, keepdims=True)
        exponent = exponent.astype(BF)
        exp_ref[0, h] = exponent
        inv_ref[0, 0, h : h + 1] = inverse
        return exponent, inverse

    def mix(h, pair):
        at = slice(h * HEAD, (h + 1) * HEAD)
        mixed = dot_nn(v_ref[0, at], pair[0]) * pair[1]
        raw_ref[0, at] = mixed
        mix_ref[0, at] = mixed.astype(BF)

    ahead = scored(0)
    for h in range(4):
        scores = ahead
        if h < 3:
            ahead = scored(h + 1)
        mix(h, soft(h, scores))

    if layers:
        for after, actions in GATHER_AFTER.items():
            pl.when(step == after)(functools.partial(act, actions))

        @pl.when(step == 11)
        def _():
            results[0].start()

        @pl.when(step == 13)
        def _():
            results[1].start()

        @pl.when(step == 14)
        def _():
            for copy in results:
                copy.wait()


def backward_attention(
    lens, x_ref, w_ref, rows_ref, cos_ref, sin_ref,
    q_ref, k_ref, v_ref, gmix_ref, raw_ref, inv_ref, exp_ref, gmid_ref,
    gx_ref, gw_ref, small_ref, w_t, g_t,
):
    length = x_ref.shape[1]
    seq, group = pl.program_id(0), pl.program_id(1)

    @pl.when((seq == 0) & (group == 0))
    def _():
        for j in range(3):
            w_t[pl.ds(j * D, D), :] = matrix(w_ref, j).T
        gw_ref[...] = jnp.zeros_like(gw_ref)
        small_ref[...] = jnp.zeros_like(small_ref)

    limit = lens[seq]
    scale = 1.0 / math.sqrt(HEAD)
    low_edge = 0
    for extent in key_extents(length):

        @pl.when((limit > low_edge) & (limit <= extent))
        def _(extent=extent):
            cosine, sine = cos_ref[...], sin_ref[...]
            start = pl.multiple_of(group * 128, 128)
            if extent < length:
                for j in (1, 2):
                    g_t[pl.ds(start + j * D, 128), extent:length] = jnp.zeros(
                        (128, length - extent), BF
                    )

            def back_turn(w, c, s):
                first, second = w[:HALF], w[HALF:]
                return jnp.concatenate(
                    [first * c + second * s, second * c - first * s], axis=0
                ).astype(BF)

            for h in range(4):
                at = slice(h * HEAD, (h + 1) * HEAD)
                row = start + h * HEAD
                query, key = q_ref[0, at], k_ref[0, at, 0:extent]
                exponent = exp_ref[0, h, 0:extent]
                inverse = inv_ref[0, 0, h : h + 1]
                grad_mixed = (gmix_ref[0, at].astype(F32) * inverse).astype(BF)
                inner = jnp.sum(
                    raw_ref[0, at] * grad_mixed.astype(F32), axis=0, keepdims=True
                )
                grad_probs = dot_tn(v_ref[0, at, 0:extent], grad_mixed)
                grad_scores = (exponent.astype(F32) * (grad_probs - inner)).astype(BF)
                grad_value = dot_nt(grad_mixed, exponent)
                grad_key = dot_nt(query, grad_scores)
                grad_query = dot_nn(key, grad_scores) * scale
                g_t[pl.ds(row, HEAD), :] = back_turn(grad_query, cosine, sine)
                g_t[pl.ds(row + D, HEAD), 0:extent] = back_turn(
                    grad_key, cosine[:, 0:extent], sine[:, 0:extent]
                )
                g_t[pl.ds(row + 2 * D, HEAD), 0:extent] = grad_value.astype(BF)

        low_edge = extent

    @pl.when(group == pl.num_programs(1) - 1)
    def _():
        whitened, inverse = whiten(x_ref[0].astype(F32))
        gain = rows_ref[0:1, :]
        hidden = (whitened * gain + rows_ref[2:3, :]).astype(BF)
        hidden_t = hidden.T
        grads = g_t[...]
        ones = jnp.ones((8, length), BF)
        grad_hidden = dot_tn(grads, w_t[...])
        for j in range(3):
            part = grads[j * D : (j + 1) * D]
            small_ref[2 + j : 3 + j, :] += dot_nt(ones, part)[0:1]
            gw_ref[pl.ds(j * D, D), :] += dot_nt(hidden_t, part)
        small_ref[0:1, :] += jnp.sum(grad_hidden * whitened, axis=0, keepdims=True)
        small_ref[1:2, :] += jnp.sum(grad_hidden, axis=0, keepdims=True)
        gx_ref[0] = gmid_ref[0] + whiten_back(grad_hidden, whitened, inverse, gain)


def feed_forward(
    layers,
    x_ref, mix_ref, wo_ref, rows_ref, cot_ref, u_ref, v_ref, fbias_ref,
    head_ref, label_ref, live_ref,
    out_ref, gmid_ref, gmix_ref, gffn_ref, gfb_ref, gwo_ref, small_ref,
    middle, hidden, cot, down, grad_hidden, act_low, grad_low, x_buf, mix_buf, cot_buf,
    copied, *comm,
):
    seqs, length = x_ref.shape[0], x_ref.shape[1]
    pad = hidden.shape[0] // seqs
    step = pl.program_id(0)
    last = pl.num_programs(0) - 1
    chunk = act_low.shape[1]

    def moves(pairs, first):
        return [
            [
                pltpu.make_async_copy(a.at[s], b.at[s], copied.at[first + i, s])
                for i, (a, b) in enumerate(pairs)
            ]
            for s in range(seqs)
        ]

    arrivals = moves(((mix_ref, mix_buf), (x_ref, x_buf), (cot_ref, cot_buf)), 0)
    leavings = moves(((mix_buf, gmix_ref), (x_buf, out_ref), (middle, gmid_ref)), 3)
    if layers:
        me = position()
        terms, comm = comm[:2], comm[2:]

        def pieces(k):
            slot = lax.rem(k, 2) * 2
            return [PieceReduce(me, layers, comm, slot + j, "yx"[j]) for j in range(2)]

        def getter(j):
            def get(layer, rest, core):
                at = ((layer * 4 + rest) * 2 + core) * ROWS
                return terms[j][pl.ds(pl.multiple_of(at, ROWS), ROWS), :]

            return get

        def over_first(k):
            for j, op in enumerate(pieces(k)):
                op.over_first(getter(j))

        def over_second(k):
            for op in pieces(k):
                op.over_second()

        def over_layers(k):
            for op in pieces(k):
                op.over_layers()

        def finish(k):
            rows = pl.ds(pl.multiple_of(k * ROWS, ROWS), ROWS)
            for j, op in enumerate(pieces(k)):
                gffn_ref[j, rows, :] = op.finish()

    def later(stage, delay):
        if layers:
            pl.when(step >= delay)(lambda: stage(step - delay))

    @pl.when(step == 0)
    def _():
        for s in range(seqs):
            for copy in arrivals[s]:
                copy.start()
        if layers:
            greet(me, layers)
        blank = jnp.zeros((pad - length, D), BF)
        for s in range(seqs):
            for copy in arrivals[s]:
                copy.wait()
            branch = dot_tn(mix_buf[s], matrix(wo_ref, 0)) + rows_ref[7:8, :]
            mid = x_buf[s].astype(F32) + branch
            middle[s] = mid
            whitened, _ = whiten(mid)
            low = (whitened * rows_ref[1:2, :] + rows_ref[3:4, :]).astype(BF)
            hidden[pl.ds(s * pad, pad), :] = jnp.concatenate([low, blank], axis=0)
            cot[pl.ds(s * pad, pad), :] = jnp.concatenate([cot_buf[s], blank], axis=0)
        down[...] = jnp.zeros_like(down)
        grad_hidden[...] = jnp.zeros_like(grad_hidden)
        gfb_ref[...] = jnp.zeros_like(gfb_ref)
        if layers:
            meet(layers)

    up_w = u_ref[0].reshape(chunk, D)
    down_w = v_ref[0].reshape(chunk, D)
    fbias = fbias_ref[0]
    total = jnp.zeros_like(fbias)
    def lifted(s):
        rows = pl.ds(s * pad, pad)
        return dot_nt(hidden[rows, :], up_w) + fbias, dot_nt(cot[rows, :], down_w)

    ahead = lifted(0)
    for s in range(seqs):
        rows = pl.ds(s * pad, pad)
        upward, grad_act = ahead
        if s + 1 < seqs:
            ahead = lifted(s + 1)
        phi = 0.5 * (1.0 + lax.erf(upward * ROOT_HALF))
        act = (upward * phi).astype(BF)
        slope = phi + upward * jnp.exp(-0.5 * upward * upward) * INV_ROOT_TWO_PI
        grad_up = (grad_act * slope).astype(BF)
        act_low[rows, :] = act
        grad_low[rows, :] = grad_up
        total += jnp.sum(grad_up.astype(F32), axis=0, keepdims=True)
        down[rows, :] += dot_nn(act, down_w)
        grad_hidden[rows, :] += dot_nn(grad_up, up_w)
        if layers and s == 0:
            later(over_first, 1)
            later(over_layers, 2)
    gfb_ref[step, :, 0:chunk] = total
    grad_u = dot_tn(grad_low[...], hidden[...])
    if layers:
        later(over_second, 1)
        later(finish, 2)
        terms[0][...] = grad_u
        pieces(step)[0].over_cores(getter(0))
        terms[1][...] = dot_tn(act_low[...], cot[...])
        pieces(step)[1].over_cores(getter(1))
    else:
        gffn_ref[0, 0] = grad_u
        gffn_ref[1, 0] = dot_tn(act_low[...], cot[...])

    @pl.when(step == last)
    def _():
        gain = rows_ref[1:2, :]
        gain_sum = jnp.zeros((1, D), F32)
        shift_sum = jnp.zeros((1, D), F32)
        branch_sum = jnp.zeros((1, D), F32)
        cot_sum = jnp.zeros((1, D), F32)
        loglik = jnp.zeros((1, length), F32)
        hits = jnp.zeros((1, length), F32)
        gwo_ref[...] = jnp.zeros_like(gwo_ref)
        for s in range(seqs):
            rows = pl.ds(s * pad, length)
            mid = middle[s]
            final = mid + (down[rows, :] + rows_ref[8:9, :])
            x_buf[s] = final.astype(BF)
            leavings[s][1].start()
            unit, _ = whiten(final)
            logits = dot_nt(head_ref[...], unit.astype(BF))
            slot = lax.broadcasted_iota(jnp.int32, logits.shape, 0)
            logits = jnp.where(slot < VOCAB, logits, -1e30)
            shifted = logits - jnp.max(logits, axis=0, keepdims=True)
            logprob = shifted - jnp.log(jnp.sum(jnp.exp(shifted), axis=0, keepdims=True))
            picked = jnp.sum(
                jnp.where(slot == label_ref[s : s + 1, :], logprob, 0.0), axis=0, keepdims=True
            )
            live = live_ref[s : s + 1, :] != 0
            loglik += jnp.where(live, picked, 0.0)
            hits += jnp.where(live, jnp.exp(picked), 0.0)

            gradient = grad_hidden[rows, :]
            whitened, inverse = whiten(mid)
            gain_sum += jnp.sum(gradient * whitened, axis=0, keepdims=True)
            shift_sum += jnp.sum(gradient, axis=0, keepdims=True)
            own = cot_buf[s].astype(F32)
            cot_sum += jnp.sum(own, axis=0, keepdims=True)
            grad_mid = own + whiten_back(gradient, whitened, inverse, gain)
            middle[s] = grad_mid
            leavings[s][2].start()
            low = grad_mid.astype(BF)
            branch_sum += jnp.sum(low.astype(F32), axis=0, keepdims=True)
            gwo_ref[...] += dot_nn(mix_buf[s], low)
            mix_buf[s] = dot_nt(matrix(wo_ref, 0), low).astype(BF)
            leavings[s][0].start()
            if layers:
                if s == 0:
                    over_first(last)
                    over_layers(last - 1)
                if s == seqs - 2:
                    over_second(last)
                    finish(last - 1)
                if s == seqs - 1:
                    over_layers(last)
        small_ref[0:1, :] = gain_sum
        small_ref[1:2, :] = shift_sum
        small_ref[2:3, :] = branch_sum
        small_ref[3:4, :] = cot_sum
        small_ref[4:8, :] = jnp.zeros((4, D), F32)
        small_ref[4:5, 0:128] = jnp.broadcast_to(
            jnp.sum(loglik, axis=1, keepdims=True), (1, 128)
        )
        small_ref[4:5, 128:256] = jnp.broadcast_to(
            jnp.sum(hits, axis=1, keepdims=True), (1, 128)
        )
        for s in range(seqs):
            for copy in leavings[s]:
                copy.wait()
        if layers:
            finish(last)


def whole(shape):
    return pl.BlockSpec(shape, lambda *_: (0,) * len(shape), pipeline_mode=pl.Buffered(1))


def block_of(shape, *index):
    return pl.BlockSpec(shape, lambda *_: index, pipeline_mode=pl.Buffered(1))


def leading(shape):
    return pl.BlockSpec((1,) + tuple(shape[1:]), lambda i, *_: (i,) + (0,) * (len(shape) - 1))


def shaped(shape, dtype=F32):
    return jax.ShapeDtypeStruct(shape, dtype)


def projections(attn, first, count):
    blocks = attn.shape[0] // 4
    rows = D // blocks
    return block_of((blocks * count, rows, D), first // count, 0, 0)


def attention_forward(lengths, tokens, rows_all, attn, ffn, cosine, sine, layers):
    seqs, length, _ = tokens.shape
    heads = HEADS // 4
    flat = (seqs, D, length)
    inverse = (seqs, heads, 4, length)
    exponent = (seqs, HEADS, length, length)

    def part(block):
        return pl.BlockSpec(block, lambda g, s, *_: (s, g, 0, 0)[: len(block)])

    out_specs = [part((1, 128, length))] * 5
    out_specs += [part((1, 1, 4, length)), part((1, 4, length, length))]
    out_shape = [shaped(flat, BF)] * 4 + [shaped(flat), shaped(inverse), shaped(exponent, BF)]
    scratch = [
        pltpu.VMEM((seqs, length, D), BF), pltpu.VMEM((384, D), BF), pltpu.VMEM((D, 16), F32),
    ]
    hbm = pl.BlockSpec(memory_space=pl.ANY)
    params = dict(vmem_limit_bytes=VMEM_LIMIT)
    if layers:
        chips = (layers, 2, 2, 2)
        owned, units = attn.shape[0], ffn.shape[1]
        out_specs += [whole((16, D)), hbm, hbm]
        out_shape += [
            shaped((16, D)), shaped(chips + (owned, D), BF),
            shaped((2,) + chips + (units, D), BF),
        ]
        scratch += [
            pltpu.VMEM(chips + (owned + 16, D), BF), pltpu.VMEM((2,) + chips + (units, D), BF),
            pltpu.SemaphoreType.DMA((10, 2 + layers)), pltpu.SemaphoreType.DMA((10, 2 + layers)),
            pltpu.SemaphoreType.DMA((5,)),
        ]
        params.update(collective_id=2, has_side_effects=True)
        sources = [hbm, hbm, hbm]
    else:
        sources = [whole(rows_all.shape), whole(attn.shape), hbm]
    return pl.pallas_call(
        functools.partial(forward_attention, layers),
        grid_spec=pltpu.PrefetchScalarGridSpec(
            num_scalar_prefetch=1,
            grid=(heads, seqs),
            in_specs=[whole(tokens.shape)] + sources + [whole(cosine.shape), whole(sine.shape)],
            out_specs=out_specs,
            scratch_shapes=scratch,
        ),
        out_shape=out_shape,
        compiler_params=pltpu.CompilerParams(**params),
        name="attention_forward",
    )(lengths, tokens, rows_all, attn, ffn, cosine, sine)


def attention_backward(
    lengths, tokens, attn, rows_all, cosine, sine, query, key, value, grad_mixed, raw,
    inverse, exponent, grad_middle,
):
    seqs, length, _ = tokens.shape

    def part(block):
        return pl.BlockSpec(block, lambda s, g, *_: (s, g, 0, 0)[: len(block)])

    return pl.pallas_call(
        backward_attention,
        grid_spec=pltpu.PrefetchScalarGridSpec(
            num_scalar_prefetch=1,
            grid=(seqs, HEADS // 4),
            in_specs=[
                leading(tokens.shape), projections(attn, 0, 3), whole(rows_all.shape),
                whole(cosine.shape), whole(sine.shape),
            ]
            + [part((1, 128, length))] * 5
            + [part((1, 1, 4, length)), part((1, 4, length, length)), leading(tokens.shape)],
            out_specs=[leading(tokens.shape), whole((3 * D, D)), whole((8, D))],
            scratch_shapes=[pltpu.VMEM((3 * D, D), BF), pltpu.VMEM((3 * D, length), BF)],
        ),
        out_shape=[shaped(tokens.shape), shaped((3 * D, D)), shaped((8, D))],
        compiler_params=pltpu.CompilerParams(vmem_limit_bytes=VMEM_LIMIT),
        name="attention_backward",
    )(
        lengths, tokens, attn, rows_all, cosine, sine, query, key, value, grad_mixed, raw,
        inverse, exponent, grad_middle,
    )


def feed_forward_both(
    tokens, mixed, attn, rows_all, cotangent, ffn, fbias, head_t, labels, live, layers,
):
    seqs, length, _ = tokens.shape
    pad = (length + 15) // 16 * 16
    rows = seqs * pad
    steps, chunk = fbias.shape
    hbm = pl.BlockSpec(memory_space=pl.ANY)
    if layers:
        devices, owned = ffn.shape[1], ffn.shape[2]
        up_spec, down_spec = (
            pl.BlockSpec((1, devices, ROWS, D), lambda k, j=j: (j, 0, k, 0)) for j in range(2)
        )
        ups = downs = ffn
        grad_spec, grad_shape = whole((2, owned, D)), shaped((2, owned, D))
        extra = [pltpu.VMEM((chunk, D), F32)] * 2 + reduce_scratch(4, layers)
    else:
        chunked = (steps, chunk, D)
        ups, downs = ffn[0].reshape(chunked), ffn[1].reshape(chunked)
        up_spec = down_spec = leading(chunked)
        grad_spec = pl.BlockSpec((2, 1, chunk, D), lambda k: (0, k, 0, 0))
        grad_shape = shaped((2,) + chunked)
        extra = []
    return pl.pallas_call(
        functools.partial(feed_forward, layers),
        grid=(steps,),
        in_specs=[
            hbm, hbm, projections(attn, 3, 1), whole(rows_all.shape), hbm, up_spec, down_spec,
            leading((steps, 1, chunk)), whole(head_t.shape), whole(labels.shape),
            whole(live.shape),
        ],
        out_specs=[
            hbm, hbm, hbm, grad_spec, whole((8, 1, D)), whole((D, D)), whole((8, D)),
        ],
        out_shape=[
            shaped(tokens.shape, BF), shaped(tokens.shape), shaped(mixed.shape, BF),
            grad_shape, shaped((8, 1, D)), shaped((D, D)), shaped((8, D)),
        ],
        scratch_shapes=[
            pltpu.VMEM(tokens.shape, F32),
            pltpu.VMEM((rows, D), BF),
            pltpu.VMEM((rows, D), BF),
            pltpu.VMEM((rows, D), F32),
            pltpu.VMEM((rows, D), F32),
            pltpu.VMEM((rows, chunk), BF),
            pltpu.VMEM((rows, chunk), BF),
            pltpu.VMEM(tokens.shape, BF),
            pltpu.VMEM(mixed.shape, BF),
            pltpu.VMEM(tokens.shape, BF),
            pltpu.SemaphoreType.DMA((6, seqs)),
        ]
        + extra,
        compiler_params=pltpu.CompilerParams(
            vmem_limit_bytes=VMEM_LIMIT, **(dict(collective_id=0, has_side_effects=True) if layers else {})
        ),
        name="feed_forward",
    )(
        tokens, mixed, attn, rows_all, cotangent, ups, downs,
        fbias.reshape(steps, 1, chunk), head_t, labels, live,
    )


def reduce_tail(grad_qkv, grad_wo, small_one, small_two, units, layers):
    devices = 4 * grad_wo.shape[0]
    owned = grad_wo.shape[1]
    pieces = owned // ROWS
    return pl.pallas_call(
        functools.partial(gradient_tail, layers, pieces),
        in_specs=[pl.BlockSpec(memory_space=pltpu.VMEM)] * 5,
        out_specs=[pl.BlockSpec(memory_space=pltpu.VMEM)] * 2,
        out_shape=[shaped((owned, D)), shaped((24, D))],
        scratch_shapes=[
            pltpu.VMEM((4, 24, D), F32),
            pltpu.VMEM((3 + layers, 24, D), F32),
            pltpu.SemaphoreType.DMA((2 + layers,)),
            pltpu.SemaphoreType.DMA((2 + layers,)),
        ]
        + reduce_scratch(pieces, layers),
        compiler_params=pltpu.CompilerParams(
            vmem_limit_bytes=VMEM_LIMIT, collective_id=1, has_side_effects=True
        ),
        name="gradient_tail",
    )(grad_qkv, grad_wo, small_one, small_two, units)


def per_device(
    tokens, lengths, masked_flags, labels, attn_weights, ffn_weights, ffn_bias, norm_gains,
    biases, head_weight, cotangent,
):
    both = ("wide", "narrow")
    seqs, length, _ = tokens.shape
    wide, narrow = lax.axis_size("wide"), lax.axis_size("narrow")
    devices = wide * narrow
    shard, units = D // wide, ffn_bias.shape[0]
    owned = attn_weights.shape[0]
    layers = 4 if (wide, narrow) == (8, 4) and owned == units and owned % ROWS == 0 else 0
    at = lax.axis_index("wide")
    owner = at * narrow + lax.axis_index("narrow")
    first = (lax.axis_index("narrow") == 0).astype(BF)
    own = jnp.concatenate([norm_gains, biases], axis=0) * first
    rows_own = lax.dynamic_update_slice(jnp.zeros((16, D), BF), own, (0, at * shard))
    flat = lax.dynamic_update_slice(jnp.zeros((4 * D,), BF), ffn_bias, (owner * units,))
    rows_own = rows_own + jnp.pad(flat.reshape(4, D), ((9, 3), (0, 0)))
    cosine, sine = rotary_tables(length)
    if layers:
        rows_all, attn, ffn = rows_own, attn_weights, ffn_weights
    else:
        attn = lax.all_gather(attn_weights, both, axis=0, tiled=True).reshape(4, D, D)
        ffn = lax.all_gather(ffn_weights, both, axis=1, tiled=True)
        rows_all = lax.psum(rows_own.astype(F32), both)
    query, key, value, mixed, raw, inverse, exponent, *gathered = attention_forward(
        lengths, tokens, rows_all, attn, ffn, cosine, sine, layers
    )
    if layers:
        rows_all, attn, ffn = gathered
        attn = attn.reshape(devices, owned, D)
        ffn = ffn.reshape(2, devices, units, D)
        unit_bias = rows_all[9:13].reshape(devices, units // ROWS, ROWS).transpose(1, 0, 2)
        unit_bias = unit_bias.reshape(units // ROWS, devices * ROWS)
    else:
        unit_bias = rows_all[9:13].reshape(-1, 512)
    live = (masked_flags == 1) & (jnp.arange(length)[None, :] < lengths[:, None])
    head_t = jnp.pad(head_weight.T, ((0, 7), (0, 0)))
    (
        output, grad_middle, grad_mixed, grad_ffn, unit_sums, grad_wo, small_two,
    ) = feed_forward_both(
        tokens, mixed, attn, rows_all, cotangent, ffn, unit_bias, head_t, labels,
        live.astype(jnp.int32), layers,
    )
    if not layers:
        grad_ffn = lax.psum_scatter(
            grad_ffn.reshape(2, -1, D), both, scatter_dimension=1, tiled=True
        )
    grad_tokens, grad_qkv, small_one = attention_backward(
        lengths, tokens, attn, rows_all, cosine, sine, query, key, value, grad_mixed, raw,
        inverse, exponent, grad_middle,
    )
    steps, chunk = unit_bias.shape
    if layers:
        blocks = (-1, owned, D)
        grad_attn, sums = reduce_tail(
            grad_qkv.reshape(blocks), grad_wo.reshape(blocks), small_one, small_two, unit_sums,
            layers,
        )
        grad_ffn_bias = lax.dynamic_slice(
            sums, (16, owner * ROWS), (steps, ROWS)
        ).reshape(units)
    else:
        grad_attn = lax.psum_scatter(
            jnp.concatenate([grad_qkv, grad_wo], axis=0), both, scatter_dimension=0, tiled=True
        )
        sums = jnp.concatenate(
            [
                small_one[0:1], small_two[0:1], small_one[1:2], small_two[1:2], small_one[2:5],
                small_two[2:5], jnp.zeros((6, D), F32), unit_sums[:, 0],
            ],
            axis=0,
        )
        sums = lax.psum(sums, both)
        grad_ffn_bias = lax.dynamic_slice_in_dim(
            sums[16:, :chunk].reshape(-1), owner * units, units, 0
        )
    grad_gains = lax.dynamic_slice(sums, (0, at * shard), (2, shard))
    grad_biases = lax.dynamic_slice(sums, (2, at * shard), (7, shard))
    head_stats = (
        sums[9, 0:256:128] * jnp.array([1.0, VOCAB], F32) / (seqs * length * devices)
    )
    return (
        output, grad_tokens, grad_attn, grad_ffn, grad_ffn_bias, grad_gains, grad_biases,
        head_stats,
    )


def solution(mesh):
    both = ("wide", "narrow")
    return jax.shard_map(
        per_device,
        mesh=mesh,
        in_specs=(
            P(both, None, None),
            P(both),
            P(both, None),
            P(both, None),
            P(both, None),
            P(None, both, None),
            P(both),
            P(None, "wide"),
            P(None, "wide"),
            P(),
            P(both, None, None),
        ),
        out_specs=(
            P(both, None, None),
            P(both, None, None),
            P(both, None),
            P(None, both, None),
            P(both),
            P(None, "wide"),
            P(None, "wide"),
            P(),
        ),
        check_vma=False,
    )
```

```python
import functools
import math

import jax
import jax.numpy as jnp
import numpy as np
from jax import lax
from jax.experimental import pallas as pl
from jax.experimental.pallas import tpu as pltpu
from jax.sharding import PartitionSpec as P

D = 640
HEADS = 20
HEAD = 32
HALF = HEAD // 2
VOCAB = 33
EPS = 1e-05
ROOT_HALF = 0.7071067811865476
INV_ROOT_TWO_PI = 0.3989422804014327
BF = jnp.bfloat16
F32 = jnp.float32
VMEM_LIMIT = 60 << 20

MESH = pl.DeviceIdType.MESH
ROWS = 16


def position():
    wide, narrow = lax.axis_index("wide"), lax.axis_index("narrow")
    return {
        "z": lax.div(wide, 2), "x": lax.rem(wide, 2),
        "y": lax.div(narrow, 2), "c": lax.rem(narrow, 2),
    }


def partner(me, axis, offset, size):
    there = dict(me)
    there[axis] = lax.rem(me[axis] + offset, size)
    return (there["z"] * 2 + there["x"], there["y"] * 2 + there["c"])


def greet(me, layers):
    barrier = pltpu.get_barrier_semaphore()
    peers = [partner(me, axis, 1, 2) for axis in "cyx"]
    peers += [partner(me, "z", offset, layers) for offset in range(1, layers)]
    for peer in peers:
        pl.semaphore_signal(barrier, inc=1, device_id=peer, device_id_type=MESH)


def meet(layers):
    pl.semaphore_wait(pltpu.get_barrier_semaphore(), 2 + layers)


def reduce_scratch(slots, layers):
    def blocks(count, dtype):
        return pltpu.VMEM((slots, count, ROWS, D), dtype)

    return [
        blocks(4 * layers, BF), blocks(4 * layers, BF),
        blocks(2 * layers, BF), blocks(2 * layers, BF), blocks(2 * layers, F32),
        blocks(layers, BF), blocks(layers, BF), blocks(layers, F32),
        blocks(layers, BF), blocks(layers, BF), blocks(1, F32),
        pltpu.SemaphoreType.DMA((slots, 3 + layers)),
        pltpu.SemaphoreType.DMA((slots, 3 + layers)),
    ]


class PieceReduce:
    def __init__(self, me, layers, refs, slot, first):
        (
            self.s0, self.r0, self.s1, self.r1, self.k1, self.s2, self.r2, self.k2,
            self.s3, self.r3, self.k3,
        ) = (ref.at[slot] for ref in refs[:11])
        self.send, self.recv = (ref.at[slot] for ref in refs[11:])
        self.me, self.layers = me, layers
        self.first, self.second = ("y", "x") if first == "y" else ("x", "y")

    def exchange(self, stage, source, target, axis):
        return pltpu.make_async_remote_copy(
            src_ref=source, dst_ref=target, send_sem=self.send.at[stage],
            recv_sem=self.recv.at[stage], device_id=partner(self.me, axis, 1, 2),
            device_id_type=MESH,
        )

    def layer_copies(self):
        me, layers = self.me, self.layers
        return [
            pltpu.make_async_remote_copy(
                src_ref=self.s3.at[lax.rem(me["z"] + offset, layers)],
                dst_ref=self.r3.at[offset], send_sem=self.send.at[2 + offset],
                recv_sem=self.recv.at[2 + offset],
                device_id=partner(me, "z", offset, layers), device_id_type=MESH,
            )
            for offset in range(1, layers)
        ]

    def rest(self, along, other):
        return other * 2 + along if self.first == "y" else along * 2 + other

    def over_cores(self, get):
        core = self.me["c"]
        for layer in range(self.layers):
            for rest in range(4):
                self.s0[layer * 4 + rest] = get(layer, rest, 1 - core).astype(BF)
        self.exchange(0, self.s0, self.r0, "c").start()

    def over_first(self, get):
        self.exchange(0, self.s0, self.r0, "c").wait()
        core, along = self.me["c"], self.me[self.first]
        for layer in range(self.layers):
            for other in range(2):
                away, near = self.rest(1 - along, other), self.rest(along, other)
                at = layer * 2 + other
                self.s1[at] = (
                    get(layer, away, core) + self.r0[layer * 4 + away].astype(F32)
                ).astype(BF)
                self.k1[at] = get(layer, near, core) + self.r0[layer * 4 + near].astype(F32)
        self.exchange(1, self.s1, self.r1, self.first).start()

    def over_second(self):
        self.exchange(1, self.s1, self.r1, self.first).wait()
        along = self.me[self.second]
        for layer in range(self.layers):
            away, near = layer * 2 + (1 - along), layer * 2 + along
            self.s2[layer] = (self.k1[away] + self.r1[away].astype(F32)).astype(BF)
            self.k2[layer] = self.k1[near] + self.r1[near].astype(F32)
        self.exchange(2, self.s2, self.r2, self.second).start()

    def over_layers(self):
        self.exchange(2, self.s2, self.r2, self.second).wait()
        own = self.me["z"]
        for layer in range(self.layers):
            self.s3[layer] = (self.k2[layer] + self.r2[layer].astype(F32)).astype(BF)
        self.k3[0] = self.k2[own] + self.r2[own].astype(F32)
        for copy in self.layer_copies():
            copy.start()

    def finish(self):
        for copy in self.layer_copies():
            copy.wait()
        total = self.k3[0]
        for offset in range(1, self.layers):
            total = total + self.r3[offset].astype(F32)
        return total


class PieceGather:
    def __init__(self, me, layers, buf, tail, send, recv, first):
        self.me, self.layers, self.buf, self.tail = me, layers, buf, tail
        self.send, self.recv, self.first = send, recv, first

    def view(self, *lead):
        return self.buf.at[lead + self.tail]

    def copy(self, lead, peer, at):
        return pltpu.make_async_remote_copy(
            src_ref=self.view(*lead), dst_ref=self.view(*lead), send_sem=self.send.at[at],
            recv_sem=self.recv.at[at], device_id=peer, device_id_type=MESH,
        )

    def copies(self, stage):
        me, every = self.me, slice(None)
        z, x, y, core = me["z"], me["x"], me["y"], me["c"]
        if stage == 0:
            return [
                self.copy((z, x, y, core), partner(me, "z", offset, self.layers), 2 + offset)
                for offset in range(1, self.layers)
            ]
        if stage == 1:
            lead, axis = (every, x, y, core), self.first
        elif stage == 2:
            lead = (every, every, y, core) if self.first == "x" else (every, x, every, core)
            axis = "y" if self.first == "x" else "x"
        else:
            lead, axis = (every, every, every, core), "c"
        return [self.copy(lead, partner(me, axis, 1, 2), stage - 1)]

    def start(self, stage):
        for copy in self.copies(stage):
            copy.start()

    def wait(self, stage):
        for copy in self.copies(stage):
            copy.wait()

    def advance(self, stage):
        self.wait(stage - 1)
        self.start(stage)


class SmallReduce:
    def __init__(self, me, layers, sent, got, send, recv):
        self.me, self.layers = me, layers
        self.sent, self.got, self.send, self.recv = sent, got, send, recv

    def exchange(self, stage):
        return pltpu.make_async_remote_copy(
            src_ref=self.sent.at[stage], dst_ref=self.got.at[stage],
            send_sem=self.send.at[stage], recv_sem=self.recv.at[stage],
            device_id=partner(self.me, "cyx"[stage], 1, 2), device_id_type=MESH,
        )

    def layer_copies(self):
        own = self.me["z"]
        return [
            pltpu.make_async_remote_copy(
                src_ref=self.sent.at[3], dst_ref=self.got.at[3 + own],
                send_sem=self.send.at[2 + offset], recv_sem=self.recv.at[2 + offset],
                device_id=partner(self.me, "z", offset, self.layers), device_id_type=MESH,
            )
            for offset in range(1, self.layers)
        ]

    def start(self, stage):
        if stage:
            self.exchange(stage - 1).wait()
            self.sent[stage] = self.sent[stage - 1] + self.got[stage - 1]
        if stage < 3:
            self.exchange(stage).start()
        else:
            for copy in self.layer_copies():
                copy.start()
            self.got[3 + self.me["z"]] = self.sent[3]

    def finish(self):
        for copy in self.layer_copies():
            copy.wait()
        total = self.got[3]
        for layer in range(1, self.layers):
            total = total + self.got[3 + layer]
        return total


TAIL_ORDER = (
    (0, 0), (1, 0), (2, 0), (7, 0), (3, 0), (4, 0), (0, 1), (1, 1), (7, 1), (5, 0), (6, 0),
    (2, 1), (3, 1), (4, 1), (5, 1), (7, 2), (6, 1), (0, 2), (1, 2), (2, 2), (3, 2), (7, 3),
    (4, 2), (0, 3), (1, 3), (5, 2), (6, 2), (2, 3), (3, 3), (4, 3), (0, 4), (1, 4), (7, 4),
    (5, 3), (6, 3), (2, 4), (3, 4), (4, 4), (5, 4), (6, 4),
)


def gradient_tail(layers, qkv_ref, wo_ref, late_ref, part_ref, one_ref, two_ref, units_ref,
                  grad_ref, gffn_ref, sums_ref, terms, loaded, sent, got, small_send,
                  small_recv, *refs):
    me = position()
    greet(me, layers)
    own, wo = qkv_ref.shape[0], wo_ref.shape[0]
    loads = []
    for p in range(terms.shape[0]):
        if p < 2:
            moves = [(late_ref.at[p], terms.at[p])]
        else:
            rows = slice((p - 2) * ROWS, (p - 1) * ROWS)
            moves = [
                (qkv_ref.at[:, rows], terms.at[p, 0:own]),
                (wo_ref.at[:, rows], terms.at[p, own : own + wo]),
            ]
        loads.append(
            [
                pltpu.make_async_copy(source, target, loaded.at[p, i])
                for i, (source, target) in enumerate(moves)
            ]
        )
        for copy in loads[-1]:
            copy.start()
    order = [(one_ref, 0), (two_ref, 0), (one_ref, 1), (two_ref, 1)]
    order += [(one_ref, 2), (one_ref, 3), (one_ref, 4), (two_ref, 2), (two_ref, 3), (two_ref, 4)]
    sent[0, 8:16] = jnp.zeros((8, D), F32)
    for row, (ref, at) in enumerate(order):
        sent[0, row : row + 1] = ref[at : at + 1]
    for k in range(8):
        sent[0, 16 + k : 17 + k] = units_ref[k]
    small = SmallReduce(me, layers, sent, got, small_send, small_recv)
    ops = [PieceReduce(me, layers, refs, p, "yx"[p % 2]) for p in range(terms.shape[0])]
    kept = part_ref.shape[1]
    gffn_ref[:, 0:kept] = part_ref[...]
    meet(layers)

    def getter(p):
        return lambda layer, rest, core: terms[p, layer * 8 + rest * 2 + core]

    for p, stage in TAIL_ORDER:
        if p == len(ops):
            if stage < 4:
                small.start(stage)
            else:
                sums_ref[...] = small.finish()
        elif stage == 0:
            for copy in loads[p]:
                copy.wait()
            ops[p].over_cores(getter(p))
        elif stage == 1:
            ops[p].over_first(getter(p))
        elif stage == 2:
            ops[p].over_second()
        elif stage == 3:
            ops[p].over_layers()
        elif p < 2:
            gffn_ref[p, kept:] = ops[p].finish()
        else:
            grad_ref[(p - 2) * ROWS : (p - 1) * ROWS] = ops[p].finish()


def dot_nn(a, b):
    return lax.dot_general(a, b, (((1,), (0,)), ((), ())), preferred_element_type=F32)


def dot_nt(a, b):
    return lax.dot_general(a, b, (((1,), (1,)), ((), ())), preferred_element_type=F32)


def dot_tn(a, b):
    return lax.dot_general(a, b, (((0,), (0,)), ((), ())), preferred_element_type=F32)


def matrix(ref, j):
    rows = ref.shape[1]
    blocks = D // rows
    return ref[j * blocks : (j + 1) * blocks].reshape(D, D)


def whiten(values):
    center = jnp.mean(values, axis=-1, keepdims=True)
    offset = values - center
    spread = jnp.mean(offset * offset, axis=-1, keepdims=True)
    inverse = lax.rsqrt(spread + EPS)
    return offset * inverse, inverse


def whiten_back(gradient, whitened, inverse, gain):
    scaled = gradient * gain
    mean_grad = jnp.mean(scaled, axis=-1, keepdims=True)
    mean_cross = jnp.mean(scaled * whitened, axis=-1, keepdims=True)
    return inverse * (scaled - mean_grad - whitened * mean_cross)


def rotary_tables(length):
    frequency = (
        np.float32(1.0)
        / np.float32(10000.0) ** (np.arange(HALF, dtype=np.float32) * np.float32(2.0 / HEAD))
    ).astype(np.float32)
    angles = frequency[:, None] * np.arange(length, dtype=np.float32)[None, :]
    return np.cos(angles).astype(np.float32), np.sin(angles).astype(np.float32)


def key_extents(length):
    extents = list(range(256, length, 128))
    return extents + [length]


def halves(values):
    length = values.shape[-1]
    split = values.reshape(values.shape[0] // HEAD, 2, HALF, length)
    return split[:, 0], split[:, 1]


def joined(first, second):
    length = first.shape[-1]
    both = jnp.concatenate([first[:, None], second[:, None]], axis=1)
    return both.reshape(first.shape[0] * HEAD, length)


GATHER_AHEAD = (
    (0, 1), (1, 1), (2, 1), (0, 2), (3, 1), (1, 2), (4, 1), (2, 2), (5, 1), (0, 3), (6, 1),
    (3, 2), (1, 3), (0, 4),
)
GATHER_FIRST = ((7, 1), (4, 2), (1, 4), (8, 1))
GATHER_AFTER = {
    0: ((2, 3), (6, 2), (9, 1), (5, 2)), 1: ((7, 2), (3, 3), (2, 4), (8, 2)),
    2: ((4, 3), (5, 3)), 3: ((6, 3), (9, 2)), 4: ((7, 3), (3, 4)), 5: ((8, 3),),
    6: ((9, 3),), 7: ((4, 4),), 8: ((5, 4),), 10: ((6, 4), (7, 4), (8, 4), (9, 4)),
}
EARLY = 2


def forward_attention(
    layers,
    lens, x_ref, rows_ref, w_ref, ffn_ref, cos_ref, sin_ref,
    q_ref, k_ref, v_ref, mix_ref, raw_ref, inv_ref, exp_ref, *rest,
):
    seqs, length = x_ref.shape[0], x_ref.shape[1]
    group, seq = pl.program_id(0), pl.program_id(1)
    step = group * seqs + seq
    if layers:
        all_rows_ref, attn_ref, ffn_all_ref, hidden, w_t, bias_t, white = rest[:7]
        w_all, ffn_all, send, recv, local = rest[7:]
        me = position()
        spot = (me["z"], me["x"], me["y"], me["c"])
        owned = w_all.shape[4] - 16
        every = slice(None)
        tails = [(slice(owned, owned + 16), every)]
        tails += [(slice(0, owned), slice(i * 128, i * 128 + 128)) for i in range(D // 128)]
        pieces = [
            PieceGather(me, layers, w_all, tail, send.at[i], recv.at[i], "xy"[i % 2])
            for i, tail in enumerate(tails)
        ]
        for k in range(EARLY):
            for j in range(2):
                i = len(pieces)
                pieces.append(
                    PieceGather(
                        me, layers, ffn_all.at[j, k], (), send.at[i], recv.at[i], "xy"[i % 2]
                    )
                )

        def act(actions):
            for piece, stage in actions:
                if stage < 4:
                    pieces[piece].advance(stage)
                else:
                    pieces[piece].wait(3)

        results = [
            pltpu.make_async_copy(w_all.at[:, :, :, :, 0:owned], attn_ref, local.at[0]),
            pltpu.make_async_copy(ffn_all, ffn_all_ref, local.at[1]),
        ]
    else:
        hidden, w_t, bias_t, white = rest

    @pl.when(step == 0)
    def _():
        if layers:
            greet(me, layers)
            own = [
                pltpu.make_async_copy(source, w_all.at[spot + (pl.ds(*at),)], local.at[i])
                for i, source, at in ((0, w_ref, (0, owned)), (2, rows_ref, (owned, 16)))
            ]
            own += [
                pltpu.make_async_copy(
                    ffn_ref.at[j, k * ROWS : (k + 1) * ROWS], ffn_all.at[(j, k) + spot],
                    local.at[3 + j * EARLY + k],
                )
                for j in range(2)
                for k in range(EARLY)
            ]
            for copy in own:
                copy.start()
            for copy in own:
                copy.wait()
            meet(layers)
            for piece in pieces:
                piece.start(0)
        for s in range(seqs):
            white[s] = whiten(x_ref[s].astype(F32))[0]
        if layers:
            act(GATHER_AHEAD)
            rows = jnp.zeros((16, D), F32)
            for z in range(layers):
                for i in range(8):
                    rows += w_all[z, i // 4, i // 2 % 2, i % 2, owned : owned + 16].astype(F32)
            all_rows_ref[...] = rows
        else:
            rows = rows_ref[...]
        bias_t[...] = rows.T
        for s in range(seqs):
            hidden[s] = (white[s] * rows[0:1] + rows[2:3]).astype(BF)
        if layers:
            act(GATHER_FIRST)

    columns = pl.ds(pl.multiple_of(group * 128, 128), 128)

    @pl.when(seq == 0)
    def _():
        for j in range(3):
            if layers:
                block = w_all[j, :, :, :, 0:owned, columns].reshape(D, 128)
            else:
                block = w_ref[j, :, columns]
            w_t[j * 128 : (j + 1) * 128] = block.T

    cosine, sine = cos_ref[...], sin_ref[...]
    scale = 1.0 / math.sqrt(HEAD)
    lin = dot_nt(w_t[...], hidden[seq])
    for j, out_ref in enumerate((q_ref, k_ref, v_ref)):
        part = lin[j * 128 : (j + 1) * 128] + bias_t[columns, 4 + j : 5 + j]
        if j < 2:
            first, second = halves(part)
            part = joined(first * cosine - second * sine, second * cosine + first * sine)
            if j == 0:
                part = part * scale
        out_ref[0] = part.astype(BF)

    spots = lax.broadcasted_iota(jnp.int32, (16, length), 1)
    lead = lax.broadcasted_iota(jnp.int32, (16, length), 0) == 0
    mask = jnp.where(lead & (spots >= lens[seq]), -1e9, 0.0).astype(BF)
    ones = jnp.where(lead, 1.0, 0.0).astype(BF)
    keys = jnp.concatenate([k_ref[0], mask], axis=0).T

    def scored(h):
        blank = jnp.zeros((HEAD, length), BF)
        rows_q = [blank] * 4
        rows_q[h] = q_ref[0, h * HEAD : (h + 1) * HEAD]
        return dot_nn(keys, jnp.concatenate(rows_q + [ones], axis=0))

    def soft(h, scores):
        exponent = jnp.exp(scores - jnp.max(scores, axis=0, keepdims=True))
        inverse = 1.0 / jnp.sum(exponent, axis=0, keepdims=True)
        exponent = exponent.astype(BF)
        exp_ref[0, h] = exponent
        inv_ref[0, 0, h : h + 1] = inverse
        return exponent, inverse

    def mix(h, pair):
        at = slice(h * HEAD, (h + 1) * HEAD)
        mixed = dot_nn(v_ref[0, at], pair[0]) * pair[1]
        raw_ref[0, at] = mixed
        mix_ref[0, at] = mixed.astype(BF)

    ahead = scored(0)
    for h in range(4):
        scores = ahead
        if h < 3:
            ahead = scored(h + 1)
        mix(h, soft(h, scores))

    if layers:
        for after, actions in GATHER_AFTER.items():
            pl.when(step == after)(functools.partial(act, actions))

        @pl.when(step == 8)
        def _():
            results[0].start()

        @pl.when(step == 10)
        def _():
            results[1].start()

        @pl.when(step == 14)
        def _():
            for copy in results:
                copy.wait()


def backward_attention(
    lens, x_ref, w_ref, rows_ref, cos_ref, sin_ref,
    q_ref, k_ref, v_ref, gmix_ref, raw_ref, inv_ref, exp_ref, gmid_ref,
    gx_ref, gw_ref, small_ref, w_t, g_t,
):
    length = x_ref.shape[1]
    seq, group = pl.program_id(0), pl.program_id(1)

    @pl.when((seq == 0) & (group == 0))
    def _():
        for j in range(3):
            w_t[pl.ds(j * D, D), :] = matrix(w_ref, j).T
        gw_ref[...] = jnp.zeros_like(gw_ref)
        small_ref[...] = jnp.zeros_like(small_ref)

    limit = lens[seq]
    scale = 1.0 / math.sqrt(HEAD)
    low_edge = 0
    for extent in key_extents(length):

        @pl.when((limit > low_edge) & (limit <= extent))
        def _(extent=extent):
            cosine, sine = cos_ref[...], sin_ref[...]
            start = pl.multiple_of(group * 128, 128)
            if extent < length:
                for j in (1, 2):
                    g_t[pl.ds(start + j * D, 128), extent:length] = jnp.zeros(
                        (128, length - extent), BF
                    )

            def back_turn(w, c, s):
                first, second = w[:HALF], w[HALF:]
                return jnp.concatenate(
                    [first * c + second * s, second * c - first * s], axis=0
                ).astype(BF)

            for h in range(4):
                at = slice(h * HEAD, (h + 1) * HEAD)
                row = start + h * HEAD
                query, key = q_ref[0, at], k_ref[0, at, 0:extent]
                exponent = exp_ref[0, h, 0:extent]
                inverse = inv_ref[0, 0, h : h + 1]
                grad_mixed = (gmix_ref[0, at].astype(F32) * inverse).astype(BF)
                inner = jnp.sum(
                    raw_ref[0, at] * grad_mixed.astype(F32), axis=0, keepdims=True
                )
                grad_probs = dot_tn(v_ref[0, at, 0:extent], grad_mixed)
                grad_scores = (exponent.astype(F32) * (grad_probs - inner)).astype(BF)
                grad_value = dot_nt(grad_mixed, exponent)
                grad_key = dot_nt(query, grad_scores)
                grad_query = dot_nn(key, grad_scores) * scale
                g_t[pl.ds(row, HEAD), :] = back_turn(grad_query, cosine, sine)
                g_t[pl.ds(row + D, HEAD), 0:extent] = back_turn(
                    grad_key, cosine[:, 0:extent], sine[:, 0:extent]
                )
                g_t[pl.ds(row + 2 * D, HEAD), 0:extent] = grad_value.astype(BF)

        low_edge = extent

    @pl.when(group == pl.num_programs(1) - 1)
    def _():
        whitened, inverse = whiten(x_ref[0].astype(F32))
        gain = rows_ref[0:1, :]
        hidden = (whitened * gain + rows_ref[2:3, :]).astype(BF)
        hidden_t = hidden.T
        grads = g_t[...]
        ones = jnp.ones((8, length), BF)
        grad_hidden = dot_tn(grads, w_t[...])
        for j in range(3):
            part = grads[j * D : (j + 1) * D]
            small_ref[2 + j : 3 + j, :] += dot_nt(ones, part)[0:1]
            gw_ref[pl.ds(j * D, D), :] += dot_nt(hidden_t, part)
        small_ref[0:1, :] += jnp.sum(grad_hidden * whitened, axis=0, keepdims=True)
        small_ref[1:2, :] += jnp.sum(grad_hidden, axis=0, keepdims=True)
        gx_ref[0] = gmid_ref[0] + whiten_back(grad_hidden, whitened, inverse, gain)


def feed_forward(
    layers,
    x_ref, mix_ref, wo_ref, rows_ref, cot_ref, u_ref, v_ref, fbias_ref,
    head_ref, label_ref, live_ref,
    out_ref, gmid_ref, gmix_ref, gffn_ref, gfb_ref, gwo_ref, small_ref, late_ref,
    middle, hidden, cot, down, grad_hidden, act_low, grad_low, x_buf, mix_buf, cot_buf,
    copied, *comm,
):
    seqs, length = x_ref.shape[0], x_ref.shape[1]
    pad = hidden.shape[0] // seqs
    step = pl.program_id(0)
    last = pl.num_programs(0) - 1
    chunk = act_low.shape[1]

    def moves(pairs, first):
        return [
            [
                pltpu.make_async_copy(a.at[s], b.at[s], copied.at[first + i, s])
                for i, (a, b) in enumerate(pairs)
            ]
            for s in range(seqs)
        ]

    arrivals = moves(((mix_ref, mix_buf), (x_ref, x_buf), (cot_ref, cot_buf)), 0)
    leavings = moves(((mix_buf, gmix_ref), (x_buf, out_ref), (middle, gmid_ref)), 3)
    if layers:
        me = position()
        terms, weights, w_send, w_recv, w_local = comm[:5]
        comm = comm[5:]
        spot = (me["z"], me["x"], me["y"], me["c"])
        chunks = weights.shape[1]
        late = range(EARLY, chunks)
        loads = [
            pltpu.make_async_copy(u_ref.at[j], weights.at[j, 0:EARLY], w_local.at[j])
            for j in range(2)
        ]
        own = [
            pltpu.make_async_copy(
                v_ref.at[j, k * ROWS : (k + 1) * ROWS], weights.at[(j, k) + spot],
                w_local.at[2 + j * chunks + k],
            )
            for j in range(2)
            for k in late
        ]
        gathers = {
            k: [
                PieceGather(
                    me, layers, weights.at[j, k], (), w_send.at[k, j], w_recv.at[k, j], "xy"[j]
                )
                for j in range(2)
            ]
            for k in late
        }

        def gather(stage, *which):
            for k in which:
                for piece in gathers[k]:
                    if stage < 4:
                        piece.advance(stage)
                    else:
                        piece.wait(3)

        farewell = [
            pltpu.make_async_copy(terms.at[j], late_ref.at[j], w_local.at[j]) for j in range(2)
        ]

        def pieces(k):
            slot = lax.rem(k, 2) * 2
            return [PieceReduce(me, layers, comm, slot + j, "yx"[j]) for j in range(2)]

        def getter(j):
            def get(layer, rest, core):
                at = ((layer * 4 + rest) * 2 + core) * ROWS
                return terms[j, pl.ds(pl.multiple_of(at, ROWS), ROWS), :]

            return get

        def over_first(k):
            for j, op in enumerate(pieces(k)):
                op.over_first(getter(j))

        def over_second(k):
            for op in pieces(k):
                op.over_second()

        def over_layers(k):
            for op in pieces(k):
                op.over_layers()

        def finish(k):
            rows = pl.ds(pl.multiple_of(k * ROWS, ROWS), ROWS)
            for j, op in enumerate(pieces(k)):
                gffn_ref[j, rows, :] = op.finish()

    def later(stage, delay):
        if layers:
            pl.when(step >= delay)(lambda: stage(step - delay))

    def at_step(k, *args):
        if layers:
            pl.when(step == k)(functools.partial(gather, *args))

    @pl.when(step == 0)
    def _():
        for s in range(seqs):
            for copy in arrivals[s]:
                copy.start()
        if layers:
            greet(me, layers)
            for copy in own + loads:
                copy.start()
            for copy in own:
                copy.wait()
            meet(layers)
            for k in late:
                for piece in gathers[k]:
                    piece.start(0)
        blank = jnp.zeros((pad - length, D), BF)
        for s in range(seqs):
            for copy in arrivals[s]:
                copy.wait()
            branch = dot_tn(mix_buf[s], matrix(wo_ref, 0)) + rows_ref[7:8, :]
            mid = x_buf[s].astype(F32) + branch
            middle[s] = mid
            whitened, _ = whiten(mid)
            low = (whitened * rows_ref[1:2, :] + rows_ref[3:4, :]).astype(BF)
            hidden[pl.ds(s * pad, pad), :] = jnp.concatenate([low, blank], axis=0)
            cot[pl.ds(s * pad, pad), :] = jnp.concatenate([cot_buf[s], blank], axis=0)
            if layers and s == 1:
                gather(1, 2)
        down[...] = jnp.zeros_like(down)
        grad_hidden[...] = jnp.zeros_like(grad_hidden)
        gfb_ref[...] = jnp.zeros_like(gfb_ref)
        if layers:
            for copy in loads:
                copy.wait()
            gather(1, 3)

    if layers:
        up_w = weights[0, step].reshape(chunk, D)
        down_w = weights[1, step].reshape(chunk, D)
    else:
        up_w, down_w = u_ref[0], v_ref[0]
    fbias = fbias_ref[0]
    total = jnp.zeros_like(fbias)
    def lifted(s):
        rows = pl.ds(s * pad, pad)
        return dot_nt(hidden[rows, :], up_w) + fbias, dot_nt(cot[rows, :], down_w)

    ahead = lifted(0)
    for s in range(seqs):
        rows = pl.ds(s * pad, pad)
        upward, grad_act = ahead
        if s + 1 < seqs:
            ahead = lifted(s + 1)
        phi = 0.5 * (1.0 + lax.erf(upward * ROOT_HALF))
        act = (upward * phi).astype(BF)
        slope = phi + upward * jnp.exp(-0.5 * upward * upward) * INV_ROOT_TWO_PI
        grad_up = (grad_act * slope).astype(BF)
        act_low[rows, :] = act
        grad_low[rows, :] = grad_up
        total += jnp.sum(grad_up.astype(F32), axis=0, keepdims=True)
        down[rows, :] += dot_nn(act, down_w)
        grad_hidden[rows, :] += dot_nn(grad_up, up_w)
        if layers and s == 1:
            at_step(0, 2, 2)
            at_step(0, 1, 4)
            at_step(1, 4, 2)
            at_step(2, 4, 3, 4)
            later(over_first, 1)
            later(over_layers, 2)
    gfb_ref[step, :, 0:chunk] = total
    grad_u = dot_tn(grad_low[...], hidden[...])
    if layers:
        terms[0] = grad_u
        terms[1] = dot_tn(act_low[...], cot[...])

        @pl.when(step < last)
        def _():
            for j, op in enumerate(pieces(step)):
                op.over_cores(getter(j))

        @pl.when(step == last)
        def _():
            for copy in farewell:
                copy.start()

        at_step(0, 3, 2)
        at_step(0, 2, 3, 4)
        at_step(1, 3, 3, 4)
        later(over_second, 1)
        later(finish, 2)
    else:
        gffn_ref[0, 0] = grad_u
        gffn_ref[1, 0] = dot_tn(act_low[...], cot[...])

    @pl.when(step == last)
    def _():
        gain = rows_ref[1:2, :]
        gain_sum = jnp.zeros((1, D), F32)
        shift_sum = jnp.zeros((1, D), F32)
        branch_sum = jnp.zeros((1, D), F32)
        cot_sum = jnp.zeros((1, D), F32)
        loglik = jnp.zeros((1, length), F32)
        hits = jnp.zeros((1, length), F32)
        gwo_ref[...] = jnp.zeros_like(gwo_ref)
        for s in range(seqs):
            rows = pl.ds(s * pad, length)
            mid = middle[s]
            final = mid + (down[rows, :] + rows_ref[8:9, :])
            x_buf[s] = final.astype(BF)
            leavings[s][1].start()
            unit, _ = whiten(final)
            logits = dot_nt(head_ref[...], unit.astype(BF))
            slot = lax.broadcasted_iota(jnp.int32, logits.shape, 0)
            logits = jnp.where(slot < VOCAB, logits, -1e30)
            shifted = logits - jnp.max(logits, axis=0, keepdims=True)
            logprob = shifted - jnp.log(jnp.sum(jnp.exp(shifted), axis=0, keepdims=True))
            picked = jnp.sum(
                jnp.where(slot == label_ref[s : s + 1, :], logprob, 0.0), axis=0, keepdims=True
            )
            live = live_ref[s : s + 1, :] != 0
            loglik += jnp.where(live, picked, 0.0)
            hits += jnp.where(live, jnp.exp(picked), 0.0)

            gradient = grad_hidden[rows, :]
            whitened, inverse = whiten(mid)
            gain_sum += jnp.sum(gradient * whitened, axis=0, keepdims=True)
            shift_sum += jnp.sum(gradient, axis=0, keepdims=True)
            own = cot_buf[s].astype(F32)
            cot_sum += jnp.sum(own, axis=0, keepdims=True)
            grad_mid = own + whiten_back(gradient, whitened, inverse, gain)
            middle[s] = grad_mid
            leavings[s][2].start()
            low = grad_mid.astype(BF)
            branch_sum += jnp.sum(low.astype(F32), axis=0, keepdims=True)
            gwo_ref[...] += dot_nn(mix_buf[s], low)
            mix_buf[s] = dot_nt(matrix(wo_ref, 0), low).astype(BF)
            leavings[s][0].start()
            if layers:
                if s == 0:
                    over_layers(last - 1)
                if s == seqs - 1:
                    finish(last - 1)
        small_ref[0:1, :] = gain_sum
        small_ref[1:2, :] = shift_sum
        small_ref[2:3, :] = branch_sum
        small_ref[3:4, :] = cot_sum
        small_ref[4:8, :] = jnp.zeros((4, D), F32)
        small_ref[4:5, 0:128] = jnp.broadcast_to(
            jnp.sum(loglik, axis=1, keepdims=True), (1, 128)
        )
        small_ref[4:5, 128:256] = jnp.broadcast_to(
            jnp.sum(hits, axis=1, keepdims=True), (1, 128)
        )
        for s in range(seqs):
            for copy in leavings[s]:
                copy.wait()
        if layers:
            for copy in farewell:
                copy.wait()


def whole(shape):
    return pl.BlockSpec(shape, lambda *_: (0,) * len(shape), pipeline_mode=pl.Buffered(1))


def block_of(shape, *index):
    return pl.BlockSpec(shape, lambda *_: index, pipeline_mode=pl.Buffered(1))


def leading(shape):
    return pl.BlockSpec((1,) + tuple(shape[1:]), lambda i, *_: (i,) + (0,) * (len(shape) - 1))


def shaped(shape, dtype=F32):
    return jax.ShapeDtypeStruct(shape, dtype)


def projections(attn, first, count):
    blocks = attn.shape[0] // 4
    rows = D // blocks
    return block_of((blocks * count, rows, D), first // count, 0, 0)


def attention_forward(lengths, tokens, rows_all, attn, ffn, cosine, sine, layers):
    seqs, length, _ = tokens.shape
    heads = HEADS // 4
    flat = (seqs, D, length)
    inverse = (seqs, heads, 4, length)
    exponent = (seqs, HEADS, length, length)

    def part(block):
        return pl.BlockSpec(block, lambda g, s, *_: (s, g, 0, 0)[: len(block)])

    out_specs = [part((1, 128, length))] * 5
    out_specs += [part((1, 1, 4, length)), part((1, 4, length, length))]
    out_shape = [shaped(flat, BF)] * 4 + [shaped(flat), shaped(inverse), shaped(exponent, BF)]
    scratch = [
        pltpu.VMEM((seqs, length, D), BF), pltpu.VMEM((384, D), BF), pltpu.VMEM((D, 16), F32),
        pltpu.VMEM((seqs, length, D), F32),
    ]
    hbm = pl.BlockSpec(memory_space=pl.ANY)
    params = dict(vmem_limit_bytes=VMEM_LIMIT)
    if layers:
        chips = (layers, 2, 2, 2)
        owned = attn.shape[0]
        early = (2, EARLY) + chips + (ROWS, D)
        out_specs += [whole((16, D)), hbm, hbm]
        out_shape += [
            shaped((16, D)), shaped(chips + (owned, D), BF),
            shaped(early, BF),
        ]
        scratch += [
            pltpu.VMEM(chips + (owned + 16, D), BF), pltpu.VMEM(early, BF),
            pltpu.SemaphoreType.DMA((10, 2 + layers)), pltpu.SemaphoreType.DMA((10, 2 + layers)),
            pltpu.SemaphoreType.DMA((3 + 2 * EARLY,)),
        ]
        params.update(collective_id=2, has_side_effects=True)
        sources = [hbm, hbm, hbm]
    else:
        sources = [whole(rows_all.shape), whole(attn.shape), hbm]
    return pl.pallas_call(
        functools.partial(forward_attention, layers),
        grid_spec=pltpu.PrefetchScalarGridSpec(
            num_scalar_prefetch=1,
            grid=(heads, seqs),
            in_specs=[whole(tokens.shape)] + sources + [whole(cosine.shape), whole(sine.shape)],
            out_specs=out_specs,
            scratch_shapes=scratch,
        ),
        out_shape=out_shape,
        compiler_params=pltpu.CompilerParams(**params),
        name="attention_forward",
    )(lengths, tokens, rows_all, attn, ffn, cosine, sine)


def attention_backward(
    lengths, tokens, attn, rows_all, cosine, sine, query, key, value, grad_mixed, raw,
    inverse, exponent, grad_middle,
):
    seqs, length, _ = tokens.shape

    def part(block):
        return pl.BlockSpec(block, lambda s, g, *_: (s, g, 0, 0)[: len(block)])

    return pl.pallas_call(
        backward_attention,
        grid_spec=pltpu.PrefetchScalarGridSpec(
            num_scalar_prefetch=1,
            grid=(seqs, HEADS // 4),
            in_specs=[
                leading(tokens.shape), projections(attn, 0, 3), whole(rows_all.shape),
                whole(cosine.shape), whole(sine.shape),
            ]
            + [part((1, 128, length))] * 5
            + [part((1, 1, 4, length)), part((1, 4, length, length)), leading(tokens.shape)],
            out_specs=[leading(tokens.shape), whole((3 * D, D)), whole((8, D))],
            scratch_shapes=[pltpu.VMEM((3 * D, D), BF), pltpu.VMEM((3 * D, length), BF)],
        ),
        out_shape=[shaped(tokens.shape), shaped((3 * D, D)), shaped((8, D))],
        compiler_params=pltpu.CompilerParams(vmem_limit_bytes=VMEM_LIMIT),
        name="attention_backward",
    )(
        lengths, tokens, attn, rows_all, cosine, sine, query, key, value, grad_mixed, raw,
        inverse, exponent, grad_middle,
    )


def feed_forward_both(
    tokens, mixed, attn, rows_all, cotangent, ffn, fbias, head_t, labels, live, layers,
):
    seqs, length, _ = tokens.shape
    pad = (length + 15) // 16 * 16
    rows = seqs * pad
    steps, chunk = fbias.shape
    hbm = pl.BlockSpec(memory_space=pl.ANY)
    if layers:
        ups, downs = ffn
        up_spec = down_spec = hbm
        owned = downs.shape[1]
        grad_spec, grad_shape = whole((2, owned - ROWS, D)), shaped((2, owned - ROWS, D))
        late_shape = (2, chunk, D)
        chips = (layers, 2, 2, 2)
        extra = [
            pltpu.VMEM(late_shape, F32), pltpu.VMEM((2, steps) + chips + (ROWS, D), BF),
            pltpu.SemaphoreType.DMA((steps, 2, 2 + layers)),
            pltpu.SemaphoreType.DMA((steps, 2, 2 + layers)),
            pltpu.SemaphoreType.DMA((2 + 2 * steps,)),
        ]
        extra += reduce_scratch(4, layers)
    else:
        chunked = (steps, chunk, D)
        ups, downs = ffn[0].reshape(chunked), ffn[1].reshape(chunked)
        up_spec = down_spec = leading(chunked)
        grad_spec = pl.BlockSpec((2, 1, chunk, D), lambda k: (0, k, 0, 0))
        grad_shape = shaped((2,) + chunked)
        late_shape = (8, 128)
        extra = []
    return pl.pallas_call(
        functools.partial(feed_forward, layers),
        grid=(steps,),
        in_specs=[
            hbm, hbm, projections(attn, 3, 1), whole(rows_all.shape), hbm, up_spec, down_spec,
            leading((steps, 1, chunk)), whole(head_t.shape), whole(labels.shape),
            whole(live.shape),
        ],
        out_specs=[
            hbm, hbm, hbm, grad_spec, whole((8, 1, D)), whole((D, D)), whole((8, D)), hbm,
        ],
        out_shape=[
            shaped(tokens.shape, BF), shaped(tokens.shape), shaped(mixed.shape, BF),
            grad_shape, shaped((8, 1, D)), shaped((D, D)), shaped((8, D)), shaped(late_shape),
        ],
        scratch_shapes=[
            pltpu.VMEM(tokens.shape, F32),
            pltpu.VMEM((rows, D), BF),
            pltpu.VMEM((rows, D), BF),
            pltpu.VMEM((rows, D), F32),
            pltpu.VMEM((rows, D), F32),
            pltpu.VMEM((rows, chunk), BF),
            pltpu.VMEM((rows, chunk), BF),
            pltpu.VMEM(tokens.shape, BF),
            pltpu.VMEM(mixed.shape, BF),
            pltpu.VMEM(tokens.shape, BF),
            pltpu.SemaphoreType.DMA((6, seqs)),
        ]
        + extra,
        compiler_params=pltpu.CompilerParams(
            vmem_limit_bytes=VMEM_LIMIT, **(dict(collective_id=0, has_side_effects=True) if layers else {})
        ),
        name="feed_forward",
    )(
        tokens, mixed, attn, rows_all, cotangent, ups, downs,
        fbias.reshape(steps, 1, chunk), head_t, labels, live,
    )


def reduce_tail(grad_qkv, grad_wo, late, part, small_one, small_two, units, layers):
    owned = grad_wo.shape[1]
    pieces = 2 + owned // ROWS
    devices = grad_qkv.shape[0] + grad_wo.shape[0]
    hbm, vmem = pl.BlockSpec(memory_space=pl.ANY), pl.BlockSpec(memory_space=pltpu.VMEM)
    return pl.pallas_call(
        functools.partial(gradient_tail, layers),
        in_specs=[hbm] * 3 + [vmem] * 4,
        out_specs=[vmem] * 3,
        out_shape=[shaped((owned, D)), shaped((2, owned, D)), shaped((24, D))],
        scratch_shapes=[
            pltpu.VMEM((pieces, devices, ROWS, D), F32),
            pltpu.SemaphoreType.DMA((pieces, 2)),
            pltpu.VMEM((4, 24, D), F32),
            pltpu.VMEM((3 + layers, 24, D), F32),
            pltpu.SemaphoreType.DMA((2 + layers,)),
            pltpu.SemaphoreType.DMA((2 + layers,)),
        ]
        + reduce_scratch(pieces, layers),
        compiler_params=pltpu.CompilerParams(
            vmem_limit_bytes=VMEM_LIMIT, collective_id=1, has_side_effects=True
        ),
        name="gradient_tail",
    )(grad_qkv, grad_wo, late.reshape(2, devices, ROWS, D), part, small_one, small_two, units)


def per_device(
    tokens, lengths, masked_flags, labels, attn_weights, ffn_weights, ffn_bias, norm_gains,
    biases, head_weight, cotangent,
):
    both = ("wide", "narrow")
    seqs, length, _ = tokens.shape
    wide, narrow = lax.axis_size("wide"), lax.axis_size("narrow")
    devices = wide * narrow
    shard, units = D // wide, ffn_bias.shape[0]
    owned = attn_weights.shape[0]
    layers = 4 if (wide, narrow) == (8, 4) and owned == units and owned % ROWS == 0 else 0
    at = lax.axis_index("wide")
    owner = at * narrow + lax.axis_index("narrow")
    first = (lax.axis_index("narrow") == 0).astype(BF)
    own = jnp.concatenate([norm_gains, biases], axis=0) * first
    rows_own = lax.dynamic_update_slice(jnp.zeros((16, D), BF), own, (0, at * shard))
    flat = lax.dynamic_update_slice(jnp.zeros((4 * D,), BF), ffn_bias, (owner * units,))
    rows_own = rows_own + jnp.pad(flat.reshape(4, D), ((9, 3), (0, 0)))
    cosine, sine = rotary_tables(length)
    if layers:
        rows_all, attn, ffn = rows_own, attn_weights, ffn_weights
    else:
        attn = lax.all_gather(attn_weights, both, axis=0, tiled=True).reshape(4, D, D)
        ffn = lax.all_gather(ffn_weights, both, axis=1, tiled=True)
        rows_all = lax.psum(rows_own.astype(F32), both)
    query, key, value, mixed, raw, inverse, exponent, *gathered = attention_forward(
        lengths, tokens, rows_all, attn, ffn, cosine, sine, layers
    )
    if layers:
        rows_all, attn, ffn = gathered
        attn = attn.reshape(devices, owned, D)
        ffn = (ffn, ffn_weights)
        unit_bias = rows_all[9:13].reshape(devices, units // ROWS, ROWS).transpose(1, 0, 2)
        unit_bias = unit_bias.reshape(units // ROWS, devices * ROWS)
    else:
        unit_bias = rows_all[9:13].reshape(-1, 512)
    live = (masked_flags == 1) & (jnp.arange(length)[None, :] < lengths[:, None])
    head_t = jnp.pad(head_weight.T, ((0, 7), (0, 0)))
    (
        output, grad_middle, grad_mixed, grad_ffn, unit_sums, grad_wo, small_two, late,
    ) = feed_forward_both(
        tokens, mixed, attn, rows_all, cotangent, ffn, unit_bias, head_t, labels,
        live.astype(jnp.int32), layers,
    )
    if not layers:
        grad_ffn = lax.psum_scatter(
            grad_ffn.reshape(2, -1, D), both, scatter_dimension=1, tiled=True
        )
    grad_tokens, grad_qkv, small_one = attention_backward(
        lengths, tokens, attn, rows_all, cosine, sine, query, key, value, grad_mixed, raw,
        inverse, exponent, grad_middle,
    )
    steps, chunk = unit_bias.shape
    if layers:
        blocks = (-1, owned, D)
        grad_attn, grad_ffn, sums = reduce_tail(
            grad_qkv.reshape(blocks), grad_wo.reshape(blocks), late, grad_ffn, small_one,
            small_two, unit_sums, layers,
        )
        grad_ffn_bias = lax.dynamic_slice(
            sums, (16, owner * ROWS), (steps, ROWS)
        ).reshape(units)
    else:
        grad_attn = lax.psum_scatter(
            jnp.concatenate([grad_qkv, grad_wo], axis=0), both, scatter_dimension=0, tiled=True
        )
        sums = jnp.concatenate(
            [
                small_one[0:1], small_two[0:1], small_one[1:2], small_two[1:2], small_one[2:5],
                small_two[2:5], jnp.zeros((6, D), F32), unit_sums[:, 0],
            ],
            axis=0,
        )
        sums = lax.psum(sums, both)
        grad_ffn_bias = lax.dynamic_slice_in_dim(
            sums[16:, :chunk].reshape(-1), owner * units, units, 0
        )
    grad_gains = lax.dynamic_slice(sums, (0, at * shard), (2, shard))
    grad_biases = lax.dynamic_slice(sums, (2, at * shard), (7, shard))
    head_stats = (
        sums[9, 0:256:128] * jnp.array([1.0, VOCAB], F32) / (seqs * length * devices)
    )
    return (
        output, grad_tokens, grad_attn, grad_ffn, grad_ffn_bias, grad_gains, grad_biases,
        head_stats,
    )


def solution(mesh):
    both = ("wide", "narrow")
    return jax.shard_map(
        per_device,
        mesh=mesh,
        in_specs=(
            P(both, None, None),
            P(both),
            P(both, None),
            P(both, None),
            P(both, None),
            P(None, both, None),
            P(both),
            P(None, "wide"),
            P(None, "wide"),
            P(),
            P(both, None, None),
        ),
        out_specs=(
            P(both, None, None),
            P(both, None, None),
            P(both, None),
            P(None, both, None),
            P(both),
            P(None, "wide"),
            P(None, "wide"),
            P(),
        ),
        check_vma=False,
    )
```

```python
import functools
import math

import jax
import jax.numpy as jnp
import numpy as np
from jax import lax
from jax.experimental import pallas as pl
from jax.experimental.pallas import tpu as pltpu
from jax.sharding import PartitionSpec as P

D = 640
HEADS = 20
HEAD = 32
HALF = HEAD // 2
VOCAB = 33
EPS = 1e-05
ROOT_HALF = 0.7071067811865476
INV_ROOT_TWO_PI = 0.3989422804014327
BF = jnp.bfloat16
F32 = jnp.float32
VMEM_LIMIT = 60 << 20

MESH = pl.DeviceIdType.MESH
ROWS = 16


def position():
    wide, narrow = lax.axis_index("wide"), lax.axis_index("narrow")
    return {
        "z": lax.div(wide, 2), "x": lax.rem(wide, 2),
        "y": lax.div(narrow, 2), "c": lax.rem(narrow, 2),
    }


def partner(me, axis, offset, size):
    there = dict(me)
    there[axis] = lax.rem(me[axis] + offset, size)
    return (there["z"] * 2 + there["x"], there["y"] * 2 + there["c"])


def across(me):
    return partner({**me, "x": 1 - me["x"]}, "y", 1, 2)


def greet(me, layers, corner=False):
    barrier = pltpu.get_barrier_semaphore()
    peers = [partner(me, axis, 1, 2) for axis in "cyx"]
    peers += [partner(me, "z", offset, layers) for offset in range(1, layers)]
    if corner:
        peers.append(across(me))
    for peer in peers:
        pl.semaphore_signal(barrier, inc=1, device_id=peer, device_id_type=MESH)


def meet(layers, corner=False):
    pl.semaphore_wait(pltpu.get_barrier_semaphore(), 2 + layers + corner)


def reduce_scratch(slots, layers):
    def blocks(count, dtype):
        return pltpu.VMEM((slots, count, ROWS, D), dtype)

    return [
        blocks(4 * layers, BF), blocks(4 * layers, BF),
        blocks(2 * layers, BF), blocks(2 * layers, BF), blocks(2 * layers, F32),
        blocks(layers, BF), blocks(layers, BF), blocks(layers, F32),
        blocks(layers, BF), blocks(layers, BF), blocks(1, F32),
        pltpu.SemaphoreType.DMA((slots, 3 + layers)),
        pltpu.SemaphoreType.DMA((slots, 3 + layers)),
    ]


class PieceReduce:
    def __init__(self, me, layers, refs, slot, first):
        (
            self.s0, self.r0, self.s1, self.r1, self.k1, self.s2, self.r2, self.k2,
            self.s3, self.r3, self.k3,
        ) = (ref.at[slot] for ref in refs[:11])
        self.send, self.recv = (ref.at[slot] for ref in refs[11:])
        self.me, self.layers = me, layers
        self.first, self.second = ("y", "x") if first == "y" else ("x", "y")

    def exchange(self, stage, source, target, axis):
        return pltpu.make_async_remote_copy(
            src_ref=source, dst_ref=target, send_sem=self.send.at[stage],
            recv_sem=self.recv.at[stage], device_id=partner(self.me, axis, 1, 2),
            device_id_type=MESH,
        )

    def layer_copies(self):
        me, layers = self.me, self.layers
        return [
            pltpu.make_async_remote_copy(
                src_ref=self.s3.at[lax.rem(me["z"] + offset, layers)],
                dst_ref=self.r3.at[offset], send_sem=self.send.at[2 + offset],
                recv_sem=self.recv.at[2 + offset],
                device_id=partner(me, "z", offset, layers), device_id_type=MESH,
            )
            for offset in range(1, layers)
        ]

    def rest(self, along, other):
        return other * 2 + along if self.first == "y" else along * 2 + other

    def over_cores(self, get):
        core = self.me["c"]

        @pl.loop(0, 4 * self.layers)
        def _(i):
            self.s0[i] = get(i, 1 - core).astype(BF)

        self.exchange(0, self.s0, self.r0, "c").start()

    def over_first(self, get):
        self.exchange(0, self.s0, self.r0, "c").wait()
        core, along = self.me["c"], self.me[self.first]

        @pl.loop(0, self.layers)
        def _(layer):
            for other in range(2):
                away = layer * 4 + self.rest(1 - along, other)
                near = layer * 4 + self.rest(along, other)
                at = layer * 2 + other
                self.s1[at] = (get(away, core) + self.r0[away].astype(F32)).astype(BF)
                self.k1[at] = get(near, core) + self.r0[near].astype(F32)

        self.exchange(1, self.s1, self.r1, self.first).start()

    def over_second(self):
        self.exchange(1, self.s1, self.r1, self.first).wait()
        along = self.me[self.second]

        @pl.loop(0, self.layers)
        def _(layer):
            away, near = layer * 2 + (1 - along), layer * 2 + along
            self.s2[layer] = (self.k1[away] + self.r1[away].astype(F32)).astype(BF)
            self.k2[layer] = self.k1[near] + self.r1[near].astype(F32)

        self.exchange(2, self.s2, self.r2, self.second).start()

    def over_layers(self):
        self.exchange(2, self.s2, self.r2, self.second).wait()
        own = self.me["z"]

        @pl.loop(0, self.layers)
        def _(layer):
            self.s3[layer] = (self.k2[layer] + self.r2[layer].astype(F32)).astype(BF)

        self.k3[0] = self.k2[own] + self.r2[own].astype(F32)
        for copy in self.layer_copies():
            copy.start()

    def finish(self):
        for copy in self.layer_copies():
            copy.wait()
        total = self.k3[0]
        for offset in range(1, self.layers):
            total = total + self.r3[offset].astype(F32)
        return total


class PieceGather:
    def __init__(self, me, layers, buf, tail, send, recv, first):
        self.me, self.layers, self.buf, self.tail = me, layers, buf, tail
        self.send, self.recv, self.first = send, recv, first

    def view(self, *lead):
        return self.buf.at[lead + self.tail]

    def copy(self, lead, peer, at):
        return pltpu.make_async_remote_copy(
            src_ref=self.view(*lead), dst_ref=self.view(*lead), send_sem=self.send.at[at],
            recv_sem=self.recv.at[at], device_id=peer, device_id_type=MESH,
        )

    def copies(self, stage):
        me, every = self.me, slice(None)
        z, x, y, core = me["z"], me["x"], me["y"], me["c"]
        if stage == 0:
            return [
                self.copy((z, x, y, core), partner(me, "z", offset, self.layers), 2 + offset)
                for offset in range(1, self.layers)
            ]
        if self.first == "xy" and stage < 3:
            if stage == 2:
                return []
            peers = partner(me, "x", 1, 2), partner(me, "y", 1, 2), across(me)
            return [
                self.copy((every, x, y, core), peer, at)
                for peer, at in zip(peers, (0, 1, 2 + self.layers))
            ]
        if stage == 1:
            lead, axis = (every, x, y, core), self.first
        elif stage == 2:
            lead = (every, every, y, core) if self.first == "x" else (every, x, every, core)
            axis = "y" if self.first == "x" else "x"
        else:
            lead, axis = (every, every, every, core), "c"
        return [self.copy(lead, partner(me, axis, 1, 2), stage - 1)]

    def start(self, stage):
        for copy in self.copies(stage):
            copy.start()

    def wait(self, stage):
        for copy in self.copies(stage):
            copy.wait()

    def advance(self, stage):
        self.wait(stage - 1)
        self.start(stage)


class SmallReduce:
    def __init__(self, me, layers, sent, got, send, recv):
        self.me, self.layers = me, layers
        self.sent, self.got, self.send, self.recv = sent, got, send, recv

    def exchange(self, stage):
        return pltpu.make_async_remote_copy(
            src_ref=self.sent.at[stage], dst_ref=self.got.at[stage],
            send_sem=self.send.at[stage], recv_sem=self.recv.at[stage],
            device_id=partner(self.me, "cyx"[stage], 1, 2), device_id_type=MESH,
        )

    def layer_copies(self):
        own = self.me["z"]
        return [
            pltpu.make_async_remote_copy(
                src_ref=self.sent.at[3], dst_ref=self.got.at[3 + own],
                send_sem=self.send.at[2 + offset], recv_sem=self.recv.at[2 + offset],
                device_id=partner(self.me, "z", offset, self.layers), device_id_type=MESH,
            )
            for offset in range(1, self.layers)
        ]

    def start(self, stage):
        if stage:
            self.exchange(stage - 1).wait()
            self.sent[stage] = self.sent[stage - 1] + self.got[stage - 1]
        if stage < 3:
            self.exchange(stage).start()
        else:
            for copy in self.layer_copies():
                copy.start()
            self.got[3 + self.me["z"]] = self.sent[3]

    def finish(self):
        for copy in self.layer_copies():
            copy.wait()
        total = self.got[3]
        for layer in range(1, self.layers):
            total = total + self.got[3 + layer]
        return total


TAIL_ORDER = (
    (0, 0), (1, 0), (2, 0), (7, 0), (3, 0), (4, 0), (0, 1), (1, 1), (7, 1), (5, 0), (6, 0),
    (2, 1), (3, 1), (4, 1), (5, 1), (7, 2), (6, 1), (0, 2), (1, 2), (2, 2), (3, 2), (7, 3),
    (4, 2), (0, 3), (1, 3), (5, 2), (6, 2), (2, 3), (3, 3), (4, 3), (0, 4), (1, 4), (7, 4),
    (5, 3), (6, 3), (2, 4), (3, 4), (4, 4), (5, 4), (6, 4),
)


def gradient_tail(layers, qkv_ref, wo_ref, late_ref, part_ref, one_ref, two_ref, units_ref,
                  grad_ref, gffn_ref, sums_ref, terms, loaded, sent, got, small_send,
                  small_recv, *refs):
    me = position()
    greet(me, layers)
    own, wo = qkv_ref.shape[0], wo_ref.shape[0]
    loads = []
    for p in range(terms.shape[0]):
        if p < 2:
            moves = [(late_ref.at[p], terms.at[p])]
        else:
            rows = slice((p - 2) * ROWS, (p - 1) * ROWS)
            moves = [
                (qkv_ref.at[:, rows], terms.at[p, 0:own]),
                (wo_ref.at[:, rows], terms.at[p, own : own + wo]),
            ]
        loads.append(
            [
                pltpu.make_async_copy(source, target, loaded.at[p, i])
                for i, (source, target) in enumerate(moves)
            ]
        )
        for copy in loads[-1]:
            copy.start()
    order = [(one_ref, 0), (two_ref, 0), (one_ref, 1), (two_ref, 1)]
    order += [(one_ref, 2), (one_ref, 3), (one_ref, 4), (two_ref, 2), (two_ref, 3), (two_ref, 4)]
    sent[0, 8:16] = jnp.zeros((8, D), F32)
    for row, (ref, at) in enumerate(order):
        sent[0, row : row + 1] = ref[at : at + 1]
    for k in range(8):
        sent[0, 16 + k : 17 + k] = units_ref[k]
    small = SmallReduce(me, layers, sent, got, small_send, small_recv)
    ops = [PieceReduce(me, layers, refs, p, "yx"[p % 2]) for p in range(terms.shape[0])]
    kept = part_ref.shape[1]
    gffn_ref[:, 0:kept] = part_ref[...]
    meet(layers)

    def getter(p):
        return lambda i, core: terms[p, i * 2 + core]

    for p, stage in TAIL_ORDER:
        if p == len(ops):
            if stage < 4:
                small.start(stage)
            else:
                sums_ref[...] = small.finish()
        elif stage == 0:
            for copy in loads[p]:
                copy.wait()
            ops[p].over_cores(getter(p))
        elif stage == 1:
            ops[p].over_first(getter(p))
        elif stage == 2:
            ops[p].over_second()
        elif stage == 3:
            ops[p].over_layers()
        elif p < 2:
            gffn_ref[p, kept:] = ops[p].finish()
        else:
            grad_ref[(p - 2) * ROWS : (p - 1) * ROWS] = ops[p].finish()


def dot_nn(a, b):
    return lax.dot_general(a, b, (((1,), (0,)), ((), ())), preferred_element_type=F32)


def dot_nt(a, b):
    return lax.dot_general(a, b, (((1,), (1,)), ((), ())), preferred_element_type=F32)


def dot_tn(a, b):
    return lax.dot_general(a, b, (((0,), (0,)), ((), ())), preferred_element_type=F32)


def matrix(ref, j):
    rows = ref.shape[1]
    blocks = D // rows
    return ref[j * blocks : (j + 1) * blocks].reshape(D, D)


def whiten(values):
    center = jnp.mean(values, axis=-1, keepdims=True)
    offset = values - center
    spread = jnp.mean(offset * offset, axis=-1, keepdims=True)
    inverse = lax.rsqrt(spread + EPS)
    return offset * inverse, inverse


def whiten_back(gradient, whitened, inverse, gain):
    scaled = gradient * gain
    mean_grad = jnp.mean(scaled, axis=-1, keepdims=True)
    mean_cross = jnp.mean(scaled * whitened, axis=-1, keepdims=True)
    return inverse * (scaled - mean_grad - whitened * mean_cross)


def rotary_tables(length):
    frequency = (
        np.float32(1.0)
        / np.float32(10000.0) ** (np.arange(HALF, dtype=np.float32) * np.float32(2.0 / HEAD))
    ).astype(np.float32)
    angles = frequency[:, None] * np.arange(length, dtype=np.float32)[None, :]
    return np.cos(angles).astype(np.float32), np.sin(angles).astype(np.float32)


def key_extents(length):
    extents = list(range(256, length, 128))
    return extents + [length]


def halves(values):
    length = values.shape[-1]
    split = values.reshape(values.shape[0] // HEAD, 2, HALF, length)
    return split[:, 0], split[:, 1]


def joined(first, second):
    length = first.shape[-1]
    both = jnp.concatenate([first[:, None], second[:, None]], axis=1)
    return both.reshape(first.shape[0] * HEAD, length)


GATHER_AHEAD = (
    (0, 1), (1, 1), (2, 1), (3, 1), (0, 2), (0, 3), (4, 1), (0, 4),
)
GATHER_FIRST = ((1, 2), (1, 3), (5, 1), (2, 2), (6, 1), (1, 4))
GATHER_AFTER = {
    0: ((7, 1), (3, 2), (8, 1), (4, 2)), 1: ((2, 3), (6, 2), (9, 1), (5, 2)),
    2: ((2, 4), (7, 2), (3, 3), (8, 2)), 3: ((4, 3), (9, 2)), 4: ((5, 3), (6, 3), (3, 4)),
    5: ((7, 3), (8, 3)), 6: ((9, 3),), 7: ((4, 4),), 8: ((5, 4),),
    10: ((6, 4), (7, 4), (8, 4), (9, 4)),
}
EARLY = 2


def forward_attention(
    layers,
    lens, x_ref, rows_ref, w_ref, ffn_ref, cos_ref, sin_ref,
    q_ref, k_ref, v_ref, mix_ref, raw_ref, inv_ref, exp_ref, *rest,
):
    seqs, length = x_ref.shape[0], x_ref.shape[1]
    group, seq = pl.program_id(0), pl.program_id(1)
    step = group * seqs + seq
    if layers:
        all_rows_ref, attn_ref, ffn_all_ref, hidden, w_t, bias_t, white = rest[:7]
        w_all, ffn_all, send, recv, local = rest[7:]
        me = position()
        spot = (me["z"], me["x"], me["y"], me["c"])
        owned = w_all.shape[4] - 16
        every = slice(None)
        tails = [(slice(owned, owned + 16), every)]
        tails += [(slice(0, owned), slice(i * 128, i * 128 + 128)) for i in range(D // 128)]
        pieces = [
            PieceGather(
                me, layers, w_all, tail, send.at[i], recv.at[i], "xy" if i < 2 else "xy"[i % 2]
            )
            for i, tail in enumerate(tails)
        ]
        for k in range(EARLY):
            for j in range(2):
                i = len(pieces)
                pieces.append(
                    PieceGather(
                        me, layers, ffn_all.at[j, k], (), send.at[i], recv.at[i], "xy"[i % 2]
                    )
                )

        def act(actions):
            for piece, stage in actions:
                if stage < 4:
                    pieces[piece].advance(stage)
                else:
                    pieces[piece].wait(3)

        results = [
            pltpu.make_async_copy(w_all.at[:, :, :, :, 0:owned], attn_ref, local.at[0]),
            pltpu.make_async_copy(ffn_all, ffn_all_ref, local.at[1]),
        ]
    else:
        hidden, w_t, bias_t, white = rest

    @pl.when(step == 0)
    def _():
        if layers:
            greet(me, layers, True)
            own = [
                pltpu.make_async_copy(source, w_all.at[spot + (pl.ds(*at),)], local.at[i])
                for i, source, at in ((0, w_ref, (0, owned)), (2, rows_ref, (owned, 16)))
            ]
            own += [
                pltpu.make_async_copy(
                    ffn_ref.at[j, k * ROWS : (k + 1) * ROWS], ffn_all.at[(j, k) + spot],
                    local.at[3 + j * EARLY + k],
                )
                for j in range(2)
                for k in range(EARLY)
            ]
            for copy in own:
                copy.start()
            for copy in own:
                copy.wait()
            meet(layers, True)
            for piece in pieces:
                piece.start(0)
        for s in range(seqs):
            white[s] = whiten(x_ref[s].astype(F32))[0]
        if layers:
            act(GATHER_AHEAD)
            rows = jnp.zeros((16, D), F32)
            for z in range(layers):
                for i in range(8):
                    rows += w_all[z, i // 4, i // 2 % 2, i % 2, owned : owned + 16].astype(F32)
            all_rows_ref[...] = rows
        else:
            rows = rows_ref[...]
        bias_t[...] = rows.T
        for s in range(seqs):
            hidden[s] = (white[s] * rows[0:1] + rows[2:3]).astype(BF)
        if layers:
            act(GATHER_FIRST)

    columns = pl.ds(pl.multiple_of(group * 128, 128), 128)

    @pl.when(seq == 0)
    def _():
        for j in range(3):
            if layers:
                block = w_all[j, :, :, :, 0:owned, columns].reshape(D, 128)
            else:
                block = w_ref[j, :, columns]
            w_t[j * 128 : (j + 1) * 128] = block.T

    cosine, sine = cos_ref[...], sin_ref[...]
    scale = 1.0 / math.sqrt(HEAD)
    lin = dot_nt(w_t[...], hidden[seq])
    for j, out_ref in enumerate((q_ref, k_ref, v_ref)):
        part = lin[j * 128 : (j + 1) * 128] + bias_t[columns, 4 + j : 5 + j]
        if j < 2:
            first, second = halves(part)
            part = joined(first * cosine - second * sine, second * cosine + first * sine)
            if j == 0:
                part = part * scale
        out_ref[0] = part.astype(BF)

    spots = lax.broadcasted_iota(jnp.int32, (16, length), 1)
    lead = lax.broadcasted_iota(jnp.int32, (16, length), 0) == 0
    mask = jnp.where(lead & (spots >= lens[seq]), -1e9, 0.0).astype(BF)
    ones = jnp.where(lead, 1.0, 0.0).astype(BF)
    keys = jnp.concatenate([k_ref[0], mask], axis=0).T

    def scored(h):
        blank = jnp.zeros((HEAD, length), BF)
        rows_q = [blank] * 4
        rows_q[h] = q_ref[0, h * HEAD : (h + 1) * HEAD]
        return dot_nn(keys, jnp.concatenate(rows_q + [ones], axis=0))

    def soft(h, scores):
        exponent = jnp.exp(scores - jnp.max(scores, axis=0, keepdims=True))
        inverse = 1.0 / jnp.sum(exponent, axis=0, keepdims=True)
        exponent = exponent.astype(BF)
        exp_ref[0, h] = exponent
        inv_ref[0, 0, h : h + 1] = inverse
        return exponent, inverse

    def mix(h, pair):
        at = slice(h * HEAD, (h + 1) * HEAD)
        mixed = dot_nn(v_ref[0, at], pair[0]) * pair[1]
        raw_ref[0, at] = mixed
        mix_ref[0, at] = mixed.astype(BF)

    ahead = scored(0)
    for h in range(4):
        scores = ahead
        if h < 3:
            ahead = scored(h + 1)
        mix(h, soft(h, scores))

    if layers:
        for after, actions in GATHER_AFTER.items():
            pl.when(step == after)(functools.partial(act, actions))

        @pl.when(step == 8)
        def _():
            results[0].start()

        @pl.when(step == 10)
        def _():
            results[1].start()

        @pl.when(step == 14)
        def _():
            for copy in results:
                copy.wait()


def backward_attention(
    lens, x_ref, w_ref, rows_ref, cos_ref, sin_ref,
    q_ref, k_ref, v_ref, gmix_ref, raw_ref, inv_ref, exp_ref, gmid_ref,
    gx_ref, gw_ref, small_ref, w_t, g_t,
):
    length = x_ref.shape[1]
    seq, group = pl.program_id(0), pl.program_id(1)

    @pl.when((seq == 0) & (group == 0))
    def _():
        for j in range(3):
            w_t[pl.ds(j * D, D), :] = matrix(w_ref, j).T
        gw_ref[...] = jnp.zeros_like(gw_ref)
        small_ref[...] = jnp.zeros_like(small_ref)

    limit = lens[seq]
    scale = 1.0 / math.sqrt(HEAD)
    low_edge = 0
    for extent in key_extents(length):

        @pl.when((limit > low_edge) & (limit <= extent))
        def _(extent=extent):
            cosine, sine = cos_ref[...], sin_ref[...]
            start = pl.multiple_of(group * 128, 128)
            if extent < length:
                for j in (1, 2):
                    g_t[pl.ds(start + j * D, 128), extent:length] = jnp.zeros(
                        (128, length - extent), BF
                    )

            def back_turn(w, c, s):
                first, second = w[:HALF], w[HALF:]
                return jnp.concatenate(
                    [first * c + second * s, second * c - first * s], axis=0
                ).astype(BF)

            for h in range(4):
                at = slice(h * HEAD, (h + 1) * HEAD)
                row = start + h * HEAD
                query, key = q_ref[0, at], k_ref[0, at, 0:extent]
                exponent = exp_ref[0, h, 0:extent]
                inverse = inv_ref[0, 0, h : h + 1]
                grad_mixed = (gmix_ref[0, at].astype(F32) * inverse).astype(BF)
                inner = jnp.sum(
                    raw_ref[0, at] * grad_mixed.astype(F32), axis=0, keepdims=True
                )
                grad_probs = dot_tn(v_ref[0, at, 0:extent], grad_mixed)
                grad_scores = (exponent.astype(F32) * (grad_probs - inner)).astype(BF)
                grad_value = dot_nt(grad_mixed, exponent)
                grad_key = dot_nt(query, grad_scores)
                grad_query = dot_nn(key, grad_scores) * scale
                g_t[pl.ds(row, HEAD), :] = back_turn(grad_query, cosine, sine)
                g_t[pl.ds(row + D, HEAD), 0:extent] = back_turn(
                    grad_key, cosine[:, 0:extent], sine[:, 0:extent]
                )
                g_t[pl.ds(row + 2 * D, HEAD), 0:extent] = grad_value.astype(BF)

        low_edge = extent

    @pl.when(group == pl.num_programs(1) - 1)
    def _():
        whitened, inverse = whiten(x_ref[0].astype(F32))
        gain = rows_ref[0:1, :]
        hidden = (whitened * gain + rows_ref[2:3, :]).astype(BF)
        hidden_t = hidden.T
        grads = g_t[...]
        ones = jnp.ones((8, length), BF)
        grad_hidden = dot_tn(grads, w_t[...])
        for j in range(3):
            part = grads[j * D : (j + 1) * D]
            small_ref[2 + j : 3 + j, :] += dot_nt(ones, part)[0:1]
            gw_ref[pl.ds(j * D, D), :] += dot_nt(hidden_t, part)
        small_ref[0:1, :] += jnp.sum(grad_hidden * whitened, axis=0, keepdims=True)
        small_ref[1:2, :] += jnp.sum(grad_hidden, axis=0, keepdims=True)
        gx_ref[0] = gmid_ref[0] + whiten_back(grad_hidden, whitened, inverse, gain)


def feed_forward(
    layers,
    x_ref, mix_ref, wo_ref, rows_ref, cot_ref, u_ref, v_ref, fbias_ref,
    head_ref, label_ref, flag_ref, lens,
    out_ref, gmid_ref, gmix_ref, gffn_ref, gfb_ref, gwo_ref, small_ref, late_ref,
    middle, lefts, totals, lows, x_buf, mix_buf, cot_buf, copied, *comm,
):
    seqs, length = x_ref.shape[0], x_ref.shape[1]
    pad = lefts.shape[1] // seqs
    step = pl.program_id(0)
    last = pl.num_programs(0) - 1
    chunk = lows.shape[2]

    def moves(pairs, first, s):
        return [
            pltpu.make_async_copy(a.at[s], b.at[s], copied.at[first + i, s])
            for i, (a, b) in enumerate(pairs)
        ]

    arrivals = functools.partial(
        moves, ((mix_ref, mix_buf), (x_ref, x_buf), (cot_ref, cot_buf)), 0
    )
    leavings = functools.partial(
        moves, ((mix_buf, gmix_ref), (x_buf, out_ref), (middle, gmid_ref)), 3
    )

    def rows_of(s, count):
        if isinstance(s, int):
            return pl.ds(s * pad, count)
        return pl.ds(pl.multiple_of(s * pad, 16), count)

    if layers:
        me = position()
        terms, weights, w_send, w_recv, w_local = comm[:5]
        comm = comm[5:]
        spot = (me["z"], me["x"], me["y"], me["c"])
        chunks = weights.shape[1]
        late = range(EARLY, chunks)
        loads = [
            pltpu.make_async_copy(u_ref.at[j], weights.at[j, 0:EARLY], w_local.at[j])
            for j in range(2)
        ]
        own = [
            pltpu.make_async_copy(
                v_ref.at[j, k * ROWS : (k + 1) * ROWS], weights.at[(j, k) + spot],
                w_local.at[2 + j * chunks + k],
            )
            for j in range(2)
            for k in late
        ]
        gathers = {
            k: [
                PieceGather(
                    me, layers, weights.at[j, k], (), w_send.at[k, j], w_recv.at[k, j], "xy"[j]
                )
                for j in range(2)
            ]
            for k in late
        }

        def gather(stage, *which):
            for k in which:
                for piece in gathers[k]:
                    if stage < 4:
                        piece.advance(stage)
                    else:
                        piece.wait(3)

        farewell = [
            pltpu.make_async_copy(terms.at[j], late_ref.at[j], w_local.at[j]) for j in range(2)
        ]

        def pieces(k):
            slot = lax.rem(k, 2) * 2
            return [PieceReduce(me, layers, comm, slot + j, "yx"[j]) for j in range(2)]

        def getter(j):
            def get(i, core):
                at = (i * 2 + core) * ROWS
                return terms[j, pl.ds(pl.multiple_of(at, ROWS), ROWS), :]

            return get

        def over_first(k):
            for j, op in enumerate(pieces(k)):
                op.over_first(getter(j))

        def over_second(k):
            for op in pieces(k):
                op.over_second()

        def over_layers(k):
            for op in pieces(k):
                op.over_layers()

        def finish(k):
            rows = pl.ds(pl.multiple_of(k * ROWS, ROWS), ROWS)
            for j, op in enumerate(pieces(k)):
                gffn_ref[j, rows, :] = op.finish()

    def later(stage, delay):
        if layers:
            pl.when(step >= delay)(lambda: stage(step - delay))

    def at_step(k, *args):
        if layers:
            pl.when(step == k)(functools.partial(gather, *args))

    @pl.when(step == 0)
    def _():
        for s in range(seqs):
            for copy in arrivals(s):
                copy.start()
        if layers:
            greet(me, layers)
            for copy in own + loads:
                copy.start()
            for copy in own:
                copy.wait()
            meet(layers)
            for k in late:
                for piece in gathers[k]:
                    piece.start(0)
        blank = jnp.zeros((pad - length, D), BF)

        @pl.loop(0, seqs)
        def _(s):
            for copy in arrivals(s):
                copy.wait()
            branch = dot_tn(mix_buf[s], matrix(wo_ref, 0)) + rows_ref[7:8, :]
            mid = x_buf[s].astype(F32) + branch
            middle[s] = mid
            whitened, _ = whiten(mid)
            low = (whitened * rows_ref[1:2, :] + rows_ref[3:4, :]).astype(BF)
            lefts[0, rows_of(s, pad), :] = jnp.concatenate([low, blank], axis=0)
            lefts[1, rows_of(s, pad), :] = jnp.concatenate([cot_buf[s], blank], axis=0)
            if layers:
                pl.when(s == 1)(lambda: gather(1, 2))

        totals[...] = jnp.zeros_like(totals)
        gfb_ref[...] = jnp.zeros_like(gfb_ref)
        if layers:
            for copy in loads:
                copy.wait()
            gather(1, 3)

    def weight(j):
        if layers:
            return weights[j, step].reshape(chunk, D)
        return (u_ref, v_ref)[j][0]

    fbias = fbias_ref[0]

    def block(s, total):
        rows = rows_of(s, pad)
        upward = dot_nt(lefts[0, rows, :], weight(0)) + fbias
        grad_act = dot_nt(lefts[1, rows, :], weight(1))
        phi = 0.5 * (1.0 + lax.erf(upward * ROOT_HALF))
        act = (upward * phi).astype(BF)
        slope = phi + upward * jnp.exp(-0.5 * upward * upward) * INV_ROOT_TWO_PI
        grad_up = (grad_act * slope).astype(BF)
        lows[0, rows, :] = grad_up
        lows[1, rows, :] = act
        totals[0, rows, :] += dot_nn(grad_up, weight(0))
        totals[1, rows, :] += dot_nn(act, weight(1))
        if layers:

            @pl.when(s == 1)
            def _():
                at_step(0, 2, 2)
                at_step(0, 1, 4)
                at_step(1, 4, 2)
                at_step(2, 4, 3, 4)
                later(over_first, 1)
                later(over_layers, 2)

        return total + jnp.sum(grad_up.astype(F32), axis=0, keepdims=True)

    total = lax.fori_loop(0, seqs, block, jnp.zeros_like(fbias))
    gfb_ref[step, :, 0:chunk] = total

    for j in range(2):
        product = dot_tn(lows[j], lefts[j])
        if layers:
            terms[j] = product
        else:
            gffn_ref[j, 0] = product

    if layers:

        @pl.when(step < last)
        def _():
            for j, op in enumerate(pieces(step)):
                op.over_cores(getter(j))

        @pl.when(step == last)
        def _():
            for copy in farewell:
                copy.start()

        at_step(0, 3, 2)
        at_step(0, 2, 3, 4)
        at_step(1, 3, 3, 4)
        later(over_second, 1)
        later(finish, 2)

    @pl.when(step == last)
    def _():
        gain = rows_ref[1:2, :]
        gwo_ref[...] = jnp.zeros_like(gwo_ref)

        def sequence(s, sums):
            gain_sum, shift_sum, branch_sum, cot_sum, loglik, hits = sums
            rows = rows_of(s, length)
            mid = middle[s]
            final = mid + (totals[1, rows, :] + rows_ref[8:9, :])
            x_buf[s] = final.astype(BF)
            unit, _ = whiten(final)
            logits = lax.dot_general(
                head_ref[...], unit.astype(BF), (((0,), (1,)), ((), ())), preferred_element_type=F32
            )
            slot = lax.broadcasted_iota(jnp.int32, logits.shape, 0)
            shifted = logits - jnp.max(logits, axis=0, keepdims=True)
            logprob = shifted - jnp.log(jnp.sum(jnp.exp(shifted), axis=0, keepdims=True))
            picked = jnp.sum(
                jnp.where(slot == label_ref[pl.ds(s, 1), :], logprob, 0.0), axis=0, keepdims=True
            )
            spots = lax.broadcasted_iota(jnp.int32, (1, length), 1)
            live = (flag_ref[pl.ds(s, 1), :] == 1) & (spots < lens[s])

            gradient = totals[0, rows, :]
            whitened, inverse = whiten(mid)
            own = cot_buf[s].astype(F32)
            grad_mid = own + whiten_back(gradient, whitened, inverse, gain)
            middle[s] = grad_mid
            low = grad_mid.astype(BF)
            gwo_ref[...] += dot_nn(mix_buf[s], low)
            mix_buf[s] = dot_nt(matrix(wo_ref, 0), low).astype(BF)
            for copy in leavings(s):
                copy.start()
            if layers:
                if s == 0:
                    over_layers(last - 1)
                if s == seqs - 1:
                    finish(last - 1)
            return (
                gain_sum + jnp.sum(gradient * whitened, axis=0, keepdims=True),
                shift_sum + jnp.sum(gradient, axis=0, keepdims=True),
                branch_sum + jnp.sum(low.astype(F32), axis=0, keepdims=True),
                cot_sum + jnp.sum(own, axis=0, keepdims=True),
                loglik + jnp.where(live, picked, 0.0),
                hits + jnp.where(live, jnp.exp(picked), 0.0),
            )

        blanks = [jnp.zeros((1, D), F32)] * 4 + [jnp.zeros((1, length), F32)] * 2
        sums = tuple(blanks)
        for s in range(seqs):
            sums = sequence(s, sums)
        gain_sum, shift_sum, branch_sum, cot_sum, loglik, hits = sums
        small_ref[0:1, :] = gain_sum
        small_ref[1:2, :] = shift_sum
        small_ref[2:3, :] = branch_sum
        small_ref[3:4, :] = cot_sum
        small_ref[4:8, :] = jnp.zeros((4, D), F32)
        small_ref[4:5, 0:128] = jnp.broadcast_to(
            jnp.sum(loglik, axis=1, keepdims=True), (1, 128)
        )
        small_ref[4:5, 128:256] = jnp.broadcast_to(
            jnp.sum(hits, axis=1, keepdims=True), (1, 128)
        )
        for s in range(seqs):
            for copy in leavings(s):
                copy.wait()
        if layers:
            for copy in farewell:
                copy.wait()


def whole(shape):
    return pl.BlockSpec(shape, lambda *_: (0,) * len(shape), pipeline_mode=pl.Buffered(1))


def block_of(shape, *index):
    return pl.BlockSpec(shape, lambda *_: index, pipeline_mode=pl.Buffered(1))


def leading(shape):
    return pl.BlockSpec((1,) + tuple(shape[1:]), lambda i, *_: (i,) + (0,) * (len(shape) - 1))


def shaped(shape, dtype=F32):
    return jax.ShapeDtypeStruct(shape, dtype)


def projections(attn, first, count):
    blocks = attn.shape[0] // 4
    rows = D // blocks
    return block_of((blocks * count, rows, D), first // count, 0, 0)


def attention_forward(lengths, tokens, rows_all, attn, ffn, cosine, sine, layers):
    seqs, length, _ = tokens.shape
    heads = HEADS // 4
    flat = (seqs, D, length)
    inverse = (seqs, heads, 4, length)
    exponent = (seqs, HEADS, length, length)

    def part(block):
        return pl.BlockSpec(block, lambda g, s, *_: (s, g, 0, 0)[: len(block)])

    out_specs = [part((1, 128, length))] * 5
    out_specs += [part((1, 1, 4, length)), part((1, 4, length, length))]
    out_shape = [shaped(flat, BF)] * 4 + [shaped(flat), shaped(inverse), shaped(exponent, BF)]
    scratch = [
        pltpu.VMEM((seqs, length, D), BF), pltpu.VMEM((384, D), BF), pltpu.VMEM((D, 16), F32),
        pltpu.VMEM((seqs, length, D), F32),
    ]
    hbm = pl.BlockSpec(memory_space=pl.ANY)
    params = dict(vmem_limit_bytes=VMEM_LIMIT)
    if layers:
        chips = (layers, 2, 2, 2)
        owned = attn.shape[0]
        early = (2, EARLY) + chips + (ROWS, D)
        out_specs += [whole((16, D)), hbm, hbm]
        out_shape += [
            shaped((16, D)), shaped(chips + (owned, D), BF),
            shaped(early, BF),
        ]
        scratch += [
            pltpu.VMEM(chips + (owned + 16, D), BF), pltpu.VMEM(early, BF),
            pltpu.SemaphoreType.DMA((10, 3 + layers)), pltpu.SemaphoreType.DMA((10, 3 + layers)),
            pltpu.SemaphoreType.DMA((3 + 2 * EARLY,)),
        ]
        params.update(collective_id=2, has_side_effects=True)
        sources = [hbm, hbm, hbm]
    else:
        sources = [whole(rows_all.shape), whole(attn.shape), hbm]
    return pl.pallas_call(
        functools.partial(forward_attention, layers),
        grid_spec=pltpu.PrefetchScalarGridSpec(
            num_scalar_prefetch=1,
            grid=(heads, seqs),
            in_specs=[whole(tokens.shape)] + sources + [whole(cosine.shape), whole(sine.shape)],
            out_specs=out_specs,
            scratch_shapes=scratch,
        ),
        out_shape=out_shape,
        compiler_params=pltpu.CompilerParams(**params),
        name="attention_forward",
    )(lengths, tokens, rows_all, attn, ffn, cosine, sine)


def attention_backward(
    lengths, tokens, attn, rows_all, cosine, sine, query, key, value, grad_mixed, raw,
    inverse, exponent, grad_middle,
):
    seqs, length, _ = tokens.shape

    def part(block):
        return pl.BlockSpec(block, lambda s, g, *_: (s, g, 0, 0)[: len(block)])

    return pl.pallas_call(
        backward_attention,
        grid_spec=pltpu.PrefetchScalarGridSpec(
            num_scalar_prefetch=1,
            grid=(seqs, HEADS // 4),
            in_specs=[
                leading(tokens.shape), projections(attn, 0, 3), whole(rows_all.shape),
                whole(cosine.shape), whole(sine.shape),
            ]
            + [part((1, 128, length))] * 5
            + [part((1, 1, 4, length)), part((1, 4, length, length)), leading(tokens.shape)],
            out_specs=[leading(tokens.shape), whole((3 * D, D)), whole((8, D))],
            scratch_shapes=[pltpu.VMEM((3 * D, D), BF), pltpu.VMEM((3 * D, length), BF)],
        ),
        out_shape=[shaped(tokens.shape), shaped((3 * D, D)), shaped((8, D))],
        compiler_params=pltpu.CompilerParams(vmem_limit_bytes=VMEM_LIMIT),
        name="attention_backward",
    )(
        lengths, tokens, attn, rows_all, cosine, sine, query, key, value, grad_mixed, raw,
        inverse, exponent, grad_middle,
    )


def feed_forward_both(
    tokens, mixed, attn, rows_all, cotangent, ffn, fbias, head, labels, flags, lengths, layers,
):
    seqs, length, _ = tokens.shape
    pad = (length + 15) // 16 * 16
    rows = seqs * pad
    steps, chunk = fbias.shape
    hbm = pl.BlockSpec(memory_space=pl.ANY)
    if layers:
        ups, downs = ffn
        up_spec = down_spec = hbm
        owned = downs.shape[1]
        grad_spec, grad_shape = whole((2, owned - ROWS, D)), shaped((2, owned - ROWS, D))
        late_shape = (2, chunk, D)
        chips = (layers, 2, 2, 2)
        extra = [
            pltpu.VMEM(late_shape, F32), pltpu.VMEM((2, steps) + chips + (ROWS, D), BF),
            pltpu.SemaphoreType.DMA((steps, 2, 2 + layers)),
            pltpu.SemaphoreType.DMA((steps, 2, 2 + layers)),
            pltpu.SemaphoreType.DMA((2 + 2 * steps,)),
        ]
        extra += reduce_scratch(4, layers)
    else:
        chunked = (steps, chunk, D)
        ups, downs = ffn[0].reshape(chunked), ffn[1].reshape(chunked)
        up_spec = down_spec = leading(chunked)
        grad_spec = pl.BlockSpec((2, 1, chunk, D), lambda k: (0, k, 0, 0))
        grad_shape = shaped((2,) + chunked)
        late_shape = (8, 128)
        extra = []
    return pl.pallas_call(
        functools.partial(feed_forward, layers),
        grid=(steps,),
        in_specs=[
            hbm, hbm, projections(attn, 3, 1), whole(rows_all.shape), hbm, up_spec, down_spec,
            leading((steps, 1, chunk)), whole(head.shape), whole(labels.shape),
            whole(flags.shape), pl.BlockSpec(memory_space=pltpu.SMEM),
        ],
        out_specs=[
            hbm, hbm, hbm, grad_spec, whole((8, 1, D)), whole((D, D)), whole((8, D)), hbm,
        ],
        out_shape=[
            shaped(tokens.shape, BF), shaped(tokens.shape), shaped(mixed.shape, BF),
            grad_shape, shaped((8, 1, D)), shaped((D, D)), shaped((8, D)), shaped(late_shape),
        ],
        scratch_shapes=[
            pltpu.VMEM(tokens.shape, F32),
            pltpu.VMEM((2, rows, D), BF),
            pltpu.VMEM((2, rows, D), F32),
            pltpu.VMEM((2, rows, chunk), BF),
            pltpu.VMEM(tokens.shape, BF),
            pltpu.VMEM(mixed.shape, BF),
            pltpu.VMEM(tokens.shape, BF),
            pltpu.SemaphoreType.DMA((6, seqs)),
        ]
        + extra,
        compiler_params=pltpu.CompilerParams(
            vmem_limit_bytes=VMEM_LIMIT, **(dict(collective_id=0, has_side_effects=True) if layers else {})
        ),
        name="feed_forward",
    )(
        tokens, mixed, attn, rows_all, cotangent, ups, downs,
        fbias.reshape(steps, 1, chunk), head, labels, flags, lengths,
    )


def reduce_tail(grad_qkv, grad_wo, late, part, small_one, small_two, units, layers):
    owned = grad_wo.shape[1]
    pieces = 2 + owned // ROWS
    devices = grad_qkv.shape[0] + grad_wo.shape[0]
    hbm, vmem = pl.BlockSpec(memory_space=pl.ANY), pl.BlockSpec(memory_space=pltpu.VMEM)
    return pl.pallas_call(
        functools.partial(gradient_tail, layers),
        in_specs=[hbm] * 3 + [vmem] * 4,
        out_specs=[vmem] * 3,
        out_shape=[shaped((owned, D)), shaped((2, owned, D)), shaped((24, D))],
        scratch_shapes=[
            pltpu.VMEM((pieces, devices, ROWS, D), F32),
            pltpu.SemaphoreType.DMA((pieces, 2)),
            pltpu.VMEM((4, 24, D), F32),
            pltpu.VMEM((3 + layers, 24, D), F32),
            pltpu.SemaphoreType.DMA((2 + layers,)),
            pltpu.SemaphoreType.DMA((2 + layers,)),
        ]
        + reduce_scratch(pieces, layers),
        compiler_params=pltpu.CompilerParams(
            vmem_limit_bytes=VMEM_LIMIT, collective_id=1, has_side_effects=True
        ),
        name="gradient_tail",
    )(grad_qkv, grad_wo, late.reshape(2, devices, ROWS, D), part, small_one, small_two, units)


def per_device(
    tokens, lengths, masked_flags, labels, attn_weights, ffn_weights, ffn_bias, norm_gains,
    biases, head_weight, cotangent,
):
    both = ("wide", "narrow")
    seqs, length, _ = tokens.shape
    wide, narrow = lax.axis_size("wide"), lax.axis_size("narrow")
    devices = wide * narrow
    shard, units = D // wide, ffn_bias.shape[0]
    owned = attn_weights.shape[0]
    layers = 4 if (wide, narrow) == (8, 4) and owned == units and owned % ROWS == 0 else 0
    at = lax.axis_index("wide")
    owner = at * narrow + lax.axis_index("narrow")
    first = (lax.axis_index("narrow") == 0).astype(BF)
    own = jnp.concatenate([norm_gains, biases], axis=0) * first
    rows_own = lax.dynamic_update_slice(jnp.zeros((16, D), BF), own, (0, at * shard))
    flat = lax.dynamic_update_slice(jnp.zeros((4 * D,), BF), ffn_bias, (owner * units,))
    rows_own = rows_own + jnp.pad(flat.reshape(4, D), ((9, 3), (0, 0)))
    cosine, sine = rotary_tables(length)
    if layers:
        rows_all, attn, ffn = rows_own, attn_weights, ffn_weights
    else:
        attn = lax.all_gather(attn_weights, both, axis=0, tiled=True).reshape(4, D, D)
        ffn = lax.all_gather(ffn_weights, both, axis=1, tiled=True)
        rows_all = lax.psum(rows_own.astype(F32), both)
    query, key, value, mixed, raw, inverse, exponent, *gathered = attention_forward(
        lengths, tokens, rows_all, attn, ffn, cosine, sine, layers
    )
    if layers:
        rows_all, attn, ffn = gathered
        attn = attn.reshape(devices, owned, D)
        ffn = (ffn, ffn_weights)
        unit_bias = rows_all[9:13].reshape(devices, units // ROWS, ROWS).transpose(1, 0, 2)
        unit_bias = unit_bias.reshape(units // ROWS, devices * ROWS)
    else:
        unit_bias = rows_all[9:13].reshape(-1, 512)
    (
        output, grad_middle, grad_mixed, grad_ffn, unit_sums, grad_wo, small_two, late,
    ) = feed_forward_both(
        tokens, mixed, attn, rows_all, cotangent, ffn, unit_bias, head_weight, labels,
        masked_flags, lengths, layers,
    )
    if not layers:
        grad_ffn = lax.psum_scatter(
            grad_ffn.reshape(2, -1, D), both, scatter_dimension=1, tiled=True
        )
    grad_tokens, grad_qkv, small_one = attention_backward(
        lengths, tokens, attn, rows_all, cosine, sine, query, key, value, grad_mixed, raw,
        inverse, exponent, grad_middle,
    )
    steps, chunk = unit_bias.shape
    if layers:
        blocks = (-1, owned, D)
        grad_attn, grad_ffn, sums = reduce_tail(
            grad_qkv.reshape(blocks), grad_wo.reshape(blocks), late, grad_ffn, small_one,
            small_two, unit_sums, layers,
        )
        grad_ffn_bias = lax.dynamic_slice(
            sums, (16, owner * ROWS), (steps, ROWS)
        ).reshape(units)
    else:
        grad_attn = lax.psum_scatter(
            jnp.concatenate([grad_qkv, grad_wo], axis=0), both, scatter_dimension=0, tiled=True
        )
        sums = jnp.concatenate(
            [
                small_one[0:1], small_two[0:1], small_one[1:2], small_two[1:2], small_one[2:5],
                small_two[2:5], jnp.zeros((6, D), F32), unit_sums[:, 0],
            ],
            axis=0,
        )
        sums = lax.psum(sums, both)
        grad_ffn_bias = lax.dynamic_slice_in_dim(
            sums[16:, :chunk].reshape(-1), owner * units, units, 0
        )
    grad_gains = lax.dynamic_slice(sums, (0, at * shard), (2, shard))
    grad_biases = lax.dynamic_slice(sums, (2, at * shard), (7, shard))
    head_stats = (
        sums[9, 0:256:128] * jnp.array([1.0, VOCAB], F32) / (seqs * length * devices)
    )
    return (
        output, grad_tokens, grad_attn, grad_ffn, grad_ffn_bias, grad_gains, grad_biases,
        head_stats,
    )


def solution(mesh):
    both = ("wide", "narrow")
    return jax.shard_map(
        per_device,
        mesh=mesh,
        in_specs=(
            P(both, None, None),
            P(both),
            P(both, None),
            P(both, None),
            P(both, None),
            P(None, both, None),
            P(both),
            P(None, "wide"),
            P(None, "wide"),
            P(),
            P(both, None, None),
        ),
        out_specs=(
            P(both, None, None),
            P(both, None, None),
            P(both, None),
            P(None, both, None),
            P(both),
            P(None, "wide"),
            P(None, "wide"),
            P(),
        ),
        check_vma=False,
    )
```

```python
import functools
import math

import jax
import jax.numpy as jnp
import numpy as np
from jax import lax
from jax.experimental import pallas as pl
from jax.experimental.pallas import tpu as pltpu
from jax.sharding import PartitionSpec as P

D = 640
HEADS = 20
HEAD = 32
HALF = HEAD // 2
VOCAB = 33
EPS = 1e-05
ROOT_HALF = 0.7071067811865476
INV_ROOT_TWO_PI = 0.3989422804014327
BF = jnp.bfloat16
F32 = jnp.float32
VMEM_LIMIT = 60 << 20

MESH = pl.DeviceIdType.MESH
ROWS = 16


def position():
    wide, narrow = lax.axis_index("wide"), lax.axis_index("narrow")
    return {
        "z": lax.div(wide, 2), "x": lax.rem(wide, 2),
        "y": lax.div(narrow, 2), "c": lax.rem(narrow, 2),
    }


def partner(me, axis, offset, size):
    there = dict(me)
    there[axis] = lax.rem(me[axis] + offset, size)
    return (there["z"] * 2 + there["x"], there["y"] * 2 + there["c"])


def across(me):
    return partner({**me, "x": 1 - me["x"]}, "y", 1, 2)


def greet(me, layers, corner=False):
    barrier = pltpu.get_barrier_semaphore()
    peers = [partner(me, axis, 1, 2) for axis in "cyx"]
    peers += [partner(me, "z", offset, layers) for offset in range(1, layers)]
    if corner:
        peers.append(across(me))
    for peer in peers:
        pl.semaphore_signal(barrier, inc=1, device_id=peer, device_id_type=MESH)


def meet(layers, corner=False):
    pl.semaphore_wait(pltpu.get_barrier_semaphore(), 2 + layers + corner)


def reduce_scratch(slots, layers):
    def blocks(count, dtype):
        return pltpu.VMEM((slots, count, ROWS, D), dtype)

    return [
        blocks(4 * layers, BF), blocks(4 * layers, BF),
        blocks(2 * layers, BF), blocks(2 * layers, BF), blocks(2 * layers, F32),
        blocks(layers, BF), blocks(layers, BF), blocks(layers, F32),
        blocks(layers, BF), blocks(layers, BF), blocks(1, F32),
        pltpu.SemaphoreType.DMA((slots, 3 + layers)),
        pltpu.SemaphoreType.DMA((slots, 3 + layers)),
    ]


class PieceReduce:
    def __init__(self, me, layers, refs, slot, first):
        (
            self.s0, self.r0, self.s1, self.r1, self.k1, self.s2, self.r2, self.k2,
            self.s3, self.r3, self.k3,
        ) = (ref.at[slot] for ref in refs[:11])
        self.send, self.recv = (ref.at[slot] for ref in refs[11:])
        self.me, self.layers = me, layers
        self.first, self.second = ("y", "x") if first == "y" else ("x", "y")

    def exchange(self, stage, source, target, axis):
        return pltpu.make_async_remote_copy(
            src_ref=source, dst_ref=target, send_sem=self.send.at[stage],
            recv_sem=self.recv.at[stage], device_id=partner(self.me, axis, 1, 2),
            device_id_type=MESH,
        )

    def layer_copies(self):
        me, layers = self.me, self.layers
        return [
            pltpu.make_async_remote_copy(
                src_ref=self.s3.at[lax.rem(me["z"] + offset, layers)],
                dst_ref=self.r3.at[offset], send_sem=self.send.at[2 + offset],
                recv_sem=self.recv.at[2 + offset],
                device_id=partner(me, "z", offset, layers), device_id_type=MESH,
            )
            for offset in range(1, layers)
        ]

    def rest(self, along, other):
        return other * 2 + along if self.first == "y" else along * 2 + other

    def over_cores(self, get):
        core = self.me["c"]

        @pl.loop(0, 4 * self.layers)
        def _(i):
            self.s0[i] = get(i, 1 - core).astype(BF)

        self.exchange(0, self.s0, self.r0, "c").start()

    def over_first(self, get):
        self.exchange(0, self.s0, self.r0, "c").wait()
        core, along = self.me["c"], self.me[self.first]

        @pl.loop(0, self.layers)
        def _(layer):
            for other in range(2):
                away = layer * 4 + self.rest(1 - along, other)
                near = layer * 4 + self.rest(along, other)
                at = layer * 2 + other
                self.s1[at] = (get(away, core) + self.r0[away].astype(F32)).astype(BF)
                self.k1[at] = get(near, core) + self.r0[near].astype(F32)

        self.exchange(1, self.s1, self.r1, self.first).start()

    def over_second(self):
        self.exchange(1, self.s1, self.r1, self.first).wait()
        along = self.me[self.second]

        @pl.loop(0, self.layers)
        def _(layer):
            away, near = layer * 2 + (1 - along), layer * 2 + along
            self.s2[layer] = (self.k1[away] + self.r1[away].astype(F32)).astype(BF)
            self.k2[layer] = self.k1[near] + self.r1[near].astype(F32)

        self.exchange(2, self.s2, self.r2, self.second).start()

    def over_layers(self):
        self.exchange(2, self.s2, self.r2, self.second).wait()
        own = self.me["z"]

        @pl.loop(0, self.layers)
        def _(layer):
            self.s3[layer] = (self.k2[layer] + self.r2[layer].astype(F32)).astype(BF)

        self.k3[0] = self.k2[own] + self.r2[own].astype(F32)
        for copy in self.layer_copies():
            copy.start()

    def finish(self):
        for copy in self.layer_copies():
            copy.wait()
        total = self.k3[0]
        for offset in range(1, self.layers):
            total = total + self.r3[offset].astype(F32)
        return total


class PieceGather:
    def __init__(self, me, layers, buf, tail, send, recv, first):
        self.me, self.layers, self.buf, self.tail = me, layers, buf, tail
        self.send, self.recv, self.first = send, recv, first

    def view(self, *lead):
        return self.buf.at[lead + self.tail]

    def copy(self, lead, peer, at):
        return pltpu.make_async_remote_copy(
            src_ref=self.view(*lead), dst_ref=self.view(*lead), send_sem=self.send.at[at],
            recv_sem=self.recv.at[at], device_id=peer, device_id_type=MESH,
        )

    def copies(self, stage):
        me, every = self.me, slice(None)
        z, x, y, core = me["z"], me["x"], me["y"], me["c"]
        if stage == 0:
            return [
                self.copy((z, x, y, core), partner(me, "z", offset, self.layers), 2 + offset)
                for offset in range(1, self.layers)
            ]
        if self.first == "xy" and stage < 3:
            if stage == 2:
                return []
            peers = partner(me, "x", 1, 2), partner(me, "y", 1, 2), across(me)
            return [
                self.copy((every, x, y, core), peer, at)
                for peer, at in zip(peers, (0, 1, 2 + self.layers))
            ]
        if stage == 1:
            lead, axis = (every, x, y, core), self.first
        elif stage == 2:
            lead = (every, every, y, core) if self.first == "x" else (every, x, every, core)
            axis = "y" if self.first == "x" else "x"
        else:
            lead, axis = (every, every, every, core), "c"
        return [self.copy(lead, partner(me, axis, 1, 2), stage - 1)]

    def start(self, stage):
        for copy in self.copies(stage):
            copy.start()

    def wait(self, stage):
        for copy in self.copies(stage):
            copy.wait()

    def advance(self, stage):
        self.wait(stage - 1)
        self.start(stage)


class SmallReduce:
    def __init__(self, me, layers, sent, got, send, recv):
        self.me, self.layers = me, layers
        self.sent, self.got, self.send, self.recv = sent, got, send, recv

    def exchange(self, stage):
        return pltpu.make_async_remote_copy(
            src_ref=self.sent.at[stage], dst_ref=self.got.at[stage],
            send_sem=self.send.at[stage], recv_sem=self.recv.at[stage],
            device_id=partner(self.me, "cyx"[stage], 1, 2), device_id_type=MESH,
        )

    def layer_copies(self):
        own = self.me["z"]
        return [
            pltpu.make_async_remote_copy(
                src_ref=self.sent.at[3], dst_ref=self.got.at[3 + own],
                send_sem=self.send.at[2 + offset], recv_sem=self.recv.at[2 + offset],
                device_id=partner(self.me, "z", offset, self.layers), device_id_type=MESH,
            )
            for offset in range(1, self.layers)
        ]

    def start(self, stage):
        if stage:
            self.exchange(stage - 1).wait()
            self.sent[stage] = self.sent[stage - 1] + self.got[stage - 1]
        if stage < 3:
            self.exchange(stage).start()
        else:
            for copy in self.layer_copies():
                copy.start()
            self.got[3 + self.me["z"]] = self.sent[3]

    def finish(self):
        for copy in self.layer_copies():
            copy.wait()
        total = self.got[3]
        for layer in range(1, self.layers):
            total = total + self.got[3 + layer]
        return total


TAIL_ORDER = (
    (0, 0), (1, 0), (2, 0), (7, 0), (3, 0), (4, 0), (0, 1), (1, 1), (7, 1), (5, 0), (6, 0),
    (2, 1), (3, 1), (4, 1), (5, 1), (7, 2), (6, 1), (0, 2), (1, 2), (2, 2), (3, 2), (7, 3),
    (4, 2), (0, 3), (1, 3), (5, 2), (6, 2), (2, 3), (3, 3), (4, 3), (0, 4), (1, 4), (7, 4),
    (5, 3), (6, 3), (2, 4), (3, 4), (4, 4), (5, 4), (6, 4),
)


def gradient_tail(layers, qkv_ref, wo_ref, late_ref, part_ref, one_ref, two_ref, units_ref,
                  grad_ref, gffn_ref, sums_ref, terms, loaded, sent, got, small_send,
                  small_recv, *refs):
    me = position()
    greet(me, layers)
    own, wo = qkv_ref.shape[0], wo_ref.shape[0]
    loads = []
    for p in range(terms.shape[0]):
        if p < 2:
            moves = [(late_ref.at[p], terms.at[p])]
        else:
            rows = slice((p - 2) * ROWS, (p - 1) * ROWS)
            moves = [
                (qkv_ref.at[:, rows], terms.at[p, 0:own]),
                (wo_ref.at[:, rows], terms.at[p, own : own + wo]),
            ]
        loads.append(
            [
                pltpu.make_async_copy(source, target, loaded.at[p, i])
                for i, (source, target) in enumerate(moves)
            ]
        )
        for copy in loads[-1]:
            copy.start()
    order = [(one_ref, 0), (two_ref, 0), (one_ref, 1), (two_ref, 1)]
    order += [(one_ref, 2), (one_ref, 3), (one_ref, 4), (two_ref, 2), (two_ref, 3), (two_ref, 4)]
    sent[0, 8:16] = jnp.zeros((8, D), F32)
    for row, (ref, at) in enumerate(order):
        sent[0, row : row + 1] = ref[at : at + 1]
    for k in range(8):
        sent[0, 16 + k : 17 + k] = units_ref[k]
    small = SmallReduce(me, layers, sent, got, small_send, small_recv)
    ops = [PieceReduce(me, layers, refs, p, "yx"[p % 2]) for p in range(terms.shape[0])]
    kept = part_ref.shape[1]
    gffn_ref[:, 0:kept] = part_ref[...]
    meet(layers)

    def getter(p):
        return lambda i, core: terms[p, i * 2 + core]

    for p, stage in TAIL_ORDER:
        if p == len(ops):
            if stage < 4:
                small.start(stage)
            else:
                sums_ref[...] = small.finish()
        elif stage == 0:
            for copy in loads[p]:
                copy.wait()
            ops[p].over_cores(getter(p))
        elif stage == 1:
            ops[p].over_first(getter(p))
        elif stage == 2:
            ops[p].over_second()
        elif stage == 3:
            ops[p].over_layers()
        elif p < 2:
            gffn_ref[p, kept:] = ops[p].finish()
        else:
            grad_ref[(p - 2) * ROWS : (p - 1) * ROWS] = ops[p].finish()


def dot_nn(a, b):
    return lax.dot_general(a, b, (((1,), (0,)), ((), ())), preferred_element_type=F32)


def dot_nt(a, b):
    return lax.dot_general(a, b, (((1,), (1,)), ((), ())), preferred_element_type=F32)


def dot_tn(a, b):
    return lax.dot_general(a, b, (((0,), (0,)), ((), ())), preferred_element_type=F32)


def matrix(ref, j):
    rows = ref.shape[1]
    blocks = D // rows
    return ref[j * blocks : (j + 1) * blocks].reshape(D, D)


def whiten(values):
    center = jnp.mean(values, axis=-1, keepdims=True)
    offset = values - center
    spread = jnp.mean(offset * offset, axis=-1, keepdims=True)
    inverse = lax.rsqrt(spread + EPS)
    return offset * inverse, inverse


def whiten_back(gradient, whitened, inverse, gain):
    scaled = gradient * gain
    mean_grad = jnp.mean(scaled, axis=-1, keepdims=True)
    mean_cross = jnp.mean(scaled * whitened, axis=-1, keepdims=True)
    return inverse * (scaled - mean_grad - whitened * mean_cross)


def rotary_tables(length):
    frequency = (
        np.float32(1.0)
        / np.float32(10000.0) ** (np.arange(HALF, dtype=np.float32) * np.float32(2.0 / HEAD))
    ).astype(np.float32)
    angles = frequency[:, None] * np.arange(length, dtype=np.float32)[None, :]
    return np.cos(angles).astype(np.float32), np.sin(angles).astype(np.float32)


def key_extents(length):
    extents = list(range(256, length, 128))
    return extents + [length]


def halves(values):
    length = values.shape[-1]
    split = values.reshape(values.shape[0] // HEAD, 2, HALF, length)
    return split[:, 0], split[:, 1]


def joined(first, second):
    length = first.shape[-1]
    both = jnp.concatenate([first[:, None], second[:, None]], axis=1)
    return both.reshape(first.shape[0] * HEAD, length)


GATHER_AHEAD = (
    (0, 1), (1, 1), (2, 1), (3, 1), (0, 2), (0, 3), (4, 1), (0, 4),
)
GATHER_FIRST = ((1, 2), (1, 3), (5, 1), (2, 2), (6, 1), (1, 4))
GATHER_AFTER = {
    0: ((7, 1), (3, 2), (8, 1), (4, 2)), 1: ((2, 3), (6, 2), (9, 1), (5, 2)),
    2: ((2, 4), (7, 2), (3, 3), (8, 2)), 3: ((4, 3), (9, 2)), 4: ((5, 3), (6, 3), (3, 4)),
    5: ((7, 3), (8, 3)), 6: ((9, 3),), 7: ((4, 4),), 8: ((5, 4),),
    10: ((6, 4), (7, 4), (8, 4), (9, 4)),
}
EARLY = 2


def forward_attention(
    layers,
    lens, x_ref, rows_ref, w_ref, ffn_ref, cos_ref, sin_ref,
    q_ref, k_ref, v_ref, mix_ref, raw_ref, inv_ref, exp_ref, *rest,
):
    seqs, length = x_ref.shape[0], x_ref.shape[1]
    group, seq = pl.program_id(0), pl.program_id(1)
    step = group * seqs + seq
    if layers:
        all_rows_ref, attn_ref, ffn_all_ref, hidden, w_t, bias_t, white = rest[:7]
        w_all, ffn_all, send, recv, local = rest[7:]
        me = position()
        spot = (me["z"], me["x"], me["y"], me["c"])
        owned = w_all.shape[4] - 16
        every = slice(None)
        tails = [(slice(owned, owned + 16), every)]
        tails += [(slice(0, owned), slice(i * 128, i * 128 + 128)) for i in range(D // 128)]
        pieces = [
            PieceGather(
                me, layers, w_all, tail, send.at[i], recv.at[i], "xy" if i < 2 else "xy"[i % 2]
            )
            for i, tail in enumerate(tails)
        ]
        for k in range(EARLY):
            for j in range(2):
                i = len(pieces)
                pieces.append(
                    PieceGather(
                        me, layers, ffn_all.at[j, k], (), send.at[i], recv.at[i], "xy"[i % 2]
                    )
                )

        def act(actions):
            for piece, stage in actions:
                if stage < 4:
                    pieces[piece].advance(stage)
                else:
                    pieces[piece].wait(3)

        results = [
            pltpu.make_async_copy(w_all.at[:, :, :, :, 0:owned], attn_ref, local.at[0]),
            pltpu.make_async_copy(ffn_all, ffn_all_ref, local.at[1]),
        ]
    else:
        hidden, w_t, bias_t, white = rest

    @pl.when(step == 0)
    def _():
        if layers:
            greet(me, layers, True)
            own = [
                pltpu.make_async_copy(source, w_all.at[spot + (pl.ds(*at),)], local.at[i])
                for i, source, at in ((0, w_ref, (0, owned)), (2, rows_ref, (owned, 16)))
            ]
            own += [
                pltpu.make_async_copy(
                    ffn_ref.at[j, k * ROWS : (k + 1) * ROWS], ffn_all.at[(j, k) + spot],
                    local.at[3 + j * EARLY + k],
                )
                for j in range(2)
                for k in range(EARLY)
            ]
            for copy in own:
                copy.start()
            for copy in own:
                copy.wait()
            meet(layers, True)
            for piece in pieces:
                piece.start(0)
        for s in range(seqs):
            white[s] = whiten(x_ref[s].astype(F32))[0]
        if layers:
            act(GATHER_AHEAD)
            rows = jnp.zeros((16, D), F32)
            for z in range(layers):
                for i in range(8):
                    rows += w_all[z, i // 4, i // 2 % 2, i % 2, owned : owned + 16].astype(F32)
            all_rows_ref[...] = rows
        else:
            rows = rows_ref[...]
        bias_t[...] = rows.T
        for s in range(seqs):
            hidden[s] = (white[s] * rows[0:1] + rows[2:3]).astype(BF)
        if layers:
            act(GATHER_FIRST)

    columns = pl.ds(pl.multiple_of(group * 128, 128), 128)

    @pl.when(seq == 0)
    def _():
        for j in range(3):
            if layers:
                block = w_all[j, :, :, :, 0:owned, columns].reshape(D, 128)
            else:
                block = w_ref[j, :, columns]
            w_t[j * 128 : (j + 1) * 128] = block.T

    cosine, sine = cos_ref[...], sin_ref[...]
    scale = 1.0 / math.sqrt(HEAD)
    lin = dot_nt(w_t[...], hidden[seq])
    for j, out_ref in enumerate((q_ref, k_ref, v_ref)):
        part = lin[j * 128 : (j + 1) * 128] + bias_t[columns, 4 + j : 5 + j]
        if j < 2:
            first, second = halves(part)
            part = joined(first * cosine - second * sine, second * cosine + first * sine)
            if j == 0:
                part = part * scale
        out_ref[0] = part.astype(BF)

    spots = lax.broadcasted_iota(jnp.int32, (16, length), 1)
    lead = lax.broadcasted_iota(jnp.int32, (16, length), 0) == 0
    mask = jnp.where(lead & (spots >= lens[seq]), -1e9, 0.0).astype(BF)
    ones = jnp.where(lead, 1.0, 0.0).astype(BF)
    keys = jnp.concatenate([k_ref[0], mask], axis=0).T

    def scored(h):
        blank = jnp.zeros((HEAD, length), BF)
        rows_q = [blank] * 4
        rows_q[h] = q_ref[0, h * HEAD : (h + 1) * HEAD]
        return dot_nn(keys, jnp.concatenate(rows_q + [ones], axis=0))

    def soft(h, scores):
        exponent = jnp.exp(scores - jnp.max(scores, axis=0, keepdims=True))
        inverse = 1.0 / jnp.sum(exponent, axis=0, keepdims=True)
        exponent = exponent.astype(BF)
        exp_ref[0, h] = exponent
        inv_ref[0, 0, h : h + 1] = inverse
        return exponent, inverse

    def mix(h, pair):
        at = slice(h * HEAD, (h + 1) * HEAD)
        mixed = dot_nn(v_ref[0, at], pair[0]) * pair[1]
        raw_ref[0, at] = mixed
        mix_ref[0, at] = mixed.astype(BF)

    ahead = scored(0)
    for h in range(4):
        scores = ahead
        if h < 3:
            ahead = scored(h + 1)
        mix(h, soft(h, scores))

    if layers:
        for after, actions in GATHER_AFTER.items():
            pl.when(step == after)(functools.partial(act, actions))

        @pl.when(step == 8)
        def _():
            results[0].start()

        @pl.when(step == 10)
        def _():
            results[1].start()

        @pl.when(step == 14)
        def _():
            for copy in results:
                copy.wait()


def backward_attention(
    lens, x_ref, w_ref, rows_ref, cos_ref, sin_ref,
    q_ref, k_ref, v_ref, gmix_ref, raw_ref, inv_ref, exp_ref, gmid_ref,
    gx_ref, gw_ref, small_ref, w_t, g_t,
):
    length = x_ref.shape[1]
    seq, group = pl.program_id(0), pl.program_id(1)

    @pl.when((seq == 0) & (group == 0))
    def _():
        for j in range(3):
            w_t[pl.ds(j * D, D), :] = matrix(w_ref, j).T
        gw_ref[...] = jnp.zeros_like(gw_ref)
        small_ref[...] = jnp.zeros_like(small_ref)

    limit = lens[seq]
    scale = 1.0 / math.sqrt(HEAD)
    low_edge = 0
    for extent in key_extents(length):

        @pl.when((limit > low_edge) & (limit <= extent))
        def _(extent=extent):
            cosine, sine = cos_ref[...], sin_ref[...]
            start = pl.multiple_of(group * 128, 128)
            if extent < length:
                for j in (1, 2):
                    g_t[pl.ds(start + j * D, 128), extent:length] = jnp.zeros(
                        (128, length - extent), BF
                    )

            def back_turn(w, c, s):
                first, second = w[:HALF], w[HALF:]
                return jnp.concatenate(
                    [first * c + second * s, second * c - first * s], axis=0
                ).astype(BF)

            for h in range(4):
                at = slice(h * HEAD, (h + 1) * HEAD)
                row = start + h * HEAD
                query, key = q_ref[0, at], k_ref[0, at, 0:extent]
                exponent = exp_ref[0, h, 0:extent]
                inverse = inv_ref[0, 0, h : h + 1]
                grad_mixed = (gmix_ref[0, at].astype(F32) * inverse).astype(BF)
                inner = jnp.sum(
                    raw_ref[0, at] * grad_mixed.astype(F32), axis=0, keepdims=True
                )
                grad_probs = dot_tn(v_ref[0, at, 0:extent], grad_mixed)
                grad_scores = (exponent.astype(F32) * (grad_probs - inner)).astype(BF)
                grad_value = dot_nt(grad_mixed, exponent)
                grad_key = dot_nt(query, grad_scores)
                grad_query = dot_nn(key, grad_scores) * scale
                g_t[pl.ds(row, HEAD), :] = back_turn(grad_query, cosine, sine)
                g_t[pl.ds(row + D, HEAD), 0:extent] = back_turn(
                    grad_key, cosine[:, 0:extent], sine[:, 0:extent]
                )
                g_t[pl.ds(row + 2 * D, HEAD), 0:extent] = grad_value.astype(BF)

        low_edge = extent

    @pl.when(group == pl.num_programs(1) - 1)
    def _():
        whitened, inverse = whiten(x_ref[0].astype(F32))
        gain = rows_ref[0:1, :]
        hidden = (whitened * gain + rows_ref[2:3, :]).astype(BF)
        hidden_t = hidden.T
        grads = g_t[...]
        ones = jnp.ones((8, length), BF)
        grad_hidden = dot_tn(grads, w_t[...])
        for j in range(3):
            part = grads[j * D : (j + 1) * D]
            small_ref[2 + j : 3 + j, :] += dot_nt(ones, part)[0:1]
            gw_ref[pl.ds(j * D, D), :] += dot_nt(hidden_t, part)
        small_ref[0:1, :] += jnp.sum(grad_hidden * whitened, axis=0, keepdims=True)
        small_ref[1:2, :] += jnp.sum(grad_hidden, axis=0, keepdims=True)
        gx_ref[0] = gmid_ref[0] + whiten_back(grad_hidden, whitened, inverse, gain)


def feed_forward(
    layers,
    x_ref, mix_ref, wo_ref, rows_ref, cot_ref, u_ref, v_ref, fbias_ref,
    head_ref, label_ref, flag_ref, lens,
    out_ref, gmid_ref, gmix_ref, gffn_ref, gfb_ref, gwo_ref, small_ref, late_ref,
    middle, lefts, totals, lows, x_buf, mix_buf, cot_buf, copied, *comm,
):
    seqs, length = x_ref.shape[0], x_ref.shape[1]
    pad = lefts.shape[1] // seqs
    step = pl.program_id(0)
    last = pl.num_programs(0) - 1
    chunk = lows.shape[2]

    def moves(pairs, first, s):
        return [
            pltpu.make_async_copy(a.at[s], b.at[s], copied.at[first + i, s])
            for i, (a, b) in enumerate(pairs)
        ]

    arrivals = functools.partial(
        moves, ((mix_ref, mix_buf), (x_ref, x_buf), (cot_ref, cot_buf)), 0
    )
    leavings = functools.partial(
        moves, ((mix_buf, gmix_ref), (x_buf, out_ref), (middle, gmid_ref)), 3
    )

    def rows_of(s, count):
        return pl.ds(pl.multiple_of(s * pad, 16), count)

    if layers:
        me = position()
        terms, weights, w_send, w_recv, w_local = comm[:5]
        comm = comm[5:]
        spot = (me["z"], me["x"], me["y"], me["c"])
        chunks = weights.shape[1]
        late = range(EARLY, chunks)
        loads = [
            pltpu.make_async_copy(u_ref.at[j], weights.at[j, 0:EARLY], w_local.at[j])
            for j in range(2)
        ]
        own = [
            pltpu.make_async_copy(
                v_ref.at[j, k * ROWS : (k + 1) * ROWS], weights.at[(j, k) + spot],
                w_local.at[2 + j * chunks + k],
            )
            for j in range(2)
            for k in late
        ]
        gathers = {
            k: [
                PieceGather(
                    me, layers, weights.at[j, k], (), w_send.at[k, j], w_recv.at[k, j], "xy"[j]
                )
                for j in range(2)
            ]
            for k in late
        }

        def gather(stage, *which):
            for k in which:
                for piece in gathers[k]:
                    if stage < 4:
                        piece.advance(stage)
                    else:
                        piece.wait(3)

        farewell = [
            pltpu.make_async_copy(terms.at[j], late_ref.at[j], w_local.at[j]) for j in range(2)
        ]

        def pieces(k):
            slot = lax.rem(k, 2) * 2
            return [PieceReduce(me, layers, comm, slot + j, "yx"[j]) for j in range(2)]

        def getter(j):
            def get(i, core):
                at = (i * 2 + core) * ROWS
                return terms[j, pl.ds(pl.multiple_of(at, ROWS), ROWS), :]

            return get

        def over_first(k):
            for j, op in enumerate(pieces(k)):
                op.over_first(getter(j))

        def over_second(k):
            for op in pieces(k):
                op.over_second()

        def over_layers(k):
            for op in pieces(k):
                op.over_layers()

        def finish(k):
            rows = pl.ds(pl.multiple_of(k * ROWS, ROWS), ROWS)
            for j, op in enumerate(pieces(k)):
                gffn_ref[j, rows, :] = op.finish()

    def later(stage, delay):
        if layers:
            pl.when(step >= delay)(lambda: stage(step - delay))

    def at_step(k, *args):
        if layers:
            pl.when(step == k)(functools.partial(gather, *args))

    @pl.when(step == 0)
    def _():
        for s in range(seqs):
            for copy in arrivals(s):
                copy.start()
        if layers:
            greet(me, layers)
            for copy in own + loads:
                copy.start()
            for copy in own:
                copy.wait()
            meet(layers)
            for k in late:
                for piece in gathers[k]:
                    piece.start(0)
        blank = jnp.zeros((pad - length, D), BF)

        @pl.loop(0, seqs)
        def _(s):
            for copy in arrivals(s):
                copy.wait()
            branch = dot_tn(mix_buf[s], matrix(wo_ref, 0)) + rows_ref[7:8, :]
            mid = x_buf[s].astype(F32) + branch
            middle[s] = mid
            whitened, _ = whiten(mid)
            low = (whitened * rows_ref[1:2, :] + rows_ref[3:4, :]).astype(BF)
            lefts[0, rows_of(s, pad), :] = jnp.concatenate([low, blank], axis=0)
            lefts[1, rows_of(s, pad), :] = jnp.concatenate([cot_buf[s], blank], axis=0)
            if layers:
                pl.when(s == 1)(lambda: gather(1, 2))

        totals[...] = jnp.zeros_like(totals)
        gfb_ref[...] = jnp.zeros_like(gfb_ref)
        if layers:
            for copy in loads:
                copy.wait()
            gather(1, 3)

    def weight(j):
        if layers:
            return weights[j, step].reshape(chunk, D)
        return (u_ref, v_ref)[j][0]

    if layers:
        fbias = rows_ref[pl.ds(9 + step, 1), 0:chunk]
    else:
        fbias = fbias_ref[step]

    def block(s, total):
        rows = rows_of(s, pad)
        upward = dot_nt(lefts[0, rows, :], weight(0)) + fbias
        grad_act = dot_nt(lefts[1, rows, :], weight(1))
        phi = 0.5 * (1.0 + lax.erf(upward * ROOT_HALF))
        act = (upward * phi).astype(BF)
        slope = phi + upward * jnp.exp(-0.5 * upward * upward) * INV_ROOT_TWO_PI
        grad_up = (grad_act * slope).astype(BF)
        lows[0, rows, :] = grad_up
        lows[1, rows, :] = act
        totals[0, rows, :] += dot_nn(grad_up, weight(0))
        totals[1, rows, :] += dot_nn(act, weight(1))
        if layers:

            @pl.when(s == 1)
            def _():
                at_step(0, 2, 2)
                at_step(0, 1, 4)
                at_step(1, 4, 2)
                at_step(2, 4, 3, 4)
                later(over_first, 1)
                later(over_layers, 2)

        return total + jnp.sum(grad_up.astype(F32), axis=0, keepdims=True)

    total = lax.fori_loop(0, seqs, block, jnp.zeros_like(fbias))
    gfb_ref[step, :, 0:chunk] = total

    for j in range(2):
        product = dot_tn(lows[j], lefts[j])
        if layers:
            terms[j] = product
        else:
            gffn_ref[j, 0] = product

    if layers:

        @pl.when(step < last)
        def _():
            for j, op in enumerate(pieces(step)):
                op.over_cores(getter(j))

        @pl.when(step == last)
        def _():
            for copy in farewell:
                copy.start()

        at_step(0, 3, 2)
        at_step(0, 2, 3, 4)
        at_step(1, 3, 3, 4)
        later(over_second, 1)
        later(finish, 2)

    @pl.when(step == last)
    def _():
        gain = rows_ref[1:2, :]
        gwo_ref[...] = jnp.zeros_like(gwo_ref)

        def sequence(s, sums):
            gain_sum, shift_sum, branch_sum, cot_sum, loglik, hits = sums
            rows = rows_of(s, length)
            mid = middle[s]
            final = mid + (totals[1, rows, :] + rows_ref[8:9, :])
            x_buf[s] = final.astype(BF)
            unit, _ = whiten(final)
            logits = dot_nt(head_ref[...], unit.astype(BF))
            slot = lax.broadcasted_iota(jnp.int32, logits.shape, 0)
            shifted = logits - jnp.max(logits, axis=0, keepdims=True)
            logprob = shifted - jnp.log(jnp.sum(jnp.exp(shifted), axis=0, keepdims=True))
            picked = jnp.sum(
                jnp.where(slot == label_ref[pl.ds(s, 1), :], logprob, 0.0), axis=0, keepdims=True
            )
            spots = lax.broadcasted_iota(jnp.int32, (1, length), 1)
            live = (flag_ref[pl.ds(s, 1), :] == 1) & (spots < lens[s])

            gradient = totals[0, rows, :]
            whitened, inverse = whiten(mid)
            own = cot_buf[s].astype(F32)
            grad_mid = own + whiten_back(gradient, whitened, inverse, gain)
            middle[s] = grad_mid
            low = grad_mid.astype(BF)
            gwo_ref[...] += dot_nn(mix_buf[s], low)
            mix_buf[s] = dot_nt(matrix(wo_ref, 0), low).astype(BF)
            for copy in leavings(s):
                copy.start()
            if layers:
                pl.when(s == 0)(lambda: over_layers(last - 1))
                pl.when(s == seqs - 1)(lambda: finish(last - 1))
            return (
                gain_sum + jnp.sum(gradient * whitened, axis=0, keepdims=True),
                shift_sum + jnp.sum(gradient, axis=0, keepdims=True),
                branch_sum + jnp.sum(low.astype(F32), axis=0, keepdims=True),
                cot_sum + jnp.sum(own, axis=0, keepdims=True),
                loglik + jnp.where(live, picked, 0.0),
                hits + jnp.where(live, jnp.exp(picked), 0.0),
            )

        blanks = [jnp.zeros((1, D), F32)] * 4 + [jnp.zeros((1, length), F32)] * 2
        gain_sum, shift_sum, branch_sum, cot_sum, loglik, hits = lax.fori_loop(
            0, seqs, sequence, tuple(blanks)
        )
        small_ref[0:1, :] = gain_sum
        small_ref[1:2, :] = shift_sum
        small_ref[2:3, :] = branch_sum
        small_ref[3:4, :] = cot_sum
        small_ref[4:8, :] = jnp.zeros((4, D), F32)
        small_ref[4:5, 0:128] = jnp.broadcast_to(
            jnp.sum(loglik, axis=1, keepdims=True), (1, 128)
        )
        small_ref[4:5, 128:256] = jnp.broadcast_to(
            jnp.sum(hits, axis=1, keepdims=True), (1, 128)
        )
        for s in range(seqs):
            for copy in leavings(s):
                copy.wait()
        if layers:
            for copy in farewell:
                copy.wait()


def whole(shape):
    return pl.BlockSpec(shape, lambda *_: (0,) * len(shape), pipeline_mode=pl.Buffered(1))


def block_of(shape, *index):
    return pl.BlockSpec(shape, lambda *_: index, pipeline_mode=pl.Buffered(1))


def leading(shape):
    return pl.BlockSpec((1,) + tuple(shape[1:]), lambda i, *_: (i,) + (0,) * (len(shape) - 1))


def shaped(shape, dtype=F32):
    return jax.ShapeDtypeStruct(shape, dtype)


def projections(attn, first, count):
    blocks = attn.shape[0] // 4
    rows = D // blocks
    return block_of((blocks * count, rows, D), first // count, 0, 0)


def attention_forward(lengths, tokens, rows_all, attn, ffn, cosine, sine, layers):
    seqs, length, _ = tokens.shape
    heads = HEADS // 4
    flat = (seqs, D, length)
    inverse = (seqs, heads, 4, length)
    exponent = (seqs, HEADS, length, length)

    def part(block):
        return pl.BlockSpec(block, lambda g, s, *_: (s, g, 0, 0)[: len(block)])

    out_specs = [part((1, 128, length))] * 5
    out_specs += [part((1, 1, 4, length)), part((1, 4, length, length))]
    out_shape = [shaped(flat, BF)] * 4 + [shaped(flat), shaped(inverse), shaped(exponent, BF)]
    scratch = [
        pltpu.VMEM((seqs, length, D), BF), pltpu.VMEM((384, D), BF), pltpu.VMEM((D, 16), F32),
        pltpu.VMEM((seqs, length, D), F32),
    ]
    hbm = pl.BlockSpec(memory_space=pl.ANY)
    params = dict(vmem_limit_bytes=VMEM_LIMIT)
    if layers:
        chips = (layers, 2, 2, 2)
        owned = attn.shape[0]
        early = (2, EARLY) + chips + (ROWS, D)
        out_specs += [whole((16, D)), hbm, hbm]
        out_shape += [
            shaped((16, D)), shaped(chips + (owned, D), BF),
            shaped(early, BF),
        ]
        scratch += [
            pltpu.VMEM(chips + (owned + 16, D), BF), pltpu.VMEM(early, BF),
            pltpu.SemaphoreType.DMA((10, 3 + layers)), pltpu.SemaphoreType.DMA((10, 3 + layers)),
            pltpu.SemaphoreType.DMA((3 + 2 * EARLY,)),
        ]
        params.update(collective_id=2, has_side_effects=True)
        sources = [hbm, hbm, hbm]
    else:
        sources = [whole(rows_all.shape), whole(attn.shape), hbm]
    return pl.pallas_call(
        functools.partial(forward_attention, layers),
        grid_spec=pltpu.PrefetchScalarGridSpec(
            num_scalar_prefetch=1,
            grid=(heads, seqs),
            in_specs=[whole(tokens.shape)] + sources + [whole(cosine.shape), whole(sine.shape)],
            out_specs=out_specs,
            scratch_shapes=scratch,
        ),
        out_shape=out_shape,
        compiler_params=pltpu.CompilerParams(**params),
        name="attention_forward",
    )(lengths, tokens, rows_all, attn, ffn, cosine, sine)


def attention_backward(
    lengths, tokens, attn, rows_all, cosine, sine, query, key, value, grad_mixed, raw,
    inverse, exponent, grad_middle,
):
    seqs, length, _ = tokens.shape

    def part(block):
        return pl.BlockSpec(block, lambda s, g, *_: (s, g, 0, 0)[: len(block)])

    return pl.pallas_call(
        backward_attention,
        grid_spec=pltpu.PrefetchScalarGridSpec(
            num_scalar_prefetch=1,
            grid=(seqs, HEADS // 4),
            in_specs=[
                leading(tokens.shape), projections(attn, 0, 3), whole(rows_all.shape),
                whole(cosine.shape), whole(sine.shape),
            ]
            + [part((1, 128, length))] * 5
            + [part((1, 1, 4, length)), part((1, 4, length, length)), leading(tokens.shape)],
            out_specs=[leading(tokens.shape), whole((3 * D, D)), whole((8, D))],
            scratch_shapes=[pltpu.VMEM((3 * D, D), BF), pltpu.VMEM((3 * D, length), BF)],
        ),
        out_shape=[shaped(tokens.shape), shaped((3 * D, D)), shaped((8, D))],
        compiler_params=pltpu.CompilerParams(vmem_limit_bytes=VMEM_LIMIT),
        name="attention_backward",
    )(
        lengths, tokens, attn, rows_all, cosine, sine, query, key, value, grad_mixed, raw,
        inverse, exponent, grad_middle,
    )


def feed_forward_both(
    tokens, mixed, attn, rows_all, cotangent, ffn, fbias, head, labels, flags, lengths, layers,
):
    seqs, length, _ = tokens.shape
    pad = (length + 15) // 16 * 16
    rows = seqs * pad
    steps, chunk = fbias.shape
    hbm = pl.BlockSpec(memory_space=pl.ANY)
    if layers:
        ups, downs = ffn
        up_spec = down_spec = hbm
        owned = downs.shape[1]
        grad_spec, grad_shape = whole((2, owned - ROWS, D)), shaped((2, owned - ROWS, D))
        late_shape = (2, chunk, D)
        chips = (layers, 2, 2, 2)
        extra = [
            pltpu.VMEM(late_shape, F32), pltpu.VMEM((2, steps) + chips + (ROWS, D), BF),
            pltpu.SemaphoreType.DMA((steps, 2, 2 + layers)),
            pltpu.SemaphoreType.DMA((steps, 2, 2 + layers)),
            pltpu.SemaphoreType.DMA((2 + 2 * steps,)),
        ]
        extra += reduce_scratch(4, layers)
    else:
        chunked = (steps, chunk, D)
        ups, downs = ffn[0].reshape(chunked), ffn[1].reshape(chunked)
        up_spec = down_spec = leading(chunked)
        grad_spec = pl.BlockSpec((2, 1, chunk, D), lambda k: (0, k, 0, 0))
        grad_shape = shaped((2,) + chunked)
        late_shape = (8, 128)
        extra = []
    return pl.pallas_call(
        functools.partial(feed_forward, layers),
        grid=(steps,),
        in_specs=[
            hbm, hbm, projections(attn, 3, 1), whole(rows_all.shape), hbm, up_spec, down_spec,
            whole((steps, 1, chunk)), whole(head.shape), whole(labels.shape),
            whole(flags.shape), pl.BlockSpec(memory_space=pltpu.SMEM),
        ],
        out_specs=[
            hbm, hbm, hbm, grad_spec, whole((8, 1, D)), whole((D, D)), whole((8, D)), hbm,
        ],
        out_shape=[
            shaped(tokens.shape, BF), shaped(tokens.shape), shaped(mixed.shape, BF),
            grad_shape, shaped((8, 1, D)), shaped((D, D)), shaped((8, D)), shaped(late_shape),
        ],
        scratch_shapes=[
            pltpu.VMEM(tokens.shape, F32),
            pltpu.VMEM((2, rows, D), BF),
            pltpu.VMEM((2, rows, D), F32),
            pltpu.VMEM((2, rows, chunk), BF),
            pltpu.VMEM(tokens.shape, BF),
            pltpu.VMEM(mixed.shape, BF),
            pltpu.VMEM(tokens.shape, BF),
            pltpu.SemaphoreType.DMA((6, seqs)),
        ]
        + extra,
        compiler_params=pltpu.CompilerParams(
            vmem_limit_bytes=VMEM_LIMIT, **(dict(collective_id=0, has_side_effects=True) if layers else {})
        ),
        name="feed_forward",
    )(
        tokens, mixed, attn, rows_all, cotangent, ups, downs,
        fbias.reshape(steps, 1, chunk), head, labels, flags, lengths,
    )


def own_sums(owner, row_count, sums_ref, gains_ref, biases_ref, units_ref, stats_ref):
    sums = sums_ref[...]
    shard, width = gains_ref.shape[1], sums.shape[1]
    wide, device = owner[0], owner[1]
    local = pltpu.roll(sums[0:16], lax.rem(width - wide * shard, width), axis=1)
    gains_ref[...] = local[0:2, 0:shard]
    biases_ref[...] = local[2:9, 0:shard]
    hidden = sums[16:24]
    lane = lax.broadcasted_iota(jnp.int32, (1, width), 1)
    total = jnp.zeros((1, width), F32)
    for k in range(units_ref.shape[1] // ROWS):
        moved = pltpu.roll(hidden, lax.rem(width + k * ROWS - device * ROWS, width), axis=1)
        mine = (lane >= k * ROWS) & (lane < (k + 1) * ROWS)
        total += jnp.where(mine, moved[k : k + 1], 0.0)
    units_ref[...] = total[:, 0 : units_ref.shape[1]]
    first = lax.broadcasted_iota(jnp.int32, (1, 2), 1) == 0
    both = jnp.where(first, sums[9:10, 0:1], sums[9:10, 128:129] * float(VOCAB))
    stats_ref[...] = both / row_count


def split_sums(sums, wide, device, shard, units, row_count):
    vmem = pl.BlockSpec(memory_space=pltpu.VMEM)
    gains, biases, hidden, stats = pl.pallas_call(
        lambda owner, *refs: own_sums(owner, row_count, *refs),
        in_specs=[pl.BlockSpec(memory_space=pltpu.SMEM), vmem],
        out_specs=[vmem] * 4,
        out_shape=[
            shaped((2, shard)), shaped((7, shard)), shaped((1, units)), shaped((1, 2)),
        ],
        name="own_sums",
    )(jnp.stack([wide, device]).astype(jnp.int32), sums)
    return gains, biases, hidden.reshape(units), stats.reshape(2)


def reduce_tail(grad_qkv, grad_wo, late, part, small_one, small_two, units, layers):
    owned = grad_wo.shape[1]
    pieces = 2 + owned // ROWS
    devices = grad_qkv.shape[0] + grad_wo.shape[0]
    hbm, vmem = pl.BlockSpec(memory_space=pl.ANY), pl.BlockSpec(memory_space=pltpu.VMEM)
    return pl.pallas_call(
        functools.partial(gradient_tail, layers),
        in_specs=[hbm] * 3 + [vmem] * 4,
        out_specs=[vmem] * 3,
        out_shape=[shaped((owned, D)), shaped((2, owned, D)), shaped((24, D))],
        scratch_shapes=[
            pltpu.VMEM((pieces, devices, ROWS, D), F32),
            pltpu.SemaphoreType.DMA((pieces, 2)),
            pltpu.VMEM((4, 24, D), F32),
            pltpu.VMEM((3 + layers, 24, D), F32),
            pltpu.SemaphoreType.DMA((2 + layers,)),
            pltpu.SemaphoreType.DMA((2 + layers,)),
        ]
        + reduce_scratch(pieces, layers),
        compiler_params=pltpu.CompilerParams(
            vmem_limit_bytes=VMEM_LIMIT, collective_id=1, has_side_effects=True
        ),
        name="gradient_tail",
    )(grad_qkv, grad_wo, late.reshape(2, devices, ROWS, D), part, small_one, small_two, units)


def per_device(
    tokens, lengths, masked_flags, labels, attn_weights, ffn_weights, ffn_bias, norm_gains,
    biases, head_weight, cotangent,
):
    both = ("wide", "narrow")
    seqs, length, _ = tokens.shape
    wide, narrow = lax.axis_size("wide"), lax.axis_size("narrow")
    devices = wide * narrow
    shard, units = D // wide, ffn_bias.shape[0]
    owned = attn_weights.shape[0]
    layers = 4 if (wide, narrow) == (8, 4) and owned == units and owned % ROWS == 0 else 0
    at = lax.axis_index("wide")
    owner = at * narrow + lax.axis_index("narrow")
    first = (lax.axis_index("narrow") == 0).astype(BF)
    own = jnp.concatenate([norm_gains, biases], axis=0) * first
    rows_own = lax.dynamic_update_slice(jnp.zeros((16, D), BF), own, (0, at * shard))
    if layers:
        rows_own = lax.dynamic_update_slice(
            rows_own, ffn_bias.reshape(-1, ROWS), (9, owner * ROWS)
        )
    else:
        flat = lax.dynamic_update_slice(jnp.zeros((4 * D,), BF), ffn_bias, (owner * units,))
        rows_own = rows_own + jnp.pad(flat.reshape(4, D), ((9, 3), (0, 0)))
    cosine, sine = rotary_tables(length)
    if layers:
        rows_all, attn, ffn = rows_own, attn_weights, ffn_weights
    else:
        attn = lax.all_gather(attn_weights, both, axis=0, tiled=True).reshape(4, D, D)
        ffn = lax.all_gather(ffn_weights, both, axis=1, tiled=True)
        rows_all = lax.psum(rows_own.astype(F32), both)
    query, key, value, mixed, raw, inverse, exponent, *gathered = attention_forward(
        lengths, tokens, rows_all, attn, ffn, cosine, sine, layers
    )
    if layers:
        rows_all, attn, ffn = gathered
        attn = attn.reshape(devices, owned, D)
        ffn = (ffn, ffn_weights)
        unit_bias = jnp.zeros((units // ROWS, devices * ROWS), F32)
    else:
        unit_bias = rows_all[9:13].reshape(-1, 512)
    (
        output, grad_middle, grad_mixed, grad_ffn, unit_sums, grad_wo, small_two, late,
    ) = feed_forward_both(
        tokens, mixed, attn, rows_all, cotangent, ffn, unit_bias, head_weight.T, labels,
        masked_flags, lengths, layers,
    )
    if not layers:
        grad_ffn = lax.psum_scatter(
            grad_ffn.reshape(2, -1, D), both, scatter_dimension=1, tiled=True
        )
    grad_tokens, grad_qkv, small_one = attention_backward(
        lengths, tokens, attn, rows_all, cosine, sine, query, key, value, grad_mixed, raw,
        inverse, exponent, grad_middle,
    )
    steps, chunk = unit_bias.shape
    if layers:
        blocks = (-1, owned, D)
        grad_attn, grad_ffn, sums = reduce_tail(
            grad_qkv.reshape(blocks), grad_wo.reshape(blocks), late, grad_ffn, small_one,
            small_two, unit_sums, layers,
        )
        grad_gains, grad_biases, grad_ffn_bias, head_stats = split_sums(
            sums, at, owner, shard, units, float(seqs * length * devices)
        )
    else:
        grad_attn = lax.psum_scatter(
            jnp.concatenate([grad_qkv, grad_wo], axis=0), both, scatter_dimension=0, tiled=True
        )
        sums = jnp.concatenate(
            [
                small_one[0:1], small_two[0:1], small_one[1:2], small_two[1:2], small_one[2:5],
                small_two[2:5], jnp.zeros((6, D), F32), unit_sums[:, 0],
            ],
            axis=0,
        )
        sums = lax.psum(sums, both)
        grad_ffn_bias = lax.dynamic_slice_in_dim(
            sums[16:, :chunk].reshape(-1), owner * units, units, 0
        )
        grad_gains = lax.dynamic_slice(sums, (0, at * shard), (2, shard))
        grad_biases = lax.dynamic_slice(sums, (2, at * shard), (7, shard))
        head_stats = (
            sums[9, 0:256:128] * jnp.array([1.0, VOCAB], F32) / (seqs * length * devices)
        )
    return (
        output, grad_tokens, grad_attn, grad_ffn, grad_ffn_bias, grad_gains, grad_biases,
        head_stats,
    )


def solution(mesh):
    both = ("wide", "narrow")
    return jax.shard_map(
        per_device,
        mesh=mesh,
        in_specs=(
            P(both, None, None),
            P(both),
            P(both, None),
            P(both, None),
            P(both, None),
            P(None, both, None),
            P(both),
            P(None, "wide"),
            P(None, "wide"),
            P(),
            P(both, None, None),
        ),
        out_specs=(
            P(both, None, None),
            P(both, None, None),
            P(both, None),
            P(None, both, None),
            P(both),
            P(None, "wide"),
            P(None, "wide"),
            P(),
        ),
        check_vma=False,
    )
```

```python
import functools
import math

import jax
import jax.numpy as jnp
import numpy as np
from jax import lax
from jax.experimental import pallas as pl
from jax.experimental.pallas import tpu as pltpu
from jax.sharding import PartitionSpec as P

D = 640
HEADS = 20
HEAD = 32
HALF = HEAD // 2
VOCAB = 33
EPS = 1e-05
ROOT_HALF = 0.7071067811865476
INV_ROOT_TWO_PI = 0.3989422804014327
BF = jnp.bfloat16
F32 = jnp.float32
VMEM_LIMIT = 60 << 20

MESH = pl.DeviceIdType.MESH
ROWS = 16


def position():
    wide, narrow = lax.axis_index("wide"), lax.axis_index("narrow")
    return {
        "z": lax.div(wide, 2), "x": lax.rem(wide, 2),
        "y": lax.div(narrow, 2), "c": lax.rem(narrow, 2),
    }


def partner(me, axis, offset, size):
    there = dict(me)
    there[axis] = lax.rem(me[axis] + offset, size)
    return (there["z"] * 2 + there["x"], there["y"] * 2 + there["c"])


def across(me):
    return partner({**me, "x": 1 - me["x"]}, "y", 1, 2)


def greet(me, layers, corner=False):
    barrier = pltpu.get_barrier_semaphore()
    peers = [partner(me, axis, 1, 2) for axis in "cyx"]
    peers += [partner(me, "z", offset, layers) for offset in range(1, layers)]
    if corner:
        peers.append(across(me))
    for peer in peers:
        pl.semaphore_signal(barrier, inc=1, device_id=peer, device_id_type=MESH)


def meet(layers, corner=False):
    pl.semaphore_wait(pltpu.get_barrier_semaphore(), 2 + layers + corner)


def reduce_scratch(slots, layers):
    def blocks(count, dtype):
        return pltpu.VMEM((slots, count, ROWS, D), dtype)

    return [
        blocks(4 * layers, BF), blocks(4 * layers, BF),
        blocks(2 * layers, BF), blocks(2 * layers, BF), blocks(2 * layers, F32),
        blocks(layers, BF), blocks(layers, BF), blocks(layers, F32),
        blocks(layers, BF), blocks(layers, BF), blocks(1, F32),
        pltpu.SemaphoreType.DMA((slots, 3 + layers)),
        pltpu.SemaphoreType.DMA((slots, 3 + layers)),
    ]


class PieceReduce:
    def __init__(self, me, layers, refs, slot, first):
        (
            self.s0, self.r0, self.s1, self.r1, self.k1, self.s2, self.r2, self.k2,
            self.s3, self.r3, self.k3,
        ) = (ref.at[slot] for ref in refs[:11])
        self.send, self.recv = (ref.at[slot] for ref in refs[11:])
        self.me, self.layers = me, layers
        self.first, self.second = ("y", "x") if first == "y" else ("x", "y")

    def exchange(self, stage, source, target, axis):
        return pltpu.make_async_remote_copy(
            src_ref=source, dst_ref=target, send_sem=self.send.at[stage],
            recv_sem=self.recv.at[stage], device_id=partner(self.me, axis, 1, 2),
            device_id_type=MESH,
        )

    def layer_copies(self):
        me, layers = self.me, self.layers
        return [
            pltpu.make_async_remote_copy(
                src_ref=self.s3.at[lax.rem(me["z"] + offset, layers)],
                dst_ref=self.r3.at[offset], send_sem=self.send.at[2 + offset],
                recv_sem=self.recv.at[2 + offset],
                device_id=partner(me, "z", offset, layers), device_id_type=MESH,
            )
            for offset in range(1, layers)
        ]

    def rest(self, along, other):
        return other * 2 + along if self.first == "y" else along * 2 + other

    def over_cores(self, get):
        core = self.me["c"]

        @pl.loop(0, 4 * self.layers)
        def _(i):
            self.s0[i] = get(i, 1 - core).astype(BF)

        self.exchange(0, self.s0, self.r0, "c").start()

    def over_first(self, get):
        self.exchange(0, self.s0, self.r0, "c").wait()
        core, along = self.me["c"], self.me[self.first]

        @pl.loop(0, self.layers)
        def _(layer):
            for other in range(2):
                away = layer * 4 + self.rest(1 - along, other)
                near = layer * 4 + self.rest(along, other)
                at = layer * 2 + other
                self.s1[at] = (get(away, core) + self.r0[away].astype(F32)).astype(BF)
                self.k1[at] = get(near, core) + self.r0[near].astype(F32)

        self.exchange(1, self.s1, self.r1, self.first).start()

    def over_second(self):
        self.exchange(1, self.s1, self.r1, self.first).wait()
        along = self.me[self.second]

        @pl.loop(0, self.layers)
        def _(layer):
            away, near = layer * 2 + (1 - along), layer * 2 + along
            self.s2[layer] = (self.k1[away] + self.r1[away].astype(F32)).astype(BF)
            self.k2[layer] = self.k1[near] + self.r1[near].astype(F32)

        self.exchange(2, self.s2, self.r2, self.second).start()

    def over_layers(self):
        self.exchange(2, self.s2, self.r2, self.second).wait()
        own = self.me["z"]

        @pl.loop(0, self.layers)
        def _(layer):
            self.s3[layer] = (self.k2[layer] + self.r2[layer].astype(F32)).astype(BF)

        self.k3[0] = self.k2[own] + self.r2[own].astype(F32)
        for copy in self.layer_copies():
            copy.start()

    def finish(self):
        for copy in self.layer_copies():
            copy.wait()
        total = self.k3[0]
        for offset in range(1, self.layers):
            total = total + self.r3[offset].astype(F32)
        return total


class PieceGather:
    def __init__(self, me, layers, buf, tail, send, recv, first):
        self.me, self.layers, self.buf, self.tail = me, layers, buf, tail
        self.send, self.recv, self.first = send, recv, first

    def view(self, *lead):
        return self.buf.at[lead + self.tail]

    def copy(self, lead, peer, at):
        return pltpu.make_async_remote_copy(
            src_ref=self.view(*lead), dst_ref=self.view(*lead), send_sem=self.send.at[at],
            recv_sem=self.recv.at[at], device_id=peer, device_id_type=MESH,
        )

    def copies(self, stage):
        me, every = self.me, slice(None)
        z, x, y, core = me["z"], me["x"], me["y"], me["c"]
        if stage == 0:
            return [
                self.copy((z, x, y, core), partner(me, "z", offset, self.layers), 2 + offset)
                for offset in range(1, self.layers)
            ]
        if self.first == "xy" and stage < 3:
            if stage == 2:
                return []
            peers = partner(me, "x", 1, 2), partner(me, "y", 1, 2), across(me)
            return [
                self.copy((every, x, y, core), peer, at)
                for peer, at in zip(peers, (0, 1, 2 + self.layers))
            ]
        if stage == 1:
            lead, axis = (every, x, y, core), self.first
        elif stage == 2:
            lead = (every, every, y, core) if self.first == "x" else (every, x, every, core)
            axis = "y" if self.first == "x" else "x"
        else:
            lead, axis = (every, every, every, core), "c"
        return [self.copy(lead, partner(me, axis, 1, 2), stage - 1)]

    def start(self, stage):
        for copy in self.copies(stage):
            copy.start()

    def wait(self, stage):
        for copy in self.copies(stage):
            copy.wait()

    def advance(self, stage):
        self.wait(stage - 1)
        self.start(stage)


class SmallReduce:
    def __init__(self, me, layers, sent, got, send, recv):
        self.me, self.layers = me, layers
        self.sent, self.got, self.send, self.recv = sent, got, send, recv

    def exchange(self, stage):
        return pltpu.make_async_remote_copy(
            src_ref=self.sent.at[stage], dst_ref=self.got.at[stage],
            send_sem=self.send.at[stage], recv_sem=self.recv.at[stage],
            device_id=partner(self.me, "cyx"[stage], 1, 2), device_id_type=MESH,
        )

    def layer_copies(self):
        own = self.me["z"]
        return [
            pltpu.make_async_remote_copy(
                src_ref=self.sent.at[3], dst_ref=self.got.at[3 + own],
                send_sem=self.send.at[2 + offset], recv_sem=self.recv.at[2 + offset],
                device_id=partner(self.me, "z", offset, self.layers), device_id_type=MESH,
            )
            for offset in range(1, self.layers)
        ]

    def start(self, stage):
        if stage:
            self.exchange(stage - 1).wait()
            self.sent[stage] = self.sent[stage - 1] + self.got[stage - 1]
        if stage < 3:
            self.exchange(stage).start()
        else:
            for copy in self.layer_copies():
                copy.start()
            self.got[3 + self.me["z"]] = self.sent[3]

    def finish(self):
        for copy in self.layer_copies():
            copy.wait()
        total = self.got[3]
        for layer in range(1, self.layers):
            total = total + self.got[3 + layer]
        return total


TAIL_ORDER = (
    (0, 0), (1, 0), (2, 0), (7, 0), (3, 0), (4, 0), (0, 1), (1, 1), (7, 1), (5, 0), (6, 0),
    (2, 1), (3, 1), (4, 1), (5, 1), (7, 2), (6, 1), (0, 2), (1, 2), (2, 2), (3, 2), (7, 3),
    (4, 2), (0, 3), (1, 3), (5, 2), (6, 2), (2, 3), (3, 3), (4, 3), (0, 4), (1, 4), (7, 4),
    (5, 3), (6, 3), (2, 4), (3, 4), (4, 4), (5, 4), (6, 4),
)


def gradient_tail(layers, qkv_ref, wo_ref, late_ref, part_ref, one_ref, two_ref, units_ref,
                  grad_ref, gffn_ref, sums_ref, terms, loaded, sent, got, small_send,
                  small_recv, *refs):
    me = position()
    greet(me, layers)
    own, wo = qkv_ref.shape[0], wo_ref.shape[0]
    loads = []
    for p in range(terms.shape[0]):
        if p < 2:
            moves = [(late_ref.at[p], terms.at[p])]
        else:
            rows = slice((p - 2) * ROWS, (p - 1) * ROWS)
            moves = [
                (qkv_ref.at[:, rows], terms.at[p, 0:own]),
                (wo_ref.at[:, rows], terms.at[p, own : own + wo]),
            ]
        loads.append(
            [
                pltpu.make_async_copy(source, target, loaded.at[p, i])
                for i, (source, target) in enumerate(moves)
            ]
        )
        for copy in loads[-1]:
            copy.start()
    order = [(one_ref, 0), (two_ref, 0), (one_ref, 1), (two_ref, 1)]
    order += [(one_ref, 2), (one_ref, 3), (one_ref, 4), (two_ref, 2), (two_ref, 3), (two_ref, 4)]
    sent[0, 8:16] = jnp.zeros((8, D), F32)
    for row, (ref, at) in enumerate(order):
        sent[0, row : row + 1] = ref[at : at + 1]
    for k in range(8):
        sent[0, 16 + k : 17 + k] = units_ref[k]
    small = SmallReduce(me, layers, sent, got, small_send, small_recv)
    ops = [PieceReduce(me, layers, refs, p, "yx"[p % 2]) for p in range(terms.shape[0])]
    kept = part_ref.shape[1]
    gffn_ref[:, 0:kept] = part_ref[...]
    meet(layers)

    def getter(p):
        return lambda i, core: terms[p, i * 2 + core]

    for p, stage in TAIL_ORDER:
        if p == len(ops):
            if stage < 4:
                small.start(stage)
            else:
                sums_ref[...] = small.finish()
        elif stage == 0:
            for copy in loads[p]:
                copy.wait()
            ops[p].over_cores(getter(p))
        elif stage == 1:
            ops[p].over_first(getter(p))
        elif stage == 2:
            ops[p].over_second()
        elif stage == 3:
            ops[p].over_layers()
        elif p < 2:
            gffn_ref[p, kept:] = ops[p].finish()
        else:
            grad_ref[(p - 2) * ROWS : (p - 1) * ROWS] = ops[p].finish()


def dot_nn(a, b):
    return lax.dot_general(a, b, (((1,), (0,)), ((), ())), preferred_element_type=F32)


def dot_nt(a, b):
    return lax.dot_general(a, b, (((1,), (1,)), ((), ())), preferred_element_type=F32)


def dot_tn(a, b):
    return lax.dot_general(a, b, (((0,), (0,)), ((), ())), preferred_element_type=F32)


def matrix(ref, j):
    rows = ref.shape[1]
    blocks = D // rows
    return ref[j * blocks : (j + 1) * blocks].reshape(D, D)


def whiten(values):
    center = jnp.mean(values, axis=-1, keepdims=True)
    offset = values - center
    spread = jnp.mean(offset * offset, axis=-1, keepdims=True)
    inverse = lax.rsqrt(spread + EPS)
    return offset * inverse, inverse


def whiten_back(gradient, whitened, inverse, gain):
    scaled = gradient * gain
    mean_grad = jnp.mean(scaled, axis=-1, keepdims=True)
    mean_cross = jnp.mean(scaled * whitened, axis=-1, keepdims=True)
    return inverse * (scaled - mean_grad - whitened * mean_cross)


def rotary_tables(length):
    frequency = (
        np.float32(1.0)
        / np.float32(10000.0) ** (np.arange(HALF, dtype=np.float32) * np.float32(2.0 / HEAD))
    ).astype(np.float32)
    angles = frequency[:, None] * np.arange(length, dtype=np.float32)[None, :]
    return np.cos(angles).astype(np.float32), np.sin(angles).astype(np.float32)


def key_extents(length):
    extents = list(range(256, length, 128))
    return extents + [length]


def halves(values):
    length = values.shape[-1]
    split = values.reshape(values.shape[0] // HEAD, 2, HALF, length)
    return split[:, 0], split[:, 1]


def joined(first, second):
    length = first.shape[-1]
    both = jnp.concatenate([first[:, None], second[:, None]], axis=1)
    return both.reshape(first.shape[0] * HEAD, length)


GATHER_AHEAD = (
    (0, 1), (1, 1), (2, 1), (3, 1), (0, 2), (0, 3), (4, 1), (0, 4),
)
GATHER_FIRST = ((1, 2), (1, 3), (5, 1), (2, 2), (6, 1), (1, 4))
GATHER_AFTER = {
    0: ((7, 1), (3, 2), (8, 1), (4, 2)), 1: ((2, 3), (6, 2), (9, 1), (5, 2)),
    2: ((2, 4), (7, 2), (3, 3), (8, 2)), 3: ((4, 3), (9, 2)), 4: ((5, 3), (6, 3), (3, 4)),
    5: ((7, 3), (8, 3)), 6: ((9, 3),), 7: ((4, 4),), 8: ((5, 4),),
    10: ((6, 4), (7, 4), (8, 4), (9, 4)),
}
EARLY = 2


def forward_attention(
    layers,
    lens, x_ref, rows_ref, w_ref, ffn_ref, cos_ref, sin_ref,
    q_ref, k_ref, v_ref, mix_ref, raw_ref, inv_ref, exp_ref, *rest,
):
    seqs, length = x_ref.shape[0], x_ref.shape[1]
    group, seq = pl.program_id(0), pl.program_id(1)
    step = group * seqs + seq
    if layers:
        all_rows_ref, attn_ref, ffn_all_ref, hidden, w_t, bias_t, white = rest[:7]
        w_all, ffn_all, send, recv, local = rest[7:]
        me = position()
        spot = (me["z"], me["x"], me["y"], me["c"])
        owned = w_all.shape[4] - 16
        every = slice(None)
        tails = [(slice(owned, owned + 16), every)]
        tails += [(slice(0, owned), slice(i * 128, i * 128 + 128)) for i in range(D // 128)]
        pieces = [
            PieceGather(
                me, layers, w_all, tail, send.at[i], recv.at[i], "xy" if i < 2 else "xy"[i % 2]
            )
            for i, tail in enumerate(tails)
        ]
        for k in range(EARLY):
            for j in range(2):
                i = len(pieces)
                pieces.append(
                    PieceGather(
                        me, layers, ffn_all.at[j, k], (), send.at[i], recv.at[i], "xy"[i % 2]
                    )
                )

        def act(actions):
            for piece, stage in actions:
                if stage < 4:
                    pieces[piece].advance(stage)
                else:
                    pieces[piece].wait(3)

        results = [
            pltpu.make_async_copy(w_all.at[:, :, :, :, 0:owned], attn_ref, local.at[0]),
            pltpu.make_async_copy(ffn_all, ffn_all_ref, local.at[1]),
        ]
    else:
        hidden, w_t, bias_t, white = rest

    @pl.when(step == 0)
    def _():
        if layers:
            greet(me, layers, True)
            own = [
                pltpu.make_async_copy(source, w_all.at[spot + (pl.ds(*at),)], local.at[i])
                for i, source, at in ((0, w_ref, (0, owned)), (2, rows_ref, (owned, 16)))
            ]
            own += [
                pltpu.make_async_copy(
                    ffn_ref.at[j, k * ROWS : (k + 1) * ROWS], ffn_all.at[(j, k) + spot],
                    local.at[3 + j * EARLY + k],
                )
                for j in range(2)
                for k in range(EARLY)
            ]
            for copy in own:
                copy.start()
            for copy in own:
                copy.wait()
            meet(layers, True)
            for piece in pieces:
                piece.start(0)
        for s in range(seqs):
            white[s] = whiten(x_ref[s].astype(F32))[0].T
        if layers:
            act(GATHER_AHEAD)
            rows = jnp.zeros((16, D), F32)
            for z in range(layers):
                for i in range(8):
                    rows += w_all[z, i // 4, i // 2 % 2, i % 2, owned : owned + 16].astype(F32)
            all_rows_ref[...] = rows
        else:
            rows = rows_ref[...]
        bias_t[...] = rows.T
        for s in range(seqs):
            hidden[s] = (white[s] * bias_t[:, 0:1] + bias_t[:, 2:3]).astype(BF)
        if layers:
            act(GATHER_FIRST)

    columns = pl.ds(pl.multiple_of(group * 128, 128), 128)

    @pl.when(seq == 0)
    def _():
        for j in range(3):
            if layers:
                block = w_all[j, :, :, :, 0:owned, columns].reshape(D, 128)
            else:
                block = w_ref[j, :, columns]
            w_t[j * 128 : (j + 1) * 128] = block.T

    cosine, sine = cos_ref[...], sin_ref[...]
    scale = 1.0 / math.sqrt(HEAD)
    lin = dot_nn(w_t[...], hidden[seq])
    for j, out_ref in enumerate((q_ref, k_ref, v_ref)):
        part = lin[j * 128 : (j + 1) * 128] + bias_t[columns, 4 + j : 5 + j]
        if j < 2:
            first, second = halves(part)
            part = joined(first * cosine - second * sine, second * cosine + first * sine)
            if j == 0:
                part = part * scale
        out_ref[0] = part.astype(BF)

    spots = lax.broadcasted_iota(jnp.int32, (16, length), 1)
    lead = lax.broadcasted_iota(jnp.int32, (16, length), 0) == 0
    mask = jnp.where(lead & (spots >= lens[seq]), -1e9, 0.0).astype(BF)
    ones = jnp.where(lead, 1.0, 0.0).astype(BF)
    keys = jnp.concatenate([k_ref[0], mask], axis=0).T

    def scored(h):
        blank = jnp.zeros((HEAD, length), BF)
        rows_q = [blank] * 4
        rows_q[h] = q_ref[0, h * HEAD : (h + 1) * HEAD]
        return dot_nn(keys, jnp.concatenate(rows_q + [ones], axis=0))

    def soft(h, scores):
        exponent = jnp.exp(scores - jnp.max(scores, axis=0, keepdims=True))
        inverse = 1.0 / jnp.sum(exponent, axis=0, keepdims=True)
        exponent = exponent.astype(BF)
        exp_ref[0, h] = exponent
        inv_ref[0, 0, h : h + 1] = inverse
        return exponent, inverse

    def mix(h, pair):
        at = slice(h * HEAD, (h + 1) * HEAD)
        mixed = dot_nn(v_ref[0, at], pair[0]) * pair[1]
        raw_ref[0, at] = mixed
        mix_ref[0, at] = mixed.astype(BF)

    ahead = scored(0)
    for h in range(4):
        scores = ahead
        if h < 3:
            ahead = scored(h + 1)
        mix(h, soft(h, scores))

    if layers:
        for after, actions in GATHER_AFTER.items():
            pl.when(step == after)(functools.partial(act, actions))

        @pl.when(step == 8)
        def _():
            results[0].start()

        @pl.when(step == 10)
        def _():
            results[1].start()

        @pl.when(step == 14)
        def _():
            for copy in results:
                copy.wait()


def backward_attention(
    lens, x_ref, w_ref, rows_ref, cos_ref, sin_ref,
    q_ref, k_ref, v_ref, gmix_ref, raw_ref, inv_ref, exp_ref, gmid_ref,
    gx_ref, gw_ref, small_ref, w_t, g_t,
):
    length = x_ref.shape[1]
    seq, group = pl.program_id(0), pl.program_id(1)

    @pl.when((seq == 0) & (group == 0))
    def _():
        for j in range(3):
            w_t[pl.ds(j * D, D), :] = matrix(w_ref, j).T
        gw_ref[...] = jnp.zeros_like(gw_ref)
        small_ref[...] = jnp.zeros_like(small_ref)

    limit = lens[seq]
    scale = 1.0 / math.sqrt(HEAD)
    low_edge = 0
    for extent in key_extents(length):

        @pl.when((limit > low_edge) & (limit <= extent))
        def _(extent=extent):
            cosine, sine = cos_ref[...], sin_ref[...]
            start = pl.multiple_of(group * 128, 128)
            if extent < length:
                for j in (1, 2):
                    g_t[pl.ds(start + j * D, 128), extent:length] = jnp.zeros(
                        (128, length - extent), BF
                    )

            def back_turn(w, c, s):
                first, second = w[:HALF], w[HALF:]
                return jnp.concatenate(
                    [first * c + second * s, second * c - first * s], axis=0
                ).astype(BF)

            values = v_ref[0, :, 0:extent].T
            blank = jnp.zeros((HEAD, length), BF)
            for h in range(4):
                at = slice(h * HEAD, (h + 1) * HEAD)
                row = start + h * HEAD
                query, key = q_ref[0, at], k_ref[0, at, 0:extent]
                exponent = exp_ref[0, h, 0:extent]
                inverse = inv_ref[0, 0, h : h + 1]
                grad_mixed = (gmix_ref[0, at].astype(F32) * inverse).astype(BF)
                inner = jnp.sum(
                    raw_ref[0, at] * grad_mixed.astype(F32), axis=0, keepdims=True
                )
                padded = [blank] * 4
                padded[h] = grad_mixed
                grad_probs = dot_nn(values, jnp.concatenate(padded, axis=0))
                grad_scores = (exponent.astype(F32) * (grad_probs - inner)).astype(BF)
                grad_value = dot_nt(grad_mixed, exponent)
                grad_key = dot_nt(query, grad_scores)
                grad_query = dot_nn(key, grad_scores) * scale
                g_t[pl.ds(row, HEAD), :] = back_turn(grad_query, cosine, sine)
                g_t[pl.ds(row + D, HEAD), 0:extent] = back_turn(
                    grad_key, cosine[:, 0:extent], sine[:, 0:extent]
                )
                g_t[pl.ds(row + 2 * D, HEAD), 0:extent] = grad_value.astype(BF)

        low_edge = extent

    @pl.when(group == pl.num_programs(1) - 1)
    def _():
        whitened, inverse = whiten(x_ref[0].astype(F32))
        gain = rows_ref[0:1, :]
        hidden = (whitened * gain + rows_ref[2:3, :]).astype(BF)
        hidden_t = hidden.T
        grads = g_t[...]
        ones = jnp.ones((8, length), BF)
        grad_hidden = dot_tn(grads, w_t[...])
        for j in range(3):
            part = grads[j * D : (j + 1) * D]
            small_ref[2 + j : 3 + j, :] += dot_nt(ones, part)[0:1]
            gw_ref[pl.ds(j * D, D), :] += dot_nt(hidden_t, part)
        small_ref[0:1, :] += jnp.sum(grad_hidden * whitened, axis=0, keepdims=True)
        small_ref[1:2, :] += jnp.sum(grad_hidden, axis=0, keepdims=True)
        gx_ref[0] = gmid_ref[0] + whiten_back(grad_hidden, whitened, inverse, gain)


def feed_forward(
    layers,
    x_ref, mix_ref, wo_ref, rows_ref, cot_ref, u_ref, v_ref, fbias_ref,
    head_ref, label_ref, flag_ref, lens,
    out_ref, gmid_ref, gmix_ref, gffn_ref, gfb_ref, gwo_ref, small_ref, late_ref,
    middle, lefts, totals, lows, x_buf, mix_buf, cot_buf, copied, *comm,
):
    seqs, length = x_ref.shape[0], x_ref.shape[1]
    pad = lefts.shape[1] // seqs
    step = pl.program_id(0)
    last = pl.num_programs(0) - 1
    chunk = lows.shape[2]

    def moves(pairs, first, s):
        return [
            pltpu.make_async_copy(a.at[s], b.at[s], copied.at[first + i, s])
            for i, (a, b) in enumerate(pairs)
        ]

    arrivals = functools.partial(
        moves, ((mix_ref, mix_buf), (x_ref, x_buf), (cot_ref, cot_buf)), 0
    )
    leavings = functools.partial(
        moves, ((mix_buf, gmix_ref), (x_buf, out_ref), (middle, gmid_ref)), 3
    )

    def rows_of(s, count):
        return pl.ds(pl.multiple_of(s * pad, 16), count)

    if layers:
        me = position()
        terms, weights, w_send, w_recv, w_local = comm[:5]
        comm = comm[5:]
        spot = (me["z"], me["x"], me["y"], me["c"])
        chunks = weights.shape[1]
        late = range(EARLY, chunks)
        loads = [
            pltpu.make_async_copy(u_ref.at[j], weights.at[j, 0:EARLY], w_local.at[j])
            for j in range(2)
        ]
        own = [
            pltpu.make_async_copy(
                v_ref.at[j, k * ROWS : (k + 1) * ROWS], weights.at[(j, k) + spot],
                w_local.at[2 + j * chunks + k],
            )
            for j in range(2)
            for k in late
        ]
        gathers = {
            k: [
                PieceGather(
                    me, layers, weights.at[j, k], (), w_send.at[k, j], w_recv.at[k, j], "xy"[j]
                )
                for j in range(2)
            ]
            for k in late
        }

        def gather(stage, *which):
            for k in which:
                for piece in gathers[k]:
                    if stage < 4:
                        piece.advance(stage)
                    else:
                        piece.wait(3)

        farewell = [
            pltpu.make_async_copy(terms.at[j], late_ref.at[j], w_local.at[j]) for j in range(2)
        ]

        def pieces(k):
            slot = lax.rem(k, 2) * 2
            return [PieceReduce(me, layers, comm, slot + j, "yx"[j]) for j in range(2)]

        def getter(j):
            def get(i, core):
                at = (i * 2 + core) * ROWS
                return terms[j, pl.ds(pl.multiple_of(at, ROWS), ROWS), :]

            return get

        def over_first(k):
            for j, op in enumerate(pieces(k)):
                op.over_first(getter(j))

        def over_second(k):
            for op in pieces(k):
                op.over_second()

        def over_layers(k):
            for op in pieces(k):
                op.over_layers()

        def finish(k):
            rows = pl.ds(pl.multiple_of(k * ROWS, ROWS), ROWS)
            for j, op in enumerate(pieces(k)):
                gffn_ref[j, rows, :] = op.finish()

    def later(stage, delay):
        if layers:
            pl.when(step >= delay)(lambda: stage(step - delay))

    def at_step(k, *args):
        if layers:
            pl.when(step == k)(functools.partial(gather, *args))

    @pl.when(step == 0)
    def _():
        for s in range(seqs):
            for copy in arrivals(s):
                copy.start()
        if layers:
            greet(me, layers)
            for copy in own + loads:
                copy.start()
            for copy in own:
                copy.wait()
            meet(layers)
            for k in late:
                for piece in gathers[k]:
                    piece.start(0)
        blank = jnp.zeros((pad - length, D), BF)

        @pl.loop(0, seqs)
        def _(s):
            for copy in arrivals(s):
                copy.wait()
            branch = dot_tn(mix_buf[s], matrix(wo_ref, 0)) + rows_ref[7:8, :]
            mid = x_buf[s].astype(F32) + branch
            middle[s] = mid
            whitened, _ = whiten(mid)
            low = (whitened * rows_ref[1:2, :] + rows_ref[3:4, :]).astype(BF)
            lefts[0, rows_of(s, pad), :] = jnp.concatenate([low, blank], axis=0)
            lefts[1, rows_of(s, pad), :] = jnp.concatenate([cot_buf[s], blank], axis=0)
            if layers:
                pl.when(s == 1)(lambda: gather(1, 2))

        totals[...] = jnp.zeros_like(totals)
        gfb_ref[...] = jnp.zeros_like(gfb_ref)
        if layers:
            for copy in loads:
                copy.wait()
            gather(1, 3)

    def weight(j):
        if layers:
            return weights[j, step].reshape(chunk, D)
        return (u_ref, v_ref)[j][0]

    if layers:
        fbias = rows_ref[pl.ds(9 + step, 1), 0:chunk]
    else:
        fbias = fbias_ref[step]

    def block(s, total):
        rows = rows_of(s, pad)
        upward = dot_nt(lefts[0, rows, :], weight(0)) + fbias
        grad_act = dot_nt(lefts[1, rows, :], weight(1))
        phi = 0.5 * (1.0 + lax.erf(upward * ROOT_HALF))
        act = (upward * phi).astype(BF)
        slope = phi + upward * jnp.exp(-0.5 * upward * upward) * INV_ROOT_TWO_PI
        grad_up = (grad_act * slope).astype(BF)
        lows[0, rows, :] = grad_up
        lows[1, rows, :] = act
        totals[0, rows, :] += dot_nn(grad_up, weight(0))
        totals[1, rows, :] += dot_nn(act, weight(1))
        if layers:

            @pl.when(s == 1)
            def _():
                at_step(0, 2, 2)
                at_step(0, 1, 4)
                at_step(1, 4, 2)
                at_step(2, 4, 3, 4)
                later(over_first, 1)
                later(over_layers, 2)

        return total + jnp.sum(grad_up.astype(F32), axis=0, keepdims=True)

    total = lax.fori_loop(0, seqs, block, jnp.zeros_like(fbias))
    gfb_ref[step, :, 0:chunk] = total

    for j in range(2):
        product = dot_tn(lows[j], lefts[j])
        if layers:
            terms[j] = product
        else:
            gffn_ref[j, 0] = product

    if layers:

        @pl.when(step < last)
        def _():
            for j, op in enumerate(pieces(step)):
                op.over_cores(getter(j))

        @pl.when(step == last)
        def _():
            for copy in farewell:
                copy.start()

        at_step(0, 3, 2)
        at_step(0, 2, 3, 4)
        at_step(1, 3, 3, 4)
        later(over_second, 1)
        later(finish, 2)

    @pl.when(step == last)
    def _():
        gain = rows_ref[1:2, :]
        gwo_ref[...] = jnp.zeros_like(gwo_ref)

        def sequence(s, sums):
            gain_sum, shift_sum, branch_sum, cot_sum, loglik, hits = sums
            rows = rows_of(s, length)
            mid = middle[s]
            final = mid + (totals[1, rows, :] + rows_ref[8:9, :])
            x_buf[s] = final.astype(BF)
            unit, _ = whiten(final)
            logits = dot_nt(head_ref[...], unit.astype(BF))
            slot = lax.broadcasted_iota(jnp.int32, logits.shape, 0)
            shifted = logits - jnp.max(logits, axis=0, keepdims=True)
            logprob = shifted - jnp.log(jnp.sum(jnp.exp(shifted), axis=0, keepdims=True))
            picked = jnp.sum(
                jnp.where(slot == label_ref[pl.ds(s, 1), :], logprob, 0.0), axis=0, keepdims=True
            )
            spots = lax.broadcasted_iota(jnp.int32, (1, length), 1)
            live = (flag_ref[pl.ds(s, 1), :] == 1) & (spots < lens[s])

            gradient = totals[0, rows, :]
            whitened, inverse = whiten(mid)
            own = cot_buf[s].astype(F32)
            grad_mid = own + whiten_back(gradient, whitened, inverse, gain)
            middle[s] = grad_mid
            low = grad_mid.astype(BF)
            gwo_ref[...] += dot_nn(mix_buf[s], low)
            mix_buf[s] = dot_nt(matrix(wo_ref, 0), low).astype(BF)
            for copy in leavings(s):
                copy.start()
            if layers:
                pl.when(s == 0)(lambda: over_layers(last - 1))
                pl.when(s == seqs - 1)(lambda: finish(last - 1))
            return (
                gain_sum + jnp.sum(gradient * whitened, axis=0, keepdims=True),
                shift_sum + jnp.sum(gradient, axis=0, keepdims=True),
                branch_sum + jnp.sum(low.astype(F32), axis=0, keepdims=True),
                cot_sum + jnp.sum(own, axis=0, keepdims=True),
                loglik + jnp.where(live, picked, 0.0),
                hits + jnp.where(live, jnp.exp(picked), 0.0),
            )

        blanks = [jnp.zeros((1, D), F32)] * 4 + [jnp.zeros((1, length), F32)] * 2
        gain_sum, shift_sum, branch_sum, cot_sum, loglik, hits = lax.fori_loop(
            0, seqs, sequence, tuple(blanks)
        )
        small_ref[0:1, :] = gain_sum
        small_ref[1:2, :] = shift_sum
        small_ref[2:3, :] = branch_sum
        small_ref[3:4, :] = cot_sum
        small_ref[4:8, :] = jnp.zeros((4, D), F32)
        small_ref[4:5, 0:128] = jnp.broadcast_to(
            jnp.sum(loglik, axis=1, keepdims=True), (1, 128)
        )
        small_ref[4:5, 128:256] = jnp.broadcast_to(
            jnp.sum(hits, axis=1, keepdims=True), (1, 128)
        )
        for s in range(seqs):
            for copy in leavings(s):
                copy.wait()
        if layers:
            for copy in farewell:
                copy.wait()


def whole(shape):
    return pl.BlockSpec(shape, lambda *_: (0,) * len(shape), pipeline_mode=pl.Buffered(1))


def block_of(shape, *index):
    return pl.BlockSpec(shape, lambda *_: index, pipeline_mode=pl.Buffered(1))


def leading(shape):
    return pl.BlockSpec((1,) + tuple(shape[1:]), lambda i, *_: (i,) + (0,) * (len(shape) - 1))


def shaped(shape, dtype=F32):
    return jax.ShapeDtypeStruct(shape, dtype)


def projections(attn, first, count):
    blocks = attn.shape[0] // 4
    rows = D // blocks
    return block_of((blocks * count, rows, D), first // count, 0, 0)


def attention_forward(lengths, tokens, rows_all, attn, ffn, cosine, sine, layers):
    seqs, length, _ = tokens.shape
    heads = HEADS // 4
    flat = (seqs, D, length)
    inverse = (seqs, heads, 4, length)
    exponent = (seqs, HEADS, length, length)

    def part(block):
        return pl.BlockSpec(block, lambda g, s, *_: (s, g, 0, 0)[: len(block)])

    out_specs = [part((1, 128, length))] * 5
    out_specs += [part((1, 1, 4, length)), part((1, 4, length, length))]
    out_shape = [shaped(flat, BF)] * 4 + [shaped(flat), shaped(inverse), shaped(exponent, BF)]
    scratch = [
        pltpu.VMEM((seqs, D, length), BF), pltpu.VMEM((384, D), BF), pltpu.VMEM((D, 16), F32),
        pltpu.VMEM((seqs, D, length), F32),
    ]
    hbm = pl.BlockSpec(memory_space=pl.ANY)
    params = dict(vmem_limit_bytes=VMEM_LIMIT)
    if layers:
        chips = (layers, 2, 2, 2)
        owned = attn.shape[0]
        early = (2, EARLY) + chips + (ROWS, D)
        out_specs += [whole((16, D)), hbm, hbm]
        out_shape += [
            shaped((16, D)), shaped(chips + (owned, D), BF),
            shaped(early, BF),
        ]
        scratch += [
            pltpu.VMEM(chips + (owned + 16, D), BF), pltpu.VMEM(early, BF),
            pltpu.SemaphoreType.DMA((10, 3 + layers)), pltpu.SemaphoreType.DMA((10, 3 + layers)),
            pltpu.SemaphoreType.DMA((3 + 2 * EARLY,)),
        ]
        params.update(collective_id=2, has_side_effects=True)
        sources = [hbm, hbm, hbm]
    else:
        sources = [whole(rows_all.shape), whole(attn.shape), hbm]
    return pl.pallas_call(
        functools.partial(forward_attention, layers),
        grid_spec=pltpu.PrefetchScalarGridSpec(
            num_scalar_prefetch=1,
            grid=(heads, seqs),
            in_specs=[whole(tokens.shape)] + sources + [whole(cosine.shape), whole(sine.shape)],
            out_specs=out_specs,
            scratch_shapes=scratch,
        ),
        out_shape=out_shape,
        compiler_params=pltpu.CompilerParams(**params),
        name="attention_forward",
    )(lengths, tokens, rows_all, attn, ffn, cosine, sine)


def attention_backward(
    lengths, tokens, attn, rows_all, cosine, sine, query, key, value, grad_mixed, raw,
    inverse, exponent, grad_middle,
):
    seqs, length, _ = tokens.shape

    def part(block):
        return pl.BlockSpec(block, lambda s, g, *_: (s, g, 0, 0)[: len(block)])

    return pl.pallas_call(
        backward_attention,
        grid_spec=pltpu.PrefetchScalarGridSpec(
            num_scalar_prefetch=1,
            grid=(seqs, HEADS // 4),
            in_specs=[
                leading(tokens.shape), projections(attn, 0, 3), whole(rows_all.shape),
                whole(cosine.shape), whole(sine.shape),
            ]
            + [part((1, 128, length))] * 5
            + [part((1, 1, 4, length)), part((1, 4, length, length)), leading(tokens.shape)],
            out_specs=[leading(tokens.shape), whole((3 * D, D)), whole((8, D))],
            scratch_shapes=[pltpu.VMEM((3 * D, D), BF), pltpu.VMEM((3 * D, length), BF)],
        ),
        out_shape=[shaped(tokens.shape), shaped((3 * D, D)), shaped((8, D))],
        compiler_params=pltpu.CompilerParams(vmem_limit_bytes=VMEM_LIMIT),
        name="attention_backward",
    )(
        lengths, tokens, attn, rows_all, cosine, sine, query, key, value, grad_mixed, raw,
        inverse, exponent, grad_middle,
    )


def feed_forward_both(
    tokens, mixed, attn, rows_all, cotangent, ffn, fbias, head, labels, flags, lengths, layers,
):
    seqs, length, _ = tokens.shape
    pad = (length + 15) // 16 * 16
    rows = seqs * pad
    steps, chunk = fbias.shape
    hbm = pl.BlockSpec(memory_space=pl.ANY)
    if layers:
        ups, downs = ffn
        up_spec = down_spec = hbm
        owned = downs.shape[1]
        grad_spec, grad_shape = whole((2, owned - ROWS, D)), shaped((2, owned - ROWS, D))
        late_shape = (2, chunk, D)
        chips = (layers, 2, 2, 2)
        extra = [
            pltpu.VMEM(late_shape, F32), pltpu.VMEM((2, steps) + chips + (ROWS, D), BF),
            pltpu.SemaphoreType.DMA((steps, 2, 2 + layers)),
            pltpu.SemaphoreType.DMA((steps, 2, 2 + layers)),
            pltpu.SemaphoreType.DMA((2 + 2 * steps,)),
        ]
        extra += reduce_scratch(4, layers)
    else:
        chunked = (steps, chunk, D)
        ups, downs = ffn[0].reshape(chunked), ffn[1].reshape(chunked)
        up_spec = down_spec = leading(chunked)
        grad_spec = pl.BlockSpec((2, 1, chunk, D), lambda k: (0, k, 0, 0))
        grad_shape = shaped((2,) + chunked)
        late_shape = (8, 128)
        extra = []
    return pl.pallas_call(
        functools.partial(feed_forward, layers),
        grid=(steps,),
        in_specs=[
            hbm, hbm, projections(attn, 3, 1), whole(rows_all.shape), hbm, up_spec, down_spec,
            whole((steps, 1, chunk)), whole(head.shape), whole(labels.shape),
            whole(flags.shape), pl.BlockSpec(memory_space=pltpu.SMEM),
        ],
        out_specs=[
            hbm, hbm, hbm, grad_spec, whole((8, 1, D)), whole((D, D)), whole((8, D)), hbm,
        ],
        out_shape=[
            shaped(tokens.shape, BF), shaped(tokens.shape), shaped(mixed.shape, BF),
            grad_shape, shaped((8, 1, D)), shaped((D, D)), shaped((8, D)), shaped(late_shape),
        ],
        scratch_shapes=[
            pltpu.VMEM(tokens.shape, F32),
            pltpu.VMEM((2, rows, D), BF),
            pltpu.VMEM((2, rows, D), F32),
            pltpu.VMEM((2, rows, chunk), BF),
            pltpu.VMEM(tokens.shape, BF),
            pltpu.VMEM(mixed.shape, BF),
            pltpu.VMEM(tokens.shape, BF),
            pltpu.SemaphoreType.DMA((6, seqs)),
        ]
        + extra,
        compiler_params=pltpu.CompilerParams(
            vmem_limit_bytes=VMEM_LIMIT, **(dict(collective_id=0, has_side_effects=True) if layers else {})
        ),
        name="feed_forward",
    )(
        tokens, mixed, attn, rows_all, cotangent, ups, downs,
        fbias.reshape(steps, 1, chunk), head, labels, flags, lengths,
    )


def own_sums(owner, row_count, sums_ref, gains_ref, biases_ref, units_ref, stats_ref):
    sums = sums_ref[...]
    shard, width = gains_ref.shape[1], sums.shape[1]
    wide, device = owner[0], owner[1]
    local = pltpu.roll(sums[0:16], lax.rem(width - wide * shard, width), axis=1)
    gains_ref[...] = local[0:2, 0:shard]
    biases_ref[...] = local[2:9, 0:shard]
    hidden = sums[16:24]
    lane = lax.broadcasted_iota(jnp.int32, (1, width), 1)
    total = jnp.zeros((1, width), F32)
    for k in range(units_ref.shape[1] // ROWS):
        moved = pltpu.roll(hidden, lax.rem(width + k * ROWS - device * ROWS, width), axis=1)
        mine = (lane >= k * ROWS) & (lane < (k + 1) * ROWS)
        total += jnp.where(mine, moved[k : k + 1], 0.0)
    units_ref[...] = total[:, 0 : units_ref.shape[1]]
    first = lax.broadcasted_iota(jnp.int32, (1, 2), 1) == 0
    both = jnp.where(first, sums[9:10, 0:1], sums[9:10, 128:129] * float(VOCAB))
    stats_ref[...] = both / row_count


def split_sums(sums, wide, device, shard, units, row_count):
    vmem = pl.BlockSpec(memory_space=pltpu.VMEM)
    gains, biases, hidden, stats = pl.pallas_call(
        lambda owner, *refs: own_sums(owner, row_count, *refs),
        in_specs=[pl.BlockSpec(memory_space=pltpu.SMEM), vmem],
        out_specs=[vmem] * 4,
        out_shape=[
            shaped((2, shard)), shaped((7, shard)), shaped((1, units)), shaped((1, 2)),
        ],
        name="own_sums",
    )(jnp.stack([wide, device]).astype(jnp.int32), sums)
    return gains, biases, hidden.reshape(units), stats.reshape(2)


def reduce_tail(grad_qkv, grad_wo, late, part, small_one, small_two, units, layers):
    owned = grad_wo.shape[1]
    pieces = 2 + owned // ROWS
    devices = grad_qkv.shape[0] + grad_wo.shape[0]
    hbm, vmem = pl.BlockSpec(memory_space=pl.ANY), pl.BlockSpec(memory_space=pltpu.VMEM)
    return pl.pallas_call(
        functools.partial(gradient_tail, layers),
        in_specs=[hbm] * 3 + [vmem] * 4,
        out_specs=[vmem] * 3,
        out_shape=[shaped((owned, D)), shaped((2, owned, D)), shaped((24, D))],
        scratch_shapes=[
            pltpu.VMEM((pieces, devices, ROWS, D), F32),
            pltpu.SemaphoreType.DMA((pieces, 2)),
            pltpu.VMEM((4, 24, D), F32),
            pltpu.VMEM((3 + layers, 24, D), F32),
            pltpu.SemaphoreType.DMA((2 + layers,)),
            pltpu.SemaphoreType.DMA((2 + layers,)),
        ]
        + reduce_scratch(pieces, layers),
        compiler_params=pltpu.CompilerParams(
            vmem_limit_bytes=VMEM_LIMIT, collective_id=1, has_side_effects=True
        ),
        name="gradient_tail",
    )(grad_qkv, grad_wo, late.reshape(2, devices, ROWS, D), part, small_one, small_two, units)


def per_device(
    tokens, lengths, masked_flags, labels, attn_weights, ffn_weights, ffn_bias, norm_gains,
    biases, head_weight, cotangent,
):
    both = ("wide", "narrow")
    seqs, length, _ = tokens.shape
    wide, narrow = lax.axis_size("wide"), lax.axis_size("narrow")
    devices = wide * narrow
    shard, units = D // wide, ffn_bias.shape[0]
    owned = attn_weights.shape[0]
    layers = 4 if (wide, narrow) == (8, 4) and owned == units and owned % ROWS == 0 else 0
    at = lax.axis_index("wide")
    owner = at * narrow + lax.axis_index("narrow")
    first = (lax.axis_index("narrow") == 0).astype(BF)
    own = jnp.concatenate([norm_gains, biases], axis=0) * first
    rows_own = lax.dynamic_update_slice(jnp.zeros((16, D), BF), own, (0, at * shard))
    if layers:
        rows_own = lax.dynamic_update_slice(
            rows_own, ffn_bias.reshape(-1, ROWS), (9, owner * ROWS)
        )
    else:
        flat = lax.dynamic_update_slice(jnp.zeros((4 * D,), BF), ffn_bias, (owner * units,))
        rows_own = rows_own + jnp.pad(flat.reshape(4, D), ((9, 3), (0, 0)))
    cosine, sine = rotary_tables(length)
    if layers:
        rows_all, attn, ffn = rows_own, attn_weights, ffn_weights
    else:
        attn = lax.all_gather(attn_weights, both, axis=0, tiled=True).reshape(4, D, D)
        ffn = lax.all_gather(ffn_weights, both, axis=1, tiled=True)
        rows_all = lax.psum(rows_own.astype(F32), both)
    query, key, value, mixed, raw, inverse, exponent, *gathered = attention_forward(
        lengths, tokens, rows_all, attn, ffn, cosine, sine, layers
    )
    if layers:
        rows_all, attn, ffn = gathered
        attn = attn.reshape(devices, owned, D)
        ffn = (ffn, ffn_weights)
        unit_bias = jnp.zeros((units // ROWS, devices * ROWS), F32)
    else:
        unit_bias = rows_all[9:13].reshape(-1, 512)
    (
        output, grad_middle, grad_mixed, grad_ffn, unit_sums, grad_wo, small_two, late,
    ) = feed_forward_both(
        tokens, mixed, attn, rows_all, cotangent, ffn, unit_bias, head_weight.T, labels,
        masked_flags, lengths, layers,
    )
    if not layers:
        grad_ffn = lax.psum_scatter(
            grad_ffn.reshape(2, -1, D), both, scatter_dimension=1, tiled=True
        )
    grad_tokens, grad_qkv, small_one = attention_backward(
        lengths, tokens, attn, rows_all, cosine, sine, query, key, value, grad_mixed, raw,
        inverse, exponent, grad_middle,
    )
    steps, chunk = unit_bias.shape
    if layers:
        blocks = (-1, owned, D)
        grad_attn, grad_ffn, sums = reduce_tail(
            grad_qkv.reshape(blocks), grad_wo.reshape(blocks), late, grad_ffn, small_one,
            small_two, unit_sums, layers,
        )
        grad_gains, grad_biases, grad_ffn_bias, head_stats = split_sums(
            sums, at, owner, shard, units, float(seqs * length * devices)
        )
    else:
        grad_attn = lax.psum_scatter(
            jnp.concatenate([grad_qkv, grad_wo], axis=0), both, scatter_dimension=0, tiled=True
        )
        sums = jnp.concatenate(
            [
                small_one[0:1], small_two[0:1], small_one[1:2], small_two[1:2], small_one[2:5],
                small_two[2:5], jnp.zeros((6, D), F32), unit_sums[:, 0],
            ],
            axis=0,
        )
        sums = lax.psum(sums, both)
        grad_ffn_bias = lax.dynamic_slice_in_dim(
            sums[16:, :chunk].reshape(-1), owner * units, units, 0
        )
        grad_gains = lax.dynamic_slice(sums, (0, at * shard), (2, shard))
        grad_biases = lax.dynamic_slice(sums, (2, at * shard), (7, shard))
        head_stats = (
            sums[9, 0:256:128] * jnp.array([1.0, VOCAB], F32) / (seqs * length * devices)
        )
    return (
        output, grad_tokens, grad_attn, grad_ffn, grad_ffn_bias, grad_gains, grad_biases,
        head_stats,
    )


def solution(mesh):
    both = ("wide", "narrow")
    return jax.shard_map(
        per_device,
        mesh=mesh,
        in_specs=(
            P(both, None, None),
            P(both),
            P(both, None),
            P(both, None),
            P(both, None),
            P(None, both, None),
            P(both),
            P(None, "wide"),
            P(None, "wide"),
            P(),
            P(both, None, None),
        ),
        out_specs=(
            P(both, None, None),
            P(both, None, None),
            P(both, None),
            P(None, both, None),
            P(both),
            P(None, "wide"),
            P(None, "wide"),
            P(),
        ),
        check_vma=False,
    )
```
